32 devices in a mesh: row: 8 (over z, core), col: 4 (over y, x).
Axes of the slice: x: 2, y: 2, z: 4, core: 2. Of those that a mesh axis runs over, the one named last changes fastest.
Arguments:
- matrix_tiles: float32 [10, 8, 128, 20, 4, 128], P(None, 'row', None, None, 'col'), may hold values from -60715.73 to 60715.73
Outputs:
- reduced: float32 [10, 8, 128, 20, 4, 128], P(None, 'row', None, None, 'col')
The draws below stay inside these ranges and needn't reach their ends.
All inputs are finite; a program needn't handle non-finite values.
Results may differ from the reference program's by a relative error of at most 0.0003.
Values sent between devices are 32-bit elements; how exact they have to be, the bound alone decides.
A program may use at most 128 MiB of HBM per device.

```python
import jax
import jax.numpy as jnp
from jax import lax

ORDER = 10240
TILE = 128
BAND = 256
PANELS = 2
ROW_BLOCKS = 10
COL_BLOCKS = 20
N_ROW = 8
N_COL = 4


def draw_matrix_tiles(key, part):
    first_key = jax.random.fold_in(key, 11)
    common_key = jax.random.fold_in(key, 37)
    common = jax.random.uniform(common_key, (ORDER,), jnp.float32, -1.7320508, 1.7320508)
    base_values = jnp.clip(jax.random.normal(first_key, (ORDER, ORDER), jnp.float32), -6.0, 6.0)
    symmetric = (base_values + base_values.T) * 0.70710678
    symmetric = symmetric + 2.0 * common[:, None] * common[None, :]
    column_norms = jnp.sqrt(jnp.sum(symmetric * symmetric, axis=0))
    offsets = jnp.arange(BAND, dtype=jnp.int32)
    for panel_index in range(PANELS):
        start_col = panel_index * BAND
        start_row = start_col + BAND
        boost_values = 2.0 * column_norms[start_col + offsets]
        symmetric = symmetric.at[start_row + offsets, start_col + offsets].add(boost_values)
        symmetric = symmetric.at[start_col + offsets, start_row + offsets].add(boost_values)
    return symmetric.reshape(ROW_BLOCKS, N_ROW, TILE, COL_BLOCKS, N_COL, TILE)


def setup_inputs(seed: int = 0) -> dict:
    keys = jax.random.split(jax.random.key(seed), 2)
    matrix_tiles = draw_matrix_tiles(jax.random.fold_in(keys[1], 71), 0)
    return dict(matrix_tiles=matrix_tiles)


def multiply(first_matrix, second_matrix):
    return jnp.dot(first_matrix, second_matrix, precision=lax.Precision.HIGHEST, preferred_element_type=first_matrix.dtype)

def transposed_left(first_matrix, second_matrix):
    return lax.dot_general(first_matrix, second_matrix, (((0,), (0,)), ((), ())), precision=lax.Precision.HIGHEST, preferred_element_type=first_matrix.dtype)

def transposed_right(first_matrix, second_matrix):
    return lax.dot_general(first_matrix, second_matrix, (((1,), (1,)), ((), ())), precision=lax.Precision.HIGHEST, preferred_element_type=first_matrix.dtype)

def lower_inverse(matrix):
    factor = jnp.linalg.cholesky(matrix)
    identity = jnp.eye(matrix.shape[0], dtype=matrix.dtype)
    return lax.linalg.triangular_solve(factor, identity, left_side=True, lower=True)

def reflector_factors(gram_matrix, top_panel):
    inverse = lower_inverse(gram_matrix)
    top_basis = transposed_right(top_panel, inverse)
    sign_values = jnp.where(jnp.diagonal(top_basis) >= 0, -1.0, 1.0).astype(top_basis.dtype)
    shifted = top_basis - jnp.diag(sign_values)
    outer_inverse = lower_inverse(transposed_left(shifted, shifted))
    kernel = transposed_left(outer_inverse, outer_inverse)
    transform = -sign_values[:, None] * multiply(shifted, kernel)
    return (inverse, sign_values, transform)

def reference(matrix_tiles):
    tile_shape = matrix_tiles.shape
    order_size = tile_shape[0] * tile_shape[1] * tile_shape[2]
    matrix = matrix_tiles.reshape(order_size, order_size)
    for panel_index in range(PANELS):
        panel_start = panel_index * BAND
        below_start = panel_start + BAND
        panel_block = matrix[below_start:, panel_start:below_start]
        gram_matrix = transposed_left(panel_block, panel_block)
        inverse, sign_values, transform = reflector_factors(gram_matrix, panel_block[:BAND])
        basis_rows = transposed_right(panel_block, inverse)
        basis_rows = basis_rows.at[:BAND].add(-jnp.diag(sign_values))
        vectors = jnp.concatenate([jnp.zeros((below_start, BAND), matrix.dtype), basis_rows], 0)
        applied = multiply(multiply(matrix, vectors), transform)
        inner_term = multiply(transform.T, transposed_left(vectors, applied))
        updates = applied - 0.5 * multiply(vectors, inner_term)
        matrix = matrix - transposed_right(jnp.concatenate([vectors, updates], 1), jnp.concatenate([updates, vectors], 1))
    return matrix.reshape(tile_shape)
```

```python
import functools

import jax
import jax.numpy as jnp
from jax import lax
from jax.experimental import pallas as pl
from jax.experimental.pallas import tpu as pltpu
from jax.sharding import PartitionSpec as P

BAND = 256
PANELS = 2
BIG = 60 * 1024 * 1024
SMALL = 32 * 1024 * 1024
MESH = pl.DeviceIdType.MESH

HI = lax.Precision.HIGHEST
def mm(a, b, ca, cb):
    return lax.dot_general(a, b, (((ca,), (cb,)), ((), ())), precision=HI, preferred_element_type=jnp.float32)

def base_inverse(block, hook):
    size = block.shape[0]
    wide = (8, 2 * size)
    group = 8
    places = lax.broadcasted_iota(jnp.int32, wide, 0)
    cols = lax.broadcasted_iota(jnp.int32, wide, 1)
    work = []
    for k in range(size // 8):
        unit = jnp.where(places + 8 * k == cols, 1.0, 0.0)[:, :size]
        work.append(jnp.concatenate([block[8 * k : 8 * k + 8], unit], 1))
    for start in range(0, size, group):
        own, offset = divmod(start, 8)
        rows = [jnp.broadcast_to(work[own][offset + i : offset + i + 1], wide) for i in range(group)]
        pivot = [
            [jnp.broadcast_to(rows[i][:, start + j : start + j + 1], wide) for j in range(group)]
            for i in range(group)
        ]
        first = own if offset + group < 8 else own + 1
        columns = [
            [jnp.broadcast_to(work[k][:, start + i : start + i + 1], wide) for i in range(group)]
            for k in range(first, len(work))
        ]
        scaled = []
        for i in range(group):
            inverse = 1.0 / pivot[i][i]
            scaled.append(rows[i] * inverse)
            for j in range(i + 1, group):
                ratio = pivot[i][j] * inverse
                for l in range(j, group):
                    pivot[j][l] = pivot[j][l] - ratio * pivot[i][l]
                rows[j] = rows[j] - ratio * rows[i]
                for column in columns:
                    column[j] = column[j] - ratio * column[i]
        for k, column in zip(range(first, len(work)), columns):
            change = column[0] * scaled[0]
            for i in range(1, group):
                change = change + column[i] * scaled[i]
            if k == own:
                change = jnp.where(places >= offset + group, change, 0.0)
            work[k] = work[k] - change
        for i in range(group):
            work[own] = jnp.where(places == offset + i, rows[i], work[own])
        hook()
    result = []
    for k, value in enumerate(work):
        pivots = jnp.sum(jnp.where(places + 8 * k == cols, value, 0.0), axis=1, keepdims=True)
        result.append(value[:, size:] * (1.0 / jnp.sqrt(pivots)))
    return jnp.concatenate(result, 0)


def factor_inverse(matrix, base, hook):
    size = matrix.shape[0]
    if size <= base:
        return base_inverse(matrix, hook)
    half = size // 2
    first = factor_inverse(matrix[:half, :half], base, hook)
    lower = mm(matrix[half:, :half], first, 1, 1)
    second = factor_inverse(matrix[half:, half:] - mm(lower, lower, 1, 1), base, hook)
    corner = -mm(second, mm(lower, first, 1, 0), 1, 0)
    top = jnp.concatenate([first, jnp.zeros_like(first)], 1)
    return jnp.concatenate([top, jnp.concatenate([corner, second], 1)], 0)

def factor_body(gram, top, inverse_ref, shifted_ref, transform_ref, sign_ref, hook):
    size = gram.shape[0]
    inverse = factor_inverse(gram, 64, hook)
    inverse_ref[...] = inverse
    basis = mm(top, inverse, 0, 1)
    rows = lax.broadcasted_iota(jnp.int32, (size, size), 0)
    cols = lax.broadcasted_iota(jnp.int32, (size, size), 1)
    on_diagonal = rows == cols
    sign_square = jnp.where(on_diagonal, jnp.where(basis >= 0, -1.0, 1.0), 0.0)
    shifted = basis - sign_square
    shifted_ref[...] = shifted
    outer = factor_inverse(mm(shifted, shifted, 0, 0), 64, hook)
    sign_column = jnp.sum(sign_square, axis=1, keepdims=True)
    transform_ref[...] = -sign_column * mm(mm(shifted, outer, 1, 1), outer, 1, 0)
    sign_ref[...] = jnp.sum(sign_square, axis=0, keepdims=True)


def multiply(first, second, first_dim=1, second_dim=0, precision=HI):
    return lax.dot_general(
        first,
        second,
        (((first_dim,), (second_dim,)), ((), ())),
        precision=precision,
        preferred_element_type=jnp.float32,
    )


def remote(source, target, send_sem, recv_sem, row, col):
    return pltpu.make_async_remote_copy(
        src_ref=source,
        dst_ref=target,
        send_sem=send_sem,
        recv_sem=recv_sem,
        device_id={"row": row, "col": col},
        device_id_type=MESH,
    )


class Place:
    def __init__(self, rows, cols):
        self.rows, self.cols, self.planes = rows, cols, rows // 2
        row = lax.axis_index("row")
        self.col = lax.axis_index("col")
        self.plane = row // 2
        self.core = row % 2
        self.row = row
        self.other = 2 * self.plane + (1 - self.core)
        self.me = self.core * cols + self.col

    def peers(self):
        found = []
        for core_step in range(2):
            for col_step in range(self.cols):
                if core_step or col_step:
                    core = lax.rem(self.core + core_step, 2)
                    col = lax.rem(self.col + col_step, self.cols)
                    found.append((2 * self.plane + core, col, core * self.cols + col))
        return found

    def greet(self, line=True):
        barrier = pltpu.get_barrier_semaphore()
        count = 0
        for row, col, _ in self.peers():
            pl.semaphore_signal(
                barrier, inc=1, device_id={"row": row, "col": col}, device_id_type=MESH
            )
            count += 1
        for step in range(1, self.planes) if line else ():
            row = lax.rem(self.row + 2 * step, self.rows)
            pl.semaphore_signal(
                barrier, inc=1, device_id={"row": row, "col": self.col}, device_id_type=MESH
            )
            count += 1
        pl.semaphore_wait(barrier, count)


def plane_scatter(place, x_ref, parts, out_ref, send_sem, recv_sem):
    copies = []
    for slot, (row, col, piece) in enumerate(place.peers()):
        copies.append(
            remote(
                x_ref.at[piece], parts.at[slot], send_sem.at[slot], recv_sem.at[slot], row, col
            )
        )
        copies[-1].start()
    total = x_ref[place.me]
    for slot, copy in enumerate(copies):
        copy.wait_recv()
        total = total + parts[slot]
    out_ref[place.me] = total
    for copy in copies:
        copy.wait_send()


def plane_gather(place, out_ref, send_sem, recv_sem):
    mine = out_ref.at[place.me]
    copies = []
    for slot, (row, col, _) in enumerate(place.peers()):
        copies.append(remote(mine, mine, send_sem.at[slot], recv_sem.at[slot], row, col))
        copies[-1].start()
    return copies


def plane_kernel(rows, cols, x_ref, out_ref, parts, send_one, recv_one, send_two, recv_two):
    place = Place(rows, cols)
    place.greet(False)
    plane_scatter(place, x_ref, parts, out_ref, send_one, recv_one)
    for copy in plane_gather(place, out_ref, send_two, recv_two):
        copy.wait()


def plane_sum(x, collective_id):
    rows, cols = lax.axis_size("row"), lax.axis_size("col")
    size, width = x.shape
    count = 2 * cols
    pieces = (count, size // count, width)
    vmem = pl.BlockSpec(memory_space=pltpu.VMEM)
    out = pl.pallas_call(
        functools.partial(plane_kernel, rows, cols),
        out_shape=jax.ShapeDtypeStruct(pieces, x.dtype),
        in_specs=[vmem],
        out_specs=vmem,
        scratch_shapes=[pltpu.VMEM((count - 1,) + pieces[1:], x.dtype)]
        + [pltpu.SemaphoreType.DMA((count - 1,))] * 4,
        compiler_params=pltpu.CompilerParams(
            collective_id=collective_id, has_side_effects=True, vmem_limit_bytes=SMALL
        ),
    )(x.reshape(pieces))
    return out.reshape(size, width)


class Chain:
    def __init__(self, place, source, x_ref, panel_ref, sems):
        self.place, self.source, self.x_ref, self.ref = place, source, x_ref, panel_ref
        self.load, self.sends, self.recv, self.share_send, self.share_recv = sems
        self.tile = x_ref.shape[-1]
        self.tiles = x_ref.shape[1]
        self.chunks = self.recv.shape[0]
        self.width = panel_ref.shape[1] // self.chunks
        self.at_source = place.plane == source

    def loads(self):
        start = pl.multiple_of(self.place.core * self.tile, self.tile)
        for tile in range(self.tiles):
            yield pltpu.make_async_copy(
                self.x_ref.at[pl.ds(0, self.tile), tile, 0, :],
                self.ref.at[pl.ds(start, self.tile), pl.ds(tile * self.tile, self.tile)],
                self.load.at[tile],
            )

    def part(self, chunk):
        start = pl.multiple_of(self.place.core * self.tile, self.tile)
        return self.ref.at[pl.ds(start, self.tile), pl.ds(chunk * self.width, self.width)]

    def hop(self, chunk, step, sem):
        part = self.part(chunk)
        row = lax.rem(self.place.row + 2 * step + self.place.rows, self.place.rows)
        return remote(part, part, self.sends.at[sem, chunk], self.recv.at[chunk], row, self.place.col)

    def shared(self, chunk):
        part = self.part(chunk)
        return remote(
            part,
            part,
            self.share_send.at[chunk],
            self.share_recv.at[chunk],
            self.place.other,
            self.place.col,
        )

    def start(self):
        @pl.when(self.at_source)
        def _():
            for copy in self.loads():
                copy.start()

    def send(self):
        @pl.when(self.at_source)
        def _():
            for copy in self.loads():
                copy.wait()
            for chunk in range(self.chunks):
                self.shared(chunk).start()
                if self.source < self.place.planes - 1:
                    self.hop(chunk, 1, 0).start()
                if self.source > 0:
                    self.hop(chunk, -1, 1).start()

    def step(self, chunk):
        place = self.place
        for step, sem, away, more in (
            (1, 0, place.plane > self.source, place.plane < place.planes - 1),
            (-1, 1, place.plane < self.source, place.plane > 0),
        ):
            if step < 0 and self.source == 0 or step > 0 and self.source == place.planes - 1:
                continue

            @pl.when(away)
            def _():
                self.hop(chunk, step, sem).wait_recv()

                @pl.when(more)
                def _():
                    self.hop(chunk, step, sem).start()

                self.shared(chunk).start()

    def finish(self):
        place = self.place
        for chunk in range(self.chunks):
            self.shared(chunk).wait()
        for step, sem, sent in (
            (1, 0, (place.plane >= self.source) & (place.plane < place.planes - 1)),
            (-1, 1, (place.plane <= self.source) & (place.plane > 0)),
        ):

            @pl.when(sent)
            def _():
                for chunk in range(self.chunks):
                    self.hop(chunk, step, sem).wait_send()

    @staticmethod
    def semaphores(tiles, chunks):
        dma = pltpu.SemaphoreType.DMA
        return [dma((tiles,)), dma((2, chunks)), dma((chunks,)), dma((chunks,)), dma((chunks,))]


def gram_kernel(rows, cols, below, x_ref, out_ref, later_ref, panel, stack, parts, *sems):
    place = Place(rows, cols)
    tile, tiles = x_ref.shape[-1], x_ref.shape[1]
    load, swap_send, swap_recv, send_one, recv_one, line_send, line_recv, send_two, recv_two = sems[:9]
    later = Chain(place, 1, x_ref, later_ref, sems[9:])
    first = place.plane == 0
    start = pl.multiple_of(place.core * tile, tile)
    own = panel.at[pl.ds(start, tile), :]

    def loads():
        for index in range(tiles):
            yield pltpu.make_async_copy(
                x_ref.at[pl.ds(0, tile), index, 0, :],
                panel.at[pl.ds(start, tile), pl.ds(index * tile, tile)],
                load.at[index],
            )

    @pl.when(first)
    def _():
        for copy in loads():
            copy.start()

    later.start()
    place.greet()
    later.send()
    line = [
        remote(
            out_ref.at[place.me],
            out_ref.at[place.me],
            line_send.at[step - 1],
            line_recv.at[0],
            lax.rem(place.row + 2 * step, rows),
            place.col,
        )
        for step in range(1, place.planes)
    ]

    @pl.when(first)
    def _():
        for copy in loads():
            copy.wait()
        swap = remote(own, own, swap_send.at[0], swap_recv.at[0], place.other, place.col)
        swap.start()
        swap.wait()
        width = tile * tiles // 2
        offset = place.core * width
        lanes = lax.broadcasted_iota(jnp.int32, (panel.shape[0], width), 1) + offset
        begin = below // tile
        limit = jnp.where(place.col < begin, tile, 0)
        value = panel[:, pl.ds(pl.multiple_of(offset, tile), width)]
        value = jnp.where(lanes >= limit, value, 0.0)
        gram = mm(value, value, 1, 1)
        size = stack.shape[1]
        per = panel.shape[0] // size
        for piece in range(per):
            stack[piece] = gram[piece * size : (piece + 1) * size]
        for index in range(panel.shape[0] // tile):
            number = begin + index
            local = number // cols
            mine = (place.col == number % cols) & (place.core == 0)
            block = jnp.where(mine, panel[:, local * tile : (local + 1) * tile], 0.0)
            for piece in range(per):
                stack[per + piece, :, index * tile : (index + 1) * tile] = block[
                    piece * size : (piece + 1) * size
                ]
        plane_scatter(place, stack, parts, out_ref, send_one, recv_one)
        for copy in line:
            copy.start()

    @pl.when(place.plane > 0)
    def _():
        line[0].wait_recv()

    gathers = plane_gather(place, out_ref, send_two, recv_two)
    for chunk in range(later.chunks):
        later.step(chunk)

    @pl.when(first)
    def _():
        for copy in line:
            copy.wait_send()

    for copy in gathers:
        copy.wait()
    later.finish()


CHUNK = 256


def gram(x4, collective_id):
    rows, cols = lax.axis_size("row"), lax.axis_size("col")
    _, tiles, _, tile = x4.shape
    width = tiles * tile
    count = 2 * cols
    pieces = (count, 2 * BAND // count, BAND)
    vmem = pl.BlockSpec(memory_space=pltpu.VMEM)
    dma = pltpu.SemaphoreType.DMA
    one, later = pl.pallas_call(
        functools.partial(gram_kernel, rows, cols, BAND),
        out_shape=(
            jax.ShapeDtypeStruct(pieces, x4.dtype),
            jax.ShapeDtypeStruct((BAND, width), x4.dtype),
        ),
        in_specs=[pl.BlockSpec(memory_space=pl.ANY)],
        out_specs=(vmem, vmem),
        scratch_shapes=[
            pltpu.VMEM((BAND, width), x4.dtype),
            pltpu.VMEM(pieces, x4.dtype),
            pltpu.VMEM((count - 1,) + pieces[1:], x4.dtype),
            dma((tiles,)),
            dma((1,)),
            dma((1,)),
            dma((count - 1,)),
            dma((count - 1,)),
            dma((rows // 2 - 1,)),
            dma((1,)),
            dma((count - 1,)),
            dma((count - 1,)),
        ]
        + Chain.semaphores(tiles, width // CHUNK),
        compiler_params=pltpu.CompilerParams(
            collective_id=collective_id, has_side_effects=True, vmem_limit_bytes=SMALL
        ),
    )(x4)
    return one.reshape(2 * BAND, BAND), later


def factor_move_kernel(
    rows, cols, stack_ref, x_ref, inverse_ref, shifted_ref, transform_ref, sign_ref, rows_ref, cols_ref, *sems
):
    place = Place(rows, cols)
    tile = x_ref.shape[-1]
    load, send_row, recv_row = sems[:3]
    chain = Chain(place, 0, x_ref, cols_ref, sems[3:])
    held = PANELS * BAND // tile
    panel_tiles = BAND // tile

    def spot(col):
        start = pl.multiple_of(lax.rem(col, panel_tiles) * tile, tile)
        return rows_ref.at[col // panel_tiles, :, pl.ds(start, tile)]

    has = place.col < held
    own = spot(lax.rem(place.col, held))
    fill = pltpu.make_async_copy(x_ref.at[:, 0, 0, :], own, load.at[0])

    @pl.when(has)
    def _():
        fill.start()

    chain.start()
    place.greet()
    chain.send()
    copies = [
        remote(
            own,
            own,
            send_row.at[step - 1],
            recv_row.at[lax.rem(place.col, held)],
            place.row,
            lax.rem(place.col + step, cols),
        )
        for step in range(1, cols)
    ]

    @pl.when(has)
    def _():
        fill.wait()
        for copy in copies:
            copy.start()

    count = [0]

    def hook():
        count[0] += 1
        chunk = count[0] // 2 - 2
        if count[0] % 2 == 0 and 0 <= chunk < chain.chunks:
            chain.step(chunk)

    size = inverse_ref.shape[0]
    factor_body(
        stack_ref[:size], stack_ref[size:], inverse_ref, shifted_ref, transform_ref, sign_ref, hook
    )

    @pl.when(has)
    def _():
        for copy in copies:
            copy.wait_send()

    for col in range(held):
        @pl.when(place.col != col)
        def _():
            remote(spot(col), spot(col), send_row.at[0], recv_row.at[col], place.row, place.col).wait_recv()

    chain.finish()


def factor_kernel(stack_ref, inverse_ref, shifted_ref, transform_ref, sign_ref):
    size = inverse_ref.shape[0]
    factor_body(
        stack_ref[:size],
        stack_ref[size:],
        inverse_ref,
        shifted_ref,
        transform_ref,
        sign_ref,
        lambda: None,
    )


def factor_shapes(size):
    square = jax.ShapeDtypeStruct((size, size), jnp.float32)
    return (square, square, square, jax.ShapeDtypeStruct((1, size), jnp.float32))


def factors(stack):
    return pl.pallas_call(
        factor_kernel,
        out_shape=factor_shapes(stack.shape[1]),
        compiler_params=pltpu.CompilerParams(vmem_limit_bytes=SMALL),
    )(stack)


def factors_move(stack, x4, collective_id):
    rows, cols = lax.axis_size("row"), lax.axis_size("col")
    row_count, tiles, _, tile = x4.shape
    vmem = pl.BlockSpec(memory_space=pltpu.VMEM)
    dma = pltpu.SemaphoreType.DMA
    return pl.pallas_call(
        functools.partial(factor_move_kernel, rows, cols),
        out_shape=factor_shapes(BAND)
        + (
            jax.ShapeDtypeStruct((PANELS, row_count, BAND), jnp.float32),
            jax.ShapeDtypeStruct((BAND, tiles * tile), jnp.float32),
        ),
        in_specs=[vmem, pl.BlockSpec(memory_space=pl.ANY)],
        out_specs=(vmem,) * 6,
        scratch_shapes=[dma((1,)), dma((cols - 1,)), dma((PANELS * BAND // tile,))]
        + Chain.semaphores(tiles, tiles * tile // CHUNK),
        compiler_params=pltpu.CompilerParams(
            collective_id=collective_id, has_side_effects=True, vmem_limit_bytes=SMALL
        ),
    )(stack, x4)


def split(value):
    high = value.astype(jnp.bfloat16)
    return high, (value - high.astype(jnp.float32)).astype(jnp.bfloat16)


def split_outside(value):
    high = lax.reduce_precision(value, 8, 7)
    return high.astype(jnp.bfloat16), (value - high).astype(jnp.bfloat16)


def dot(a, b):
    return jnp.dot(a, b, preferred_element_type=jnp.float32)


def apply_kernel(rows, cols, fixed, *refs):
    place = Place(rows, cols)
    x_ref, left_ref = refs[:2]
    more = refs[2 : 2 + fixed]
    out_ref, row_ref = refs[2 + fixed : 4 + fixed]
    block, part, near, pair, left_in, right_in, left_out, right_out = refs[4 + fixed : 12 + fixed]
    (
        load, near_send, near_recv, left_send, left_recv, right_send, right_recv,
        both_send, both_recv, row_send, row_recv,
    ) = refs[12 + fixed :]
    plane, core, planes = place.plane, place.core, place.planes
    tile = x_ref.shape[-1]
    chunks = block.shape[0]
    half = left_ref.shape[0] // 2

    def load_of(chunk, index):
        return pltpu.make_async_copy(
            x_ref.at[:, 2 * chunk + index, 0, :],
            block.at[chunk, :, pl.ds(index * tile, tile)],
            load.at[chunk, index],
        )

    for chunk in range(chunks):
        for index in range(2):
            load_of(chunk, index).start()
    place.greet()

    def near_of(chunk):
        return remote(
            part.at[chunk, 1 - core],
            near.at[chunk],
            near_send.at[chunk],
            near_recv.at[chunk],
            place.other,
            place.col,
        )

    def rightward(source, chunk):
        return remote(
            source.at[chunk], left_in.at[chunk], right_send.at[chunk], left_recv.at[chunk],
            lax.rem(place.row + 2, rows), place.col,
        )

    def leftward(source, chunk):
        return remote(
            source.at[chunk], right_in.at[chunk], left_send.at[chunk], right_recv.at[chunk],
            lax.rem(place.row + rows - 2, rows), place.col,
        )

    def joined(chunk):
        near_of(chunk).wait_recv()
        pair[chunk] = part[chunk, core] + near[chunk]

        @pl.when(plane == 0)
        def _():
            rightward(pair, chunk).start()

        @pl.when(plane == planes - 1)
        def _():
            leftward(pair, chunk).start()

    def product(chunk, carry):
        for index in range(2):
            load_of(chunk, index).wait()
        high, low = split(block[chunk])
        value = dot(left_ref[...], high)
        value = value[:half] + (value[half:] + dot(left_ref[:half], low))
        if fixed:
            factor_ref, high_ref, low_ref = more
            here = pl.ds(pl.multiple_of(chunk * 2 * tile, 2 * tile), 2 * tile)
            other = dot(factor_ref[...], high_ref[:, here])
            other = other[:half] + (other[half:] + dot(factor_ref[:half], low_ref[:, here]))
            value = value - other
        part[chunk, 0] = value[:, :tile]
        part[chunk, 1] = value[:, tile:]
        near_of(chunk).start()

        @pl.when(chunk > 0)
        def _():
            joined(chunk - 1)

        return carry

    lax.fori_loop(0, chunks, product, 0)
    joined(chunks - 1)

    left_lag = jnp.maximum(plane - 1, 0)
    right_lag = jnp.maximum(planes - 2 - plane, 0)
    last_lag = jnp.maximum(left_lag, right_lag)
    held = cols * core + place.col
    source = held // 2 == plane
    target_row = 2 * plane + lax.rem(place.col, 2)
    to_self = target_row == place.row

    def spot(chunk):
        start = pl.multiple_of((2 * chunk + core) * tile, tile)
        return out_ref.at[:, pl.ds(start, tile)]

    def both_of(chunk):
        return remote(
            spot(chunk), spot(chunk), both_send.at[chunk], both_recv.at[chunk], place.other, place.col
        )

    def row_of(chunk, step):
        start = pl.multiple_of(chunk * tile, tile)
        return remote(
            spot(chunk),
            row_ref.at[:, pl.ds(start, tile)],
            row_send.at[chunk, step],
            row_recv.at[chunk],
            target_row,
            lax.rem(place.col + step, cols),
        )

    def chain(step, carry):
        index = step - left_lag

        @pl.when((plane > 0) & (index >= 0) & (index < chunks))
        def _():
            rightward(pair, index).wait_recv()

            @pl.when(plane < planes - 1)
            def _():
                right_out[index] = left_in[index] + pair[index]
                rightward(right_out, index).start()

        other = step - right_lag

        @pl.when((plane < planes - 1) & (other >= 0) & (other < chunks))
        def _():
            leftward(pair, other).wait_recv()

            @pl.when(plane > 0)
            def _():
                left_out[other] = right_in[other] + pair[other]
                leftward(left_out, other).start()

        done = step - last_lag

        @pl.when((done >= 0) & (done < chunks))
        def _():
            here = pl.ds(pl.multiple_of((2 * done + core) * tile, tile), tile)

            @pl.when(plane == 0)
            def _():
                out_ref[:, here] = pair[done] + right_in[done]

            @pl.when(plane == planes - 1)
            def _():
                out_ref[:, here] = left_in[done] + pair[done]

            @pl.when((plane > 0) & (plane < planes - 1))
            def _():
                out_ref[:, here] = right_out[done] + right_in[done]

            both_of(done).start()

            @pl.when(source)
            def _():
                for step in range(1, cols):
                    row_of(done, step).start()

                @pl.when(to_self)
                def _():
                    there = pl.ds(pl.multiple_of(done * tile, tile), tile)
                    row_ref[:, there] = out_ref[:, here]

                @pl.when(jnp.logical_not(to_self))
                def _():
                    row_of(done, 0).start()

        return carry

    lax.fori_loop(0, chunks + planes - 2, chain, 0)

    gets = jnp.logical_not(source & to_self)

    def drain(chunk, carry):
        near_of(chunk).wait_send()
        both_of(chunk).wait()

        @pl.when(plane < planes - 1)
        def _():
            rightward(pair, chunk).wait_send()

        @pl.when(plane > 0)
        def _():
            leftward(pair, chunk).wait_send()

        @pl.when(source)
        def _():
            for step in range(1, cols):
                row_of(chunk, step).wait_send()

            @pl.when(jnp.logical_not(to_self))
            def _():
                row_of(chunk, 0).wait_send()

        @pl.when(gets)
        def _():
            row_of(chunk, 0).wait_recv()

        return carry

    lax.fori_loop(0, chunks, drain, 0)


def apply(x4, left, more, collective_id):
    rows, cols = lax.axis_size("row"), lax.axis_size("col")
    row_count, tiles, _, tile = x4.shape
    width = tiles * tile
    chunks = tiles // 2
    vmem = pl.BlockSpec(memory_space=pltpu.VMEM)
    dma = pltpu.SemaphoreType.DMA
    piece = (BAND, tile)
    return pl.pallas_call(
        functools.partial(apply_kernel, rows, cols, len(more)),
        out_shape=(
            jax.ShapeDtypeStruct((BAND, width), jnp.float32),
            jax.ShapeDtypeStruct((BAND, row_count), jnp.float32),
        ),
        in_specs=[pl.BlockSpec(memory_space=pl.ANY)] + [vmem] * (1 + len(more)),
        out_specs=(vmem, vmem),
        scratch_shapes=[
            pltpu.VMEM((chunks, row_count, 2 * tile), jnp.float32),
            pltpu.VMEM((chunks, 2) + piece, jnp.float32),
        ]
        + [pltpu.VMEM((chunks,) + piece, jnp.float32)] * 6
        + [dma((chunks, 2))]
        + [dma((chunks,))] * 8
        + [dma((chunks, cols)), dma((chunks,))],
        compiler_params=pltpu.CompilerParams(
            collective_id=collective_id, has_side_effects=True, vmem_limit_bytes=BIG
        ),
    )(x4, left, *more)


def update_kernel(x_ref, left_high, left_low, right_high, right_low, out_ref, block, result, load, store):
    tile = x_ref.shape[-1]
    chunks = x_ref.shape[1] // 2

    def load_of(chunk, index):
        return pltpu.make_async_copy(
            x_ref.at[:, 2 * chunk + index, 0, :],
            block.at[lax.rem(chunk, 2), :, pl.ds(index * tile, tile)],
            load.at[lax.rem(chunk, 2), index],
        )

    def store_of(chunk, index):
        return pltpu.make_async_copy(
            result.at[lax.rem(chunk, 2), :, pl.ds(index * tile, tile)],
            out_ref.at[:, 2 * chunk + index, 0, :],
            store.at[lax.rem(chunk, 2), index],
        )

    for chunk in range(2):
        for index in range(2):
            load_of(chunk, index).start()

    rows = x_ref.shape[0]
    group = rows // 5 if rows % 40 == 0 else rows

    def body(chunk, carry):
        slot = lax.rem(chunk, 2)
        for index in range(2):
            load_of(chunk, index).wait()

        @pl.when(chunk >= 2)
        def _():
            for index in range(2):
                store_of(chunk - 2, index).wait()

        here = pl.ds(pl.multiple_of(chunk * 2 * tile, 2 * tile), 2 * tile)

        def rows_of(number, inner):
            part = pl.ds(pl.multiple_of(number * group, 8), group)
            high, low = left_high[part, :], left_low[part, :]
            value = dot(high, right_high[:, here]) + (
                dot(low, right_high[:, here]) + dot(high, right_low[:, here])
            )
            result[slot, part, :] = block[slot, part, :] - value
            return inner

        lax.fori_loop(0, rows // group, rows_of, 0)
        for index in range(2):
            store_of(chunk, index).start()

        @pl.when(chunk + 2 < chunks)
        def _():
            for index in range(2):
                load_of(chunk + 2, index).start()

        return carry

    lax.fori_loop(0, chunks, body, 0)
    for chunk in range(chunks - 2, chunks):
        for index in range(2):
            store_of(chunk, index).wait()


def update(x4, lefts, rights):
    row_count, tiles, _, tile = x4.shape
    vmem = pl.BlockSpec(memory_space=pltpu.VMEM)
    hbm = pl.BlockSpec(memory_space=pl.ANY)
    dma = pltpu.SemaphoreType.DMA
    return pl.pallas_call(
        update_kernel,
        out_shape=jax.ShapeDtypeStruct(x4.shape, x4.dtype),
        in_specs=[hbm] + [vmem] * 4,
        out_specs=hbm,
        scratch_shapes=[pltpu.VMEM((2, row_count, 2 * tile), jnp.float32)] * 2
        + [dma((2, 2)), dma((2, 2))],
        compiler_params=pltpu.CompilerParams(vmem_limit_bytes=BIG),
    )(x4, *split_outside(jnp.concatenate(lefts, 1)), *split_outside(jnp.concatenate(rights, 0)))


def on_device(matrix_tiles):
    tile_shape = matrix_tiles.shape
    block_rows, _, tile_size, block_cols = tile_shape[:4]
    row_count = block_rows * tile_size
    col_count = block_cols * tile_size
    row_devices = lax.axis_size("row")
    col_devices = lax.axis_size("col")
    row_index = lax.axis_index("row")
    col_index = lax.axis_index("col")
    panel_tiles = BAND // tile_size
    assert row_devices == 2 * col_devices and PANELS * panel_tiles <= col_devices
    high = lax.Precision.HIGH
    x4 = matrix_tiles.reshape(row_count, block_cols, 1, tile_size)

    def positions(count, devices, index):
        place = jnp.arange(count, dtype=jnp.int32)
        return (place // tile_size * devices + index) * tile_size + place % tile_size

    global_rows = positions(row_count, row_devices, row_index)
    global_cols = positions(col_count, col_devices, col_index)
    band = jnp.arange(BAND, dtype=jnp.int32)
    own_half = jnp.where(row_index % 2 == 0, 1.0, 0.0)

    def next_rows(panel, start):
        blocks = []
        for tile in range(start // tile_size, (start + BAND) // tile_size):
            local = tile // col_devices
            part = panel[:, local * tile_size : (local + 1) * tile_size]
            blocks.append(jnp.where(col_index == tile % col_devices, part * own_half, 0.0))
        return jnp.concatenate(blocks, 1)

    stacked, later_cols = gram(x4, 0)
    lefts, rights = [], []
    panel_cols = panel_rows = rows_held = None
    for panel_index in range(PANELS):
        below = (panel_index + 1) * BAND
        last = panel_index == PANELS - 1
        if panel_index == 0:
            inverse, shifted, transform, signs, rows_held, panel_cols = factors_move(stacked, x4, 1)
            panel_rows = rows_held[0]
        else:
            inverse, shifted, transform, signs = factors(stacked)
        panel_rows = jnp.where((global_rows >= below)[:, None], panel_rows, 0.0)
        panel_cols = jnp.where((global_cols >= below)[None, :], panel_cols, 0.0)
        unit_rows = (global_rows[:, None] - below == band[None, :]).astype(jnp.float32)
        unit_rows_t = (band[:, None] == global_rows[None, :] - below).astype(jnp.float32)
        unit_cols = (band[:, None] == global_cols[None, :] - below).astype(jnp.float32)
        signs_t = signs.reshape(BAND, 1)
        vec_rows = multiply(panel_rows, inverse, 1, 1) - unit_rows * signs
        vec_rows_t = multiply(inverse, panel_rows, 1, 1) - unit_rows_t * signs_t
        vec_cols = multiply(inverse, panel_cols) - unit_cols * signs_t
        more = ()
        if lefts:
            cross = jnp.concatenate([multiply(vec_rows_t, left, precision=high) for left in lefts], 1)
            more = (
                jnp.concatenate(split_outside(cross), 0),
                *split_outside(jnp.concatenate(rights, 0)),
            )
        sums, sums_rows = apply(x4, jnp.concatenate(split_outside(vec_rows_t), 0), more, 2 + panel_index)
        applied = multiply(transform, sums, 0, 0)
        applied_rows = multiply(sums_rows, transform, 0, 0)
        inner_part = 0.5 * multiply(vec_cols, applied, 1, 1)
        if last:
            inner = plane_sum(inner_part, 5)
        else:
            both = plane_sum(
                jnp.concatenate([inner_part, next_rows(applied, below)], 0), 4
            )
            inner = both[:BAND]
        half_inner = 0.5 * multiply(transform, inner, 0, 0)
        update_rows = applied_rows - multiply(vec_rows, half_inner)
        update_cols = applied - multiply(half_inner, vec_cols, 0, 0)
        lefts += [vec_rows, update_rows]
        rights += [update_cols, vec_cols]
        if not last:
            update_next = both[BAND:] - multiply(half_inner, shifted, 0, 1)
            panel_rows = (
                rows_held[panel_index + 1]
                - multiply(vec_rows, update_next)
                - multiply(update_rows, shifted, 1, 1)
            )
            panel_cols = (
                later_cols
                - multiply(update_next, vec_cols, 0, 0)
                - multiply(shifted, update_cols)
            )
            start = below + BAND
            kept = jnp.where((global_cols >= start)[None, :], panel_cols, 0.0)
            stacked = plane_sum(
                jnp.concatenate([0.5 * multiply(kept, kept, 1, 1), next_rows(panel_cols, start)], 0), 4
            )
    return update(x4, lefts, rights).reshape(tile_shape)


def solution(mesh):
    return jax.shard_map(
        on_device,
        mesh=mesh,
        in_specs=(P(None, "row", None, None, "col", None),),
        out_specs=P(None, "row", None, None, "col", None),
        check_vma=False,
    )
```

```python
import functools

import jax
import jax.numpy as jnp
from jax import lax
from jax.experimental import pallas as pl
from jax.experimental.pallas import tpu as pltpu
from jax.sharding import PartitionSpec as P

BAND = 256
PANELS = 2
MIB = 1024 * 1024
SMALL = 24 * MIB
TINY = 8 * MIB
MESH = pl.DeviceIdType.MESH

HI = lax.Precision.HIGHEST
def mm(a, b, ca, cb):
    return lax.dot_general(a, b, (((ca,), (cb,)), ((), ())), precision=HI, preferred_element_type=jnp.float32)

def base_inverse(block, hook):
    size = block.shape[0]
    wide = (8, 2 * size)
    group = 8
    places = lax.broadcasted_iota(jnp.int32, wide, 0)
    cols = lax.broadcasted_iota(jnp.int32, wide, 1)
    work = []
    for k in range(size // 8):
        unit = jnp.where(places + 8 * k == cols, 1.0, 0.0)[:, :size]
        work.append(jnp.concatenate([block[8 * k : 8 * k + 8], unit], 1))
    for start in range(0, size, group):
        own, offset = divmod(start, 8)
        rows = [jnp.broadcast_to(work[own][offset + i : offset + i + 1], wide) for i in range(group)]
        pivot = [
            [jnp.broadcast_to(rows[i][:, start + j : start + j + 1], wide) for j in range(group)]
            for i in range(group)
        ]
        first = own if offset + group < 8 else own + 1
        columns = [
            [jnp.broadcast_to(work[k][:, start + i : start + i + 1], wide) for i in range(group)]
            for k in range(first, len(work))
        ]
        scaled = []
        for i in range(group):
            inverse = 1.0 / pivot[i][i]
            scaled.append(rows[i] * inverse)
            for j in range(i + 1, group):
                ratio = pivot[i][j] * inverse
                for l in range(j, group):
                    pivot[j][l] = pivot[j][l] - ratio * pivot[i][l]
                rows[j] = rows[j] - ratio * rows[i]
                for column in columns:
                    column[j] = column[j] - ratio * column[i]
        for k, column in zip(range(first, len(work)), columns):
            change = column[0] * scaled[0]
            for i in range(1, group):
                change = change + column[i] * scaled[i]
            if k == own:
                change = jnp.where(places >= offset + group, change, 0.0)
            work[k] = work[k] - change
        for i in range(group):
            work[own] = jnp.where(places == offset + i, rows[i], work[own])
        hook()
    result = []
    for k, value in enumerate(work):
        pivots = jnp.sum(jnp.where(places + 8 * k == cols, value, 0.0), axis=1, keepdims=True)
        result.append(value[:, size:] * (1.0 / jnp.sqrt(pivots)))
    return jnp.concatenate(result, 0)


def factor_inverse(matrix, base, hook):
    size = matrix.shape[0]
    if size <= base:
        return base_inverse(matrix, hook)
    half = size // 2
    first = factor_inverse(matrix[:half, :half], base, hook)
    lower = mm(matrix[half:, :half], first, 1, 1)
    second = factor_inverse(matrix[half:, half:] - mm(lower, lower, 1, 1), base, hook)
    corner = -mm(second, mm(lower, first, 1, 0), 1, 0)
    top = jnp.concatenate([first, jnp.zeros_like(first)], 1)
    return jnp.concatenate([top, jnp.concatenate([corner, second], 1)], 0)

def orthogonal_top(gram, top, top_dim, inverse_ref, shifted_ref, sign_ref, hook):
    size = gram.shape[0]
    inverse = factor_inverse(gram, 64, hook)
    inverse_ref[...] = inverse
    basis = mm(top(), inverse, top_dim, 1)
    rows = lax.broadcasted_iota(jnp.int32, (size, size), 0)
    cols = lax.broadcasted_iota(jnp.int32, (size, size), 1)
    sign_square = jnp.where(rows == cols, jnp.where(basis >= 0, -1.0, 1.0), 0.0)
    shifted_ref[...] = basis - sign_square
    sign_ref[...] = jnp.sum(sign_square, axis=0, keepdims=True)


def block_transform(shifted, signs, hook):
    size = shifted.shape[0]
    outer = factor_inverse(mm(shifted, shifted, 0, 0), 64, hook)
    rows = lax.broadcasted_iota(jnp.int32, (size, size), 0)
    cols = lax.broadcasted_iota(jnp.int32, (size, size), 1)
    sign_column = jnp.sum(jnp.where(rows == cols, signs, 0.0), axis=1, keepdims=True)
    return -sign_column * mm(mm(shifted, outer, 1, 1), outer, 1, 0)


def multiply(first, second, first_dim=1, second_dim=0, precision=HI):
    return lax.dot_general(
        first,
        second,
        (((first_dim,), (second_dim,)), ((), ())),
        precision=precision,
        preferred_element_type=jnp.float32,
    )


def remote(source, target, send_sem, recv_sem, row, col):
    return pltpu.make_async_remote_copy(
        src_ref=source,
        dst_ref=target,
        send_sem=send_sem,
        recv_sem=recv_sem,
        device_id={"row": row, "col": col},
        device_id_type=MESH,
    )


class Place:
    def __init__(self, rows, cols):
        self.rows, self.cols, self.planes = rows, cols, rows // 2
        row = lax.axis_index("row")
        self.col = lax.axis_index("col")
        self.plane = row // 2
        self.core = row % 2
        self.row = row
        self.other = 2 * self.plane + (1 - self.core)
        self.me = self.core * cols + self.col

    def peers(self):
        found = []
        for core_step in range(2):
            for col_step in range(self.cols):
                if core_step or col_step:
                    core = lax.rem(self.core + core_step, 2)
                    col = lax.rem(self.col + col_step, self.cols)
                    found.append((2 * self.plane + core, col, core * self.cols + col))
        return found

    def greet(self, line=True):
        barrier = pltpu.get_barrier_semaphore()
        count = 0
        for row, col, _ in self.peers():
            pl.semaphore_signal(
                barrier, inc=1, device_id={"row": row, "col": col}, device_id_type=MESH
            )
            count += 1
        for step in range(1, self.planes) if line else ():
            row = lax.rem(self.row + 2 * step, self.rows)
            pl.semaphore_signal(
                barrier, inc=1, device_id={"row": row, "col": self.col}, device_id_type=MESH
            )
            count += 1
        pl.semaphore_wait(barrier, count)


def plane_scatter(place, peers, x_ref, parts, out_ref, send_sem, recv_sem):
    copies = []
    for slot, (row, col, piece) in enumerate(peers):
        copies.append(
            remote(
                x_ref.at[piece], parts.at[slot], send_sem.at[slot], recv_sem.at[slot], row, col
            )
        )
        copies[-1].start()
    total = x_ref[place.me]
    for slot, copy in enumerate(copies):
        copy.wait_recv()
        total = total + parts[slot]
    out_ref[place.me] = total
    for copy in copies:
        copy.wait_send()


def plane_gather(place, mine, send_sem, recv_sem):
    copies = []
    for slot, (row, col, _) in enumerate(place.peers()):
        copies.append(remote(mine, mine, send_sem.at[slot], recv_sem.at[slot], row, col))
        copies[-1].start()
    return copies


class Spread:
    def __init__(self, place, source_ref, tiles, target_ref, send_sem, recv_sem):
        self.place, self.source, self.tiles, self.target = place, source_ref, tiles, target_ref
        self.send_sem, self.recv_sem = send_sem, recv_sem
        self.tile = target_ref.shape[0] // 2

    def refs(self, index, core):
        start = pl.multiple_of(core * self.tile, self.tile)
        local = self.tiles[index] // self.place.cols
        return (
            self.source.at[pl.ds(start, self.tile), pl.ds(local * self.tile, self.tile)],
            self.target.at[pl.ds(start, self.tile), pl.ds(index * self.tile, self.tile)],
        )

    def holder(self, index):
        return self.place.col == self.tiles[index] % self.place.cols

    def copies(self, index):
        source, target = self.refs(index, self.place.core)
        return [
            remote(
                source,
                target,
                self.send_sem.at[index, slot],
                self.recv_sem.at[index, self.place.core],
                row,
                col,
            )
            for slot, (row, col, _) in enumerate(self.place.peers())
        ]

    def send(self):
        for index in range(len(self.tiles)):
            @pl.when(self.holder(index))
            def _():
                for copy in self.copies(index):
                    copy.start()
                source, target = self.refs(index, self.place.core)
                target[...] = source[...]

    def wait(self):
        for index in range(len(self.tiles)):
            for core in range(2):
                source, target = self.refs(index, core)

                @pl.when(jnp.logical_not(self.holder(index) & (self.place.core == core)))
                def _():
                    remote(
                        source,
                        target,
                        self.send_sem.at[index, 0],
                        self.recv_sem.at[index, core],
                        self.place.other,
                        self.place.col,
                    ).wait_recv()

    def finish(self):
        for index in range(len(self.tiles)):
            @pl.when(self.holder(index))
            def _():
                for copy in self.copies(index):
                    copy.wait_send()


def plane_kernel(rows, cols, tiles, *refs):
    place = Place(rows, cols)
    count = 2 if tiles else 1
    x_ref, out_ref = refs[0], refs[count]
    parts, send_one, recv_one, send_two, recv_two = refs[2 * count : 2 * count + 5]
    place.greet(False)
    same = [peer for peer in place.peers()[: cols - 1]]
    plane_scatter(place, same, x_ref, parts, out_ref, send_one, recv_one)
    copies = plane_gather(place, out_ref.at[place.me], send_two, recv_two)
    if tiles:
        spread = Spread(place, refs[1], tiles, refs[3], *refs[9:])
        spread.send()
    for copy in copies:
        copy.wait()
    if tiles:
        spread.wait()
        spread.finish()


def plane_sum(x, collective_id, panel=None, tiles=()):
    rows, cols = lax.axis_size("row"), lax.axis_size("col")
    size, width = x.shape
    count = 2 * cols
    pieces = (count, size // count, width)
    vmem = pl.BlockSpec(memory_space=pltpu.VMEM)
    dma = pltpu.SemaphoreType.DMA
    shapes = (jax.ShapeDtypeStruct(pieces, x.dtype),)
    scratch = [pltpu.VMEM((cols - 1,) + pieces[1:], x.dtype)]
    scratch += [dma((cols - 1,))] * 2 + [dma((count - 1,))] * 2
    operands = (x.reshape(pieces),)
    if tiles:
        shapes += (jax.ShapeDtypeStruct((size, size), x.dtype),)
        scratch += [dma((len(tiles), count - 1)), dma((len(tiles), 2))]
        operands += (panel,)
    out = pl.pallas_call(
        functools.partial(plane_kernel, rows, cols, tiles),
        out_shape=shapes,
        in_specs=[vmem] * len(operands),
        out_specs=(vmem,) * len(shapes),
        scratch_shapes=scratch,
        compiler_params=pltpu.CompilerParams(
            collective_id=collective_id, has_side_effects=True, vmem_limit_bytes=TINY
        ),
    )(*operands)
    return (out[0].reshape(size, width),) + tuple(out[1:])


class Chain:
    def __init__(self, place, source, x_ref, panel_ref, sems):
        self.place, self.source, self.x_ref, self.ref = place, source, x_ref, panel_ref
        self.load, self.sends, self.recv, self.share_send, self.share_recv = sems
        self.tile = x_ref.shape[-1]
        self.tiles = x_ref.shape[1]
        self.chunks = self.recv.shape[0]
        self.width = panel_ref.shape[1] // self.chunks
        self.at_source = place.plane == source

    def loads(self):
        start = pl.multiple_of(self.place.core * self.tile, self.tile)
        for tile in range(self.tiles):
            yield pltpu.make_async_copy(
                self.x_ref.at[pl.ds(0, self.tile), tile, 0, :],
                self.ref.at[pl.ds(start, self.tile), pl.ds(tile * self.tile, self.tile)],
                self.load.at[tile],
            )

    def part(self, chunk):
        start = pl.multiple_of(self.place.core * self.tile, self.tile)
        return self.ref.at[pl.ds(start, self.tile), pl.ds(chunk * self.width, self.width)]

    def hop(self, chunk, step, sem):
        part = self.part(chunk)
        row = lax.rem(self.place.row + 2 * step + self.place.rows, self.place.rows)
        return remote(part, part, self.sends.at[sem, chunk], self.recv.at[chunk], row, self.place.col)

    def shared(self, chunk):
        part = self.part(chunk)
        return remote(
            part,
            part,
            self.share_send.at[chunk],
            self.share_recv.at[chunk],
            self.place.other,
            self.place.col,
        )

    def start(self):
        @pl.when(self.at_source)
        def _():
            for copy in self.loads():
                copy.start()

    def share(self):
        @pl.when(self.at_source)
        def _():
            for copy in self.loads():
                copy.wait()
            for chunk in range(self.chunks):
                self.shared(chunk).start()

    def spread(self, first, last):
        @pl.when(self.at_source)
        def _():
            for chunk in range(first, last):
                if self.source < self.place.planes - 1:
                    self.hop(chunk, 1, 0).start()
                if self.source > 0:
                    self.hop(chunk, -1, 1).start()

    def step(self, chunk):
        place = self.place
        for step, sem, away, more in (
            (1, 0, place.plane > self.source, place.plane < place.planes - 1),
            (-1, 1, place.plane < self.source, place.plane > 0),
        ):
            if step < 0 and self.source == 0 or step > 0 and self.source == place.planes - 1:
                continue

            @pl.when(away)
            def _():
                self.hop(chunk, step, sem).wait_recv()

                @pl.when(more)
                def _():
                    self.hop(chunk, step, sem).start()

                self.shared(chunk).start()

    def join(self):
        for chunk in range(self.chunks):
            self.shared(chunk).wait_recv()

    def finish(self, joined=False):
        place = self.place
        if joined:
            @pl.when(jnp.logical_not(self.at_source))
            def _():
                self.join()
        else:
            self.join()
        for chunk in range(self.chunks):
            self.shared(chunk).wait_send()
        for step, sem, sent in (
            (1, 0, (place.plane >= self.source) & (place.plane < place.planes - 1)),
            (-1, 1, (place.plane <= self.source) & (place.plane > 0)),
        ):

            @pl.when(sent)
            def _():
                for chunk in range(self.chunks):
                    self.hop(chunk, step, sem).wait_send()

    @staticmethod
    def semaphores(tiles, chunks):
        dma = pltpu.SemaphoreType.DMA
        return [dma((tiles,)), dma((2, chunks)), dma((chunks,)), dma((chunks,)), dma((chunks,))]


CHUNK = 256


def later_steps(chain, first, every):
    count = [0]

    def hook():
        count[0] += 1
        chunk = first + count[0] // every - 1
        if count[0] % every == 0 and first <= chunk < chain.chunks:
            chain.step(chunk)

    return hook


EARLY = 3


def first_kernel(rows, cols, x_ref, inverse_ref, shifted_ref, sign_ref, rows_ref, cols_ref, *refs):
    stack, parts, gram_ref, top_ref = refs[:4]
    send_one, recv_one, line_send, line_recv, send_two, recv_two = refs[4:10]
    load, send_row, recv_row, top_send, top_recv = refs[10:15]
    place = Place(rows, cols)
    tile, tiles = x_ref.shape[-1], x_ref.shape[1]
    panel_tiles = BAND // tile
    held = PANELS * panel_tiles
    chain = Chain(place, 0, x_ref, cols_ref, refs[15:])
    spread = Spread(
        place, cols_ref, tuple(range(panel_tiles, 2 * panel_tiles)), top_ref, top_send, top_recv
    )
    first = place.plane == 0

    def spot(col):
        start = pl.multiple_of(lax.rem(col, panel_tiles) * tile, tile)
        return rows_ref.at[col // panel_tiles, :, pl.ds(start, tile)]

    has = place.col < held
    own = spot(lax.rem(place.col, held))
    fill = pltpu.make_async_copy(x_ref.at[:, 0, 0, :], own, load.at[0])

    @pl.when(has)
    def _():
        fill.start()

    chain.start()
    place.greet()
    copies = [
        remote(
            own,
            own,
            send_row.at[step - 1],
            recv_row.at[lax.rem(place.col, held)],
            place.row,
            lax.rem(place.col + step, cols),
        )
        for step in range(1, cols)
    ]
    line = [
        remote(
            gram_ref.at[place.me],
            gram_ref.at[place.me],
            line_send.at[step - 1],
            line_recv.at[0],
            lax.rem(place.row + 2 * step, rows),
            place.col,
        )
        for step in range(1, place.planes)
    ]
    chain.share()
    chain.spread(0, EARLY)

    @pl.when(first)
    def _():
        chain.join()
        width = tile * tiles // 2
        offset = place.core * width
        lanes = lax.broadcasted_iota(jnp.int32, (cols_ref.shape[0], width), 1) + offset
        limit = jnp.where(place.col < panel_tiles, tile, 0)
        value = cols_ref[:, pl.ds(pl.multiple_of(offset, tile), width)]
        value = jnp.where(lanes >= limit, value, 0.0)
        gram = mm(value, value, 1, 1)
        size = stack.shape[1]
        for piece in range(stack.shape[0]):
            stack[piece] = gram[piece * size : (piece + 1) * size]
        plane_scatter(place, place.peers(), stack, parts, gram_ref, send_one, recv_one)
        for copy in line:
            copy.start()

    chain.spread(EARLY, chain.chunks)

    @pl.when(place.plane > 0)
    def _():
        line[0].wait_recv()

    gathers = plane_gather(place, gram_ref.at[place.me], send_two, recv_two)
    chain.step(0)
    spread.send()

    @pl.when(has)
    def _():
        fill.wait()
        for copy in copies:
            copy.start()

    for copy in gathers:
        copy.wait()

    def top():
        spread.wait()
        return top_ref[...]

    size = inverse_ref.shape[0]
    orthogonal_top(
        gram_ref[...].reshape(size, size), top, 0, inverse_ref, shifted_ref, sign_ref,
        later_steps(chain, 1, 3),
    )

    @pl.when(first)
    def _():
        for copy in line:
            copy.wait_send()

    spread.finish()

    @pl.when(has)
    def _():
        for copy in copies:
            copy.wait_send()

    for col in range(held):
        @pl.when(place.col != col)
        def _():
            remote(spot(col), spot(col), send_row.at[0], recv_row.at[col], place.row, place.col).wait_recv()

    chain.finish(True)


def first_panel(x4, collective_id):
    rows, cols = lax.axis_size("row"), lax.axis_size("col")
    row_count, tiles, _, tile = x4.shape
    width = tiles * tile
    count = 2 * cols
    pieces = (count, BAND // count, BAND)
    vmem = pl.BlockSpec(memory_space=pltpu.VMEM)
    dma = pltpu.SemaphoreType.DMA
    panel_tiles = BAND // tile
    square = jax.ShapeDtypeStruct((BAND, BAND), x4.dtype)
    return pl.pallas_call(
        functools.partial(first_kernel, rows, cols),
        out_shape=(
            square,
            square,
            jax.ShapeDtypeStruct((1, BAND), x4.dtype),
            jax.ShapeDtypeStruct((PANELS, row_count, BAND), x4.dtype),
            jax.ShapeDtypeStruct((BAND, width), x4.dtype),
        ),
        in_specs=[pl.BlockSpec(memory_space=pltpu.HBM)],
        out_specs=(vmem,) * 5,
        scratch_shapes=[
            pltpu.VMEM(pieces, x4.dtype),
            pltpu.VMEM((count - 1,) + pieces[1:], x4.dtype),
            pltpu.VMEM(pieces, x4.dtype),
            pltpu.VMEM((BAND, BAND), x4.dtype),
            dma((count - 1,)),
            dma((count - 1,)),
            dma((rows // 2 - 1,)),
            dma((1,)),
            dma((count - 1,)),
            dma((count - 1,)),
            dma((1,)),
            dma((cols - 1,)),
            dma((PANELS * panel_tiles,)),
            dma((panel_tiles, count - 1)),
            dma((panel_tiles, 2)),
        ]
        + Chain.semaphores(tiles, width // CHUNK),
        compiler_params=pltpu.CompilerParams(
            collective_id=collective_id, has_side_effects=True, vmem_limit_bytes=SMALL
        ),
    )(x4)


def next_kernel(rows, cols, gram_in, panel_ref, x_ref, inverse_ref, shifted_ref, sign_ref, cols_ref, *refs):
    near, near_sum, parts, gram_ref, top_ref = refs[:5]
    near_send, near_recv, line_send, line_recv, send_two, recv_two = refs[5:11]
    top_line_send, top_line_recv, top_send, top_recv = refs[11:15]
    place = Place(rows, cols)
    tile = x_ref.shape[-1]
    panel_tiles = BAND // tile
    number = 2 * panel_tiles
    chain = Chain(place, 1, x_ref, cols_ref, refs[15:])
    chain.start()
    place.greet()
    swap = remote(
        gram_in.at[place.col, 1 - place.core], near.at[0], near_send.at[0], near_recv.at[0],
        place.other, place.col,
    )
    swap.start()

    top_plane = number % rows // 2
    start = pl.multiple_of(place.core * tile, tile)
    local = number // rows * tile
    block = panel_ref.at[pl.ds(local, tile), :]
    target = top_ref.at[pl.ds(start, tile), :]
    at_top = place.plane == top_plane

    def top_line(step):
        return remote(
            block, target, top_line_send.at[step - 1], top_line_recv.at[0],
            lax.rem(place.row + 2 * step, rows), place.col,
        )

    top_near = remote(target, target, top_send.at[0], top_recv.at[0], place.other, place.col)
    top_first = remote(block, target, top_send.at[0], top_recv.at[0], place.other, place.col)

    swap.wait_recv()
    near_sum[0] = gram_in[place.col, place.core] + near[0]
    line = [
        remote(
            near_sum.at[0], parts.at[step - 1], line_send.at[step - 1], line_recv.at[step - 1],
            lax.rem(place.row + 2 * step, rows), place.col,
        )
        for step in range(1, place.planes)
    ]
    for copy in line:
        copy.start()

    @pl.when(at_top)
    def _():
        for step in range(1, place.planes):
            top_line(step).start()
        top_first.start()
        target[...] = block[...]

    chain.share()
    chain.spread(0, chain.chunks)
    total = near_sum[0]
    for slot, copy in enumerate(line):
        copy.wait_recv()
        total = total + parts[slot]
    piece = 2 * place.col + place.core
    gram_ref[piece] = total
    gathers = plane_gather(place, gram_ref.at[piece], send_two, recv_two)

    @pl.when(jnp.logical_not(at_top))
    def _():
        top_line(1).wait_recv()
        top_near.start()

    for copy in gathers:
        copy.wait()

    def top():
        top_near.wait_recv()
        return top_ref[...]

    size = inverse_ref.shape[0]
    orthogonal_top(
        gram_ref[...].reshape(size, size), top, 1, inverse_ref, shifted_ref, sign_ref,
        later_steps(chain, 0, 3),
    )
    swap.wait_send()
    for copy in line:
        copy.wait_send()
    top_near.wait_send()

    @pl.when(at_top)
    def _():
        for step in range(1, place.planes):
            top_line(step).wait_send()

    chain.finish()


def next_panel(gram, panel_rows, x4, collective_id):
    rows, cols = lax.axis_size("row"), lax.axis_size("col")
    _, tiles, _, tile = x4.shape
    width = tiles * tile
    count = 2 * cols
    piece = (BAND // count, BAND)
    planes = rows // 2
    vmem = pl.BlockSpec(memory_space=pltpu.VMEM)
    dma = pltpu.SemaphoreType.DMA
    square = jax.ShapeDtypeStruct((BAND, BAND), x4.dtype)
    return pl.pallas_call(
        functools.partial(next_kernel, rows, cols),
        out_shape=(
            square,
            square,
            jax.ShapeDtypeStruct((1, BAND), x4.dtype),
            jax.ShapeDtypeStruct((BAND, width), x4.dtype),
        ),
        in_specs=[vmem, vmem, pl.BlockSpec(memory_space=pltpu.HBM)],
        out_specs=(vmem,) * 4,
        scratch_shapes=[
            pltpu.VMEM((1,) + piece, x4.dtype),
            pltpu.VMEM((1,) + piece, x4.dtype),
            pltpu.VMEM((planes - 1,) + piece, x4.dtype),
            pltpu.VMEM((count,) + piece, x4.dtype),
            pltpu.VMEM((BAND, BAND), x4.dtype),
            dma((1,)),
            dma((1,)),
            dma((planes - 1,)),
            dma((planes - 1,)),
            dma((count - 1,)),
            dma((count - 1,)),
            dma((planes - 1,)),
            dma((1,)),
            dma((1,)),
            dma((1,)),
        ]
        + Chain.semaphores(tiles, width // CHUNK),
        compiler_params=pltpu.CompilerParams(
            collective_id=collective_id, has_side_effects=True, vmem_limit_bytes=SMALL
        ),
    )(gram.reshape((cols, 2) + piece), panel_rows, x4)


def split(value):
    high = value.astype(jnp.bfloat16)
    return high, (value - high.astype(jnp.float32)).astype(jnp.bfloat16)


def split_outside(value):
    high = lax.reduce_precision(value, 8, 7)
    return high.astype(jnp.bfloat16), (value - high).astype(jnp.bfloat16)


def dot(a, b):
    return jnp.dot(a, b, preferred_element_type=jnp.float32)


def apply_kernel(rows, cols, fixed, *refs):
    place = Place(rows, cols)
    x_ref, left_ref, shifted_ref, sign_ref = refs[:4]
    if fixed:
        old_high, old_low, new_high, new_low = refs[4:8]
        kept_ref, store = refs[11], refs[-1]
        refs = refs[:8] + refs[8:11] + refs[12:-1]
    refs = refs[8 if fixed else 4 :]
    out_ref, row_ref, transform_ref = refs[:3]
    block, part, near, pair, left_in, right_in, left_out, right_out = refs[3:11]
    (
        load, near_send, near_recv, left_send, left_recv, right_send, right_recv,
        both_send, both_recv, row_send, row_recv,
    ) = refs[11:]
    plane, core, planes = place.plane, place.core, place.planes
    tile = x_ref.shape[-1]
    chunks = block.shape[0]
    half = left_ref.shape[0] // 2

    def load_of(chunk, index):
        return pltpu.make_async_copy(
            x_ref.at[:, 2 * chunk + index, 0, :],
            block.at[chunk, :, pl.ds(index * tile, tile)],
            load.at[chunk, index],
        )

    row_count = x_ref.shape[0]
    group = row_count // 5 if row_count % 40 == 0 else row_count

    def store_of(chunk, index):
        return pltpu.make_async_copy(
            block.at[chunk, :, pl.ds(index * tile, tile)],
            kept_ref.at[:, 2 * chunk + index, 0, :],
            store.at[chunk, index],
        )

    for chunk in range(chunks):
        for index in range(2):
            load_of(chunk, index).start()
    place.greet()

    def near_of(chunk):
        return remote(
            part.at[chunk, 1 - core],
            near.at[chunk],
            near_send.at[chunk],
            near_recv.at[chunk],
            place.other,
            place.col,
        )

    def rightward(source, chunk):
        return remote(
            source.at[chunk], left_in.at[chunk], right_send.at[chunk], left_recv.at[chunk],
            lax.rem(place.row + 2, rows), place.col,
        )

    def leftward(source, chunk):
        return remote(
            source.at[chunk], right_in.at[chunk], left_send.at[chunk], right_recv.at[chunk],
            lax.rem(place.row + rows - 2, rows), place.col,
        )

    def joined(chunk):
        near_of(chunk).wait_recv()
        pair[chunk] = part[chunk, core] + near[chunk]

        @pl.when(plane == 0)
        def _():
            rightward(pair, chunk).start()

        @pl.when(plane == planes - 1)
        def _():
            leftward(pair, chunk).start()

    def product(chunk, carry):
        for index in range(2):
            load_of(chunk, index).wait()
        if fixed:
            here = pl.ds(pl.multiple_of(chunk * 2 * tile, 2 * tile), 2 * tile)

            def rows_of(number, inner):
                rows_here = pl.ds(pl.multiple_of(number * group, 8), group)
                high, low = old_high[rows_here, :], old_low[rows_here, :]
                change = dot(high, new_high[:, here]) + (
                    dot(low, new_high[:, here]) + dot(high, new_low[:, here])
                )
                block[chunk, rows_here, :] = block[chunk, rows_here, :] - change
                return inner

            lax.fori_loop(0, row_count // group, rows_of, 0)
            for index in range(2):
                store_of(chunk, index).start()
        high, low = split(block[chunk])
        value = dot(left_ref[...], high)
        value = value[:half] + (value[half:] + dot(left_ref[:half], low))
        part[chunk, 0] = value[:, :tile]
        part[chunk, 1] = value[:, tile:]
        near_of(chunk).start()

        @pl.when(chunk > 0)
        def _():
            joined(chunk - 1)

        return carry

    lax.fori_loop(0, chunks, product, 0)
    joined(chunks - 1)

    left_lag = jnp.maximum(plane - 1, 0)
    right_lag = jnp.maximum(planes - 2 - plane, 0)
    last_lag = jnp.maximum(left_lag, right_lag)
    held = cols * core + place.col
    source = held // 2 == plane
    target_row = 2 * plane + lax.rem(place.col, 2)
    to_self = target_row == place.row

    def spot(chunk):
        start = pl.multiple_of((2 * chunk + core) * tile, tile)
        return out_ref.at[:, pl.ds(start, tile)]

    def both_of(chunk):
        return remote(
            spot(chunk), spot(chunk), both_send.at[chunk], both_recv.at[chunk], place.other, place.col
        )

    def row_of(chunk, step):
        start = pl.multiple_of(chunk * tile, tile)
        return remote(
            spot(chunk),
            row_ref.at[:, pl.ds(start, tile)],
            row_send.at[chunk, step],
            row_recv.at[chunk],
            target_row,
            lax.rem(place.col + step, cols),
        )

    def chain(step, carry):
        index = step - left_lag

        @pl.when((plane > 0) & (index >= 0) & (index < chunks))
        def _():
            rightward(pair, index).wait_recv()

            @pl.when(plane < planes - 1)
            def _():
                right_out[index] = left_in[index] + pair[index]
                rightward(right_out, index).start()

        other = step - right_lag

        @pl.when((plane < planes - 1) & (other >= 0) & (other < chunks))
        def _():
            leftward(pair, other).wait_recv()

            @pl.when(plane > 0)
            def _():
                left_out[other] = right_in[other] + pair[other]
                leftward(left_out, other).start()

        done = step - last_lag

        @pl.when((done >= 0) & (done < chunks))
        def _():
            here = pl.ds(pl.multiple_of((2 * done + core) * tile, tile), tile)

            @pl.when(plane == 0)
            def _():
                out_ref[:, here] = pair[done] + right_in[done]

            @pl.when(plane == planes - 1)
            def _():
                out_ref[:, here] = left_in[done] + pair[done]

            @pl.when((plane > 0) & (plane < planes - 1))
            def _():
                out_ref[:, here] = right_out[done] + right_in[done]

            both_of(done).start()

            @pl.when(source)
            def _():
                for step in range(1, cols):
                    row_of(done, step).start()

                @pl.when(to_self)
                def _():
                    there = pl.ds(pl.multiple_of(done * tile, tile), tile)
                    row_ref[:, there] = out_ref[:, here]

                @pl.when(jnp.logical_not(to_self))
                def _():
                    row_of(done, 0).start()

        return carry

    steps = chunks + planes - 2
    count = [0, 0]

    def hook():
        count[0] += 1
        if count[0] % 2 == 0 and count[1] < steps:
            chain(count[1], 0)
            count[1] += 1

    transform_ref[...] = block_transform(shifted_ref[...], sign_ref[...], hook)
    if count[1] < steps:
        lax.fori_loop(count[1], steps, chain, 0)

    gets = jnp.logical_not(source & to_self)

    def drain(chunk, carry):
        if fixed:
            for index in range(2):
                store_of(chunk, index).wait()
        near_of(chunk).wait_send()
        both_of(chunk).wait()

        @pl.when(plane < planes - 1)
        def _():
            rightward(pair, chunk).wait_send()

        @pl.when(plane > 0)
        def _():
            leftward(pair, chunk).wait_send()

        @pl.when(source)
        def _():
            for step in range(1, cols):
                row_of(chunk, step).wait_send()

            @pl.when(jnp.logical_not(to_self))
            def _():
                row_of(chunk, 0).wait_send()

        @pl.when(gets)
        def _():
            row_of(chunk, 0).wait_recv()

        return carry

    lax.fori_loop(0, chunks, drain, 0)


def apply(x4, left, shifted, signs, more, collective_id):
    rows, cols = lax.axis_size("row"), lax.axis_size("col")
    row_count, tiles, _, tile = x4.shape
    width = tiles * tile
    chunks = tiles // 2
    vmem = pl.BlockSpec(memory_space=pltpu.VMEM)
    hbm = pl.BlockSpec(memory_space=pltpu.HBM)
    dma = pltpu.SemaphoreType.DMA
    piece = (BAND, tile)
    kept = bool(more)
    shapes = (
        jax.ShapeDtypeStruct((BAND, width), jnp.float32),
        jax.ShapeDtypeStruct((BAND, row_count), jnp.float32),
        jax.ShapeDtypeStruct((BAND, BAND), jnp.float32),
    )
    return pl.pallas_call(
        functools.partial(apply_kernel, rows, cols, kept),
        out_shape=shapes + ((jax.ShapeDtypeStruct(x4.shape, x4.dtype),) if kept else ()),
        in_specs=[hbm] + [vmem] * (3 + len(more)),
        out_specs=(vmem,) * 3 + ((hbm,) if kept else ()),
        scratch_shapes=[
            pltpu.VMEM((chunks, row_count, 2 * tile), jnp.float32),
            pltpu.VMEM((chunks, 2) + piece, jnp.float32),
        ]
        + [pltpu.VMEM((chunks,) + piece, jnp.float32)] * 6
        + [dma((chunks, 2))]
        + [dma((chunks,))] * 8
        + [dma((chunks, cols)), dma((chunks,))]
        + ([dma((chunks, 2))] if kept else []),
        compiler_params=pltpu.CompilerParams(
            collective_id=collective_id, has_side_effects=True, vmem_limit_bytes=(52 if kept else 40) * MIB
        ),
    )(x4, left, shifted, signs, *more)


def update_kernel(x_ref, left_high, left_low, right_high, right_low, out_ref, block, result, load, store):
    tile = x_ref.shape[-1]
    chunks = x_ref.shape[1] // 2

    def load_of(chunk, index):
        return pltpu.make_async_copy(
            x_ref.at[:, 2 * chunk + index, 0, :],
            block.at[lax.rem(chunk, 2), :, pl.ds(index * tile, tile)],
            load.at[lax.rem(chunk, 2), index],
        )

    def store_of(chunk, index):
        return pltpu.make_async_copy(
            result.at[lax.rem(chunk, 2), :, pl.ds(index * tile, tile)],
            out_ref.at[:, 2 * chunk + index, 0, :],
            store.at[lax.rem(chunk, 2), index],
        )

    for chunk in range(2):
        for index in range(2):
            load_of(chunk, index).start()

    rows = x_ref.shape[0]
    group = rows // 5 if rows % 40 == 0 else rows

    def body(chunk, carry):
        slot = lax.rem(chunk, 2)
        for index in range(2):
            load_of(chunk, index).wait()

        @pl.when(chunk >= 2)
        def _():
            for index in range(2):
                store_of(chunk - 2, index).wait()

        here = pl.ds(pl.multiple_of(chunk * 2 * tile, 2 * tile), 2 * tile)

        def rows_of(number, inner):
            part = pl.ds(pl.multiple_of(number * group, 8), group)
            high, low = left_high[part, :], left_low[part, :]
            value = dot(high, right_high[:, here]) + (
                dot(low, right_high[:, here]) + dot(high, right_low[:, here])
            )
            result[slot, part, :] = block[slot, part, :] - value
            return inner

        lax.fori_loop(0, rows // group, rows_of, 0)
        for index in range(2):
            store_of(chunk, index).start()

        @pl.when(chunk + 2 < chunks)
        def _():
            for index in range(2):
                load_of(chunk + 2, index).start()

        return carry

    lax.fori_loop(0, chunks, body, 0)
    for chunk in range(chunks - 2, chunks):
        for index in range(2):
            store_of(chunk, index).wait()


def update(x4, left, right):
    row_count, tiles, _, tile = x4.shape
    vmem = pl.BlockSpec(memory_space=pltpu.VMEM)
    hbm = pl.BlockSpec(memory_space=pltpu.HBM)
    dma = pltpu.SemaphoreType.DMA
    return pl.pallas_call(
        update_kernel,
        out_shape=jax.ShapeDtypeStruct(x4.shape, x4.dtype),
        in_specs=[hbm] + [vmem] * 4,
        out_specs=hbm,
        scratch_shapes=[pltpu.VMEM((2, row_count, 2 * tile), jnp.float32)] * 2
        + [dma((2, 2)), dma((2, 2))],
        compiler_params=pltpu.CompilerParams(vmem_limit_bytes=48 * MIB),
    )(x4, *left, *right)


def on_device(matrix_tiles):
    tile_shape = matrix_tiles.shape
    block_rows, _, tile_size, block_cols = tile_shape[:4]
    row_count = block_rows * tile_size
    col_count = block_cols * tile_size
    row_devices = lax.axis_size("row")
    col_devices = lax.axis_size("col")
    row_index = lax.axis_index("row")
    col_index = lax.axis_index("col")
    panel_tiles = BAND // tile_size
    assert row_devices == 2 * col_devices and PANELS * panel_tiles <= col_devices
    high = lax.Precision.HIGH
    x4 = matrix_tiles.reshape(row_count, block_cols, 1, tile_size)

    def positions(count, devices, index):
        place = jnp.arange(count, dtype=jnp.int32)
        return (place // tile_size * devices + index) * tile_size + place % tile_size

    global_rows = positions(row_count, row_devices, row_index)
    global_cols = positions(col_count, col_devices, col_index)
    band = jnp.arange(BAND, dtype=jnp.int32)
    inverse, shifted, signs, rows_held, panel_cols = first_panel(x4, 0)
    panel_rows = rows_held[0]
    kept, more = x4, ()
    for panel_index in range(PANELS):
        below = (panel_index + 1) * BAND
        last = panel_index == PANELS - 1
        panel_rows = jnp.where((global_rows >= below)[:, None], panel_rows, 0.0)
        panel_cols = jnp.where((global_cols >= below)[None, :], panel_cols, 0.0)
        unit_rows = (global_rows[:, None] - below == band[None, :]).astype(jnp.float32)
        unit_rows_t = (band[:, None] == global_rows[None, :] - below).astype(jnp.float32)
        unit_cols = (band[:, None] == global_cols[None, :] - below).astype(jnp.float32)
        signs_t = signs.reshape(BAND, 1)
        vec_rows = multiply(panel_rows, inverse, 1, 1) - unit_rows * signs
        vec_rows_t = multiply(inverse, panel_rows, 1, 1) - unit_rows_t * signs_t
        vec_cols = multiply(inverse, panel_cols) - unit_cols * signs_t
        sums, sums_rows, transform, *held = apply(
            kept, jnp.concatenate(split_outside(vec_rows_t), 0), shifted, signs, more, 1 + panel_index
        )
        if held:
            kept = held[0]
        applied = multiply(transform, sums, 0, 0)
        applied_rows = multiply(sums_rows, transform, 0, 0)
        inner_part = multiply(vec_cols, applied, 1, 1)
        if last:
            (inner,) = plane_sum(inner_part, 5)
        else:
            first = below // tile_size
            inner, applied_next = plane_sum(
                inner_part, 4, applied, tuple(range(first, first + panel_tiles))
            )
        half_inner = 0.5 * multiply(transform, inner, 0, 0)
        update_rows = applied_rows - multiply(vec_rows, half_inner)
        update_cols = applied - multiply(half_inner, vec_cols, 0, 0)
        left = split_outside(jnp.concatenate([vec_rows, update_rows], 1))
        right = split_outside(jnp.concatenate([update_cols, vec_cols], 0))
        if last:
            return update(kept, left, right).reshape(tile_shape)
        more = left + right
        update_next = applied_next - multiply(half_inner, shifted, 0, 1)
        panel_rows = (
            rows_held[panel_index + 1]
            - multiply(vec_rows, update_next)
            - multiply(update_rows, shifted, 1, 1)
        )
        panel_rows = jnp.where((global_rows >= below + BAND)[:, None], panel_rows, 0.0)
        gram = multiply(panel_rows, panel_rows, 0, 0)
        old_shifted = shifted
        inverse, shifted, signs, panel_cols = next_panel(gram, panel_rows, x4, 3)
        panel_cols = (
            panel_cols - multiply(update_next, vec_cols, 0, 0) - multiply(old_shifted, update_cols)
        )


def solution(mesh):
    return jax.shard_map(
        on_device,
        mesh=mesh,
        in_specs=(P(None, "row", None, None, "col", None),),
        out_specs=P(None, "row", None, None, "col", None),
        check_vma=False,
    )
```

```python
import functools

import jax
import jax.numpy as jnp
from jax import lax
from jax.experimental import pallas as pl
from jax.experimental.pallas import tpu as pltpu
from jax.sharding import PartitionSpec as P

BAND = 256
PANELS = 2
MIB = 1024 * 1024
MESH = pl.DeviceIdType.MESH

HI = lax.Precision.HIGHEST
def mm(a, b, ca, cb):
    return lax.dot_general(a, b, (((ca,), (cb,)), ((), ())), precision=HI, preferred_element_type=jnp.float32)

def base_inverse(block, hook):
    size = block.shape[0]
    wide = (8, 2 * size)
    group = 8
    places = lax.broadcasted_iota(jnp.int32, wide, 0)
    cols = lax.broadcasted_iota(jnp.int32, wide, 1)
    work = []
    for k in range(size // 8):
        unit = jnp.where(places + 8 * k == cols, 1.0, 0.0)[:, :size]
        work.append(jnp.concatenate([block[8 * k : 8 * k + 8], unit], 1))
    for start in range(0, size, group):
        own, offset = divmod(start, 8)
        rows = [jnp.broadcast_to(work[own][offset + i : offset + i + 1], wide) for i in range(group)]
        pivot = [
            [jnp.broadcast_to(rows[i][:, start + j : start + j + 1], wide) for j in range(group)]
            for i in range(group)
        ]
        first = own if offset + group < 8 else own + 1
        columns = [
            [jnp.broadcast_to(work[k][:, start + i : start + i + 1], wide) for i in range(group)]
            for k in range(first, len(work))
        ]
        scaled = []
        for i in range(group):
            inverse = 1.0 / pivot[i][i]
            scaled.append(rows[i] * inverse)
            for j in range(i + 1, group):
                ratio = pivot[i][j] * inverse
                for l in range(j, group):
                    pivot[j][l] = pivot[j][l] - ratio * pivot[i][l]
                rows[j] = rows[j] - ratio * rows[i]
                for column in columns:
                    column[j] = column[j] - ratio * column[i]
        for k, column in zip(range(first, len(work)), columns):
            change = column[0] * scaled[0]
            for i in range(1, group):
                change = change + column[i] * scaled[i]
            if k == own:
                change = jnp.where(places >= offset + group, change, 0.0)
            work[k] = work[k] - change
        for i in range(group):
            work[own] = jnp.where(places == offset + i, rows[i], work[own])
        hook()
    result = []
    for k, value in enumerate(work):
        pivots = jnp.sum(jnp.where(places + 8 * k == cols, value, 0.0), axis=1, keepdims=True)
        result.append(value[:, size:] * (1.0 / jnp.sqrt(pivots)))
    return jnp.concatenate(result, 0)


def factor_inverse(matrix, base, hook):
    size = matrix.shape[0]
    if size <= base:
        return base_inverse(matrix, hook)
    half = size // 2
    first = factor_inverse(matrix[:half, :half], base, hook)
    lower = mm(matrix[half:, :half], first, 1, 1)
    second = factor_inverse(matrix[half:, half:] - mm(lower, lower, 1, 1), base, hook)
    corner = -mm(second, mm(lower, first, 1, 0), 1, 0)
    top = jnp.concatenate([first, jnp.zeros_like(first)], 1)
    return jnp.concatenate([top, jnp.concatenate([corner, second], 1)], 0)

def orthogonal_top(gram, top, top_dim, inverse_ref, shifted_ref, sign_ref, hook):
    size = gram.shape[0]
    inverse = factor_inverse(gram, 64, hook)
    inverse_ref[...] = inverse
    basis = mm(top(), inverse, top_dim, 1)
    rows = lax.broadcasted_iota(jnp.int32, (size, size), 0)
    cols = lax.broadcasted_iota(jnp.int32, (size, size), 1)
    sign_square = jnp.where(rows == cols, jnp.where(basis >= 0, -1.0, 1.0), 0.0)
    shifted_ref[...] = basis - sign_square
    sign_ref[...] = jnp.sum(sign_square, axis=0, keepdims=True)


def block_transform(shifted, signs, hook):
    size = shifted.shape[0]
    outer = factor_inverse(mm(shifted, shifted, 0, 0), 64, hook)
    rows = lax.broadcasted_iota(jnp.int32, (size, size), 0)
    cols = lax.broadcasted_iota(jnp.int32, (size, size), 1)
    sign_column = jnp.sum(jnp.where(rows == cols, signs, 0.0), axis=1, keepdims=True)
    return -sign_column * mm(mm(shifted, outer, 1, 1), outer, 1, 0)


def multiply(first, second, first_dim=1, second_dim=0, precision=HI):
    return lax.dot_general(
        first,
        second,
        (((first_dim,), (second_dim,)), ((), ())),
        precision=precision,
        preferred_element_type=jnp.float32,
    )


def remote(source, target, send_sem, recv_sem, row, col):
    return pltpu.make_async_remote_copy(
        src_ref=source,
        dst_ref=target,
        send_sem=send_sem,
        recv_sem=recv_sem,
        device_id={"row": row, "col": col},
        device_id_type=MESH,
    )


class Place:
    def __init__(self, rows, cols):
        self.rows, self.cols, self.planes = rows, cols, rows // 2
        row = lax.axis_index("row")
        self.col = lax.axis_index("col")
        self.plane = row // 2
        self.core = row % 2
        self.row = row
        self.other = 2 * self.plane + (1 - self.core)
        self.me = self.core * cols + self.col

    def peers(self):
        found = []
        for core_step in range(2):
            for col_step in range(self.cols):
                if core_step or col_step:
                    core = lax.rem(self.core + core_step, 2)
                    col = lax.rem(self.col + col_step, self.cols)
                    found.append((2 * self.plane + core, col, core * self.cols + col))
        return found

    def greet(self, line=True):
        barrier = pltpu.get_barrier_semaphore()
        count = 0
        for row, col, _ in self.peers():
            pl.semaphore_signal(
                barrier, inc=1, device_id={"row": row, "col": col}, device_id_type=MESH
            )
            count += 1
        for step in range(1, self.planes) if line else ():
            row = lax.rem(self.row + 2 * step, self.rows)
            pl.semaphore_signal(
                barrier, inc=1, device_id={"row": row, "col": self.col}, device_id_type=MESH
            )
            count += 1
        pl.semaphore_wait(barrier, count)


def plane_scatter(place, peers, x_ref, parts, out_ref, send_sem, recv_sem):
    copies = []
    for slot, (row, col, piece) in enumerate(peers):
        copies.append(
            remote(
                x_ref.at[piece], parts.at[slot], send_sem.at[slot], recv_sem.at[slot], row, col
            )
        )
        copies[-1].start()
    total = x_ref[place.me]
    for slot, copy in enumerate(copies):
        copy.wait_recv()
        total = total + parts[slot]
    out_ref[place.me] = total
    for copy in copies:
        copy.wait_send()


def plane_gather(place, mine, send_sem, recv_sem):
    copies = []
    for slot, (row, col, _) in enumerate(place.peers()):
        copies.append(remote(mine, mine, send_sem.at[slot], recv_sem.at[slot], row, col))
        copies[-1].start()
    return copies


class Spread:
    def __init__(self, place, source_ref, tiles, target_ref, send_sem, recv_sem):
        self.place, self.source, self.tiles, self.target = place, source_ref, tiles, target_ref
        self.send_sem, self.recv_sem = send_sem, recv_sem
        self.tile = target_ref.shape[0] // 2

    def refs(self, index, core):
        start = pl.multiple_of(core * self.tile, self.tile)
        local = self.tiles[index] // self.place.cols
        return (
            self.source.at[pl.ds(start, self.tile), pl.ds(local * self.tile, self.tile)],
            self.target.at[pl.ds(start, self.tile), pl.ds(index * self.tile, self.tile)],
        )

    def holder(self, index):
        return self.place.col == self.tiles[index] % self.place.cols

    def copies(self, index):
        source, target = self.refs(index, self.place.core)
        return [
            remote(
                source,
                target,
                self.send_sem.at[index, slot],
                self.recv_sem.at[index, self.place.core],
                row,
                col,
            )
            for slot, (row, col, _) in enumerate(self.place.peers())
        ]

    def send(self):
        for index in range(len(self.tiles)):
            @pl.when(self.holder(index))
            def _():
                for copy in self.copies(index):
                    copy.start()
                source, target = self.refs(index, self.place.core)
                target[...] = source[...]

    def wait(self):
        for index in range(len(self.tiles)):
            for core in range(2):
                source, target = self.refs(index, core)

                @pl.when(jnp.logical_not(self.holder(index) & (self.place.core == core)))
                def _():
                    remote(
                        source,
                        target,
                        self.send_sem.at[index, 0],
                        self.recv_sem.at[index, core],
                        self.place.other,
                        self.place.col,
                    ).wait_recv()

    def finish(self):
        for index in range(len(self.tiles)):
            @pl.when(self.holder(index))
            def _():
                for copy in self.copies(index):
                    copy.wait_send()


class Chain:
    def __init__(self, place, source, x_ref, panel_ref, sems):
        self.place, self.source, self.x_ref, self.ref = place, source, x_ref, panel_ref
        self.load, self.sends, self.recv, self.share_send, self.share_recv = sems
        self.tile = x_ref.shape[-1]
        self.tiles = x_ref.shape[1]
        self.chunks = self.recv.shape[0]
        self.width = panel_ref.shape[1] // self.chunks
        self.at_source = place.plane == source

    def loads(self):
        start = pl.multiple_of(self.place.core * self.tile, self.tile)
        for tile in range(self.tiles):
            yield pltpu.make_async_copy(
                self.x_ref.at[pl.ds(0, self.tile), tile, 0, :],
                self.ref.at[pl.ds(start, self.tile), pl.ds(tile * self.tile, self.tile)],
                self.load.at[tile],
            )

    def part(self, chunk):
        start = pl.multiple_of(self.place.core * self.tile, self.tile)
        return self.ref.at[pl.ds(start, self.tile), pl.ds(chunk * self.width, self.width)]

    def hop(self, chunk, step, sem):
        part = self.part(chunk)
        row = lax.rem(self.place.row + 2 * step + self.place.rows, self.place.rows)
        return remote(part, part, self.sends.at[sem, chunk], self.recv.at[chunk], row, self.place.col)

    def shared(self, chunk):
        part = self.part(chunk)
        return remote(
            part,
            part,
            self.share_send.at[chunk],
            self.share_recv.at[chunk],
            self.place.other,
            self.place.col,
        )

    def start(self):
        @pl.when(self.at_source)
        def _():
            for copy in self.loads():
                copy.start()

    def share(self):
        @pl.when(self.at_source)
        def _():
            for copy in self.loads():
                copy.wait()
            for chunk in range(self.chunks):
                self.shared(chunk).start()

    def spread(self, first, last):
        @pl.when(self.at_source)
        def _():
            for chunk in range(first, min(last, self.chunks)):
                if self.source < self.place.planes - 1:
                    self.hop(chunk, 1, 0).start()
                if self.source > 0:
                    self.hop(chunk, -1, 1).start()

    def step(self, chunk):
        place = self.place
        for step, sem, away, more in (
            (1, 0, place.plane > self.source, place.plane < place.planes - 1),
            (-1, 1, place.plane < self.source, place.plane > 0),
        ):
            if step < 0 and self.source == 0 or step > 0 and self.source == place.planes - 1:
                continue

            @pl.when(away)
            def _():
                self.hop(chunk, step, sem).wait_recv()

                @pl.when(more)
                def _():
                    self.hop(chunk, step, sem).start()

                self.shared(chunk).start()

    def join(self):
        for chunk in range(self.chunks):
            self.shared(chunk).wait_recv()

    def finish(self, joined=False):
        place = self.place
        if joined:
            @pl.when(jnp.logical_not(self.at_source))
            def _():
                self.join()
        else:
            self.join()
        for chunk in range(self.chunks):
            self.shared(chunk).wait_send()
        for step, sem, sent in (
            (1, 0, (place.plane >= self.source) & (place.plane < place.planes - 1)),
            (-1, 1, (place.plane <= self.source) & (place.plane > 0)),
        ):

            @pl.when(sent)
            def _():
                for chunk in range(self.chunks):
                    self.hop(chunk, step, sem).wait_send()

    @staticmethod
    def semaphores(tiles, chunks):
        dma = pltpu.SemaphoreType.DMA
        return [dma((tiles,)), dma((2, chunks)), dma((chunks,)), dma((chunks,)), dma((chunks,))]


CHUNK = 256


def later_steps(chain, first, every):
    count = [0]

    def hook():
        count[0] += 1
        chunk = first + count[0] // every - 1
        if count[0] % every == 0 and first <= chunk < chain.chunks:
            chain.step(chunk)

    return hook


EARLY = 3


def first_kernel(rows, cols, x_ref, inverse_ref, shifted_ref, sign_ref, rows_ref, cols_ref, *refs):
    stack, parts, gram_ref, top_ref = refs[:4]
    send_one, recv_one, line_send, line_recv, send_two, recv_two = refs[4:10]
    load, send_row, recv_row, top_send, top_recv = refs[10:15]
    place = Place(rows, cols)
    tile, tiles = x_ref.shape[-1], x_ref.shape[1]
    panel_tiles = BAND // tile
    held = PANELS * panel_tiles
    chain = Chain(place, 0, x_ref, cols_ref, refs[15:])
    spread = Spread(
        place, cols_ref, tuple(range(panel_tiles, 2 * panel_tiles)), top_ref, top_send, top_recv
    )
    first = place.plane == 0

    def spot(col):
        start = pl.multiple_of(lax.rem(col, panel_tiles) * tile, tile)
        return rows_ref.at[col // panel_tiles, :, pl.ds(start, tile)]

    has = place.col < held
    own = spot(lax.rem(place.col, held))
    fill = pltpu.make_async_copy(x_ref.at[:, 0, 0, :], own, load.at[0])

    @pl.when(has)
    def _():
        fill.start()

    chain.start()
    place.greet()
    copies = [
        remote(
            own,
            own,
            send_row.at[step - 1],
            recv_row.at[lax.rem(place.col, held)],
            place.row,
            lax.rem(place.col + step, cols),
        )
        for step in range(1, cols)
    ]
    line = [
        remote(
            gram_ref.at[place.me],
            gram_ref.at[place.me],
            line_send.at[step - 1],
            line_recv.at[0],
            lax.rem(place.row + 2 * step, rows),
            place.col,
        )
        for step in range(1, place.planes)
    ]
    chain.share()
    chain.spread(0, EARLY)

    @pl.when(first)
    def _():
        chain.join()
        width = tile * tiles // 2
        offset = place.core * width
        lanes = lax.broadcasted_iota(jnp.int32, (cols_ref.shape[0], width), 1) + offset
        limit = jnp.where(place.col < panel_tiles, tile, 0)
        value = cols_ref[:, pl.ds(pl.multiple_of(offset, tile), width)]
        value = jnp.where(lanes >= limit, value, 0.0)
        gram = mm(value, value, 1, 1)
        size = stack.shape[1]
        for piece in range(stack.shape[0]):
            stack[piece] = gram[piece * size : (piece + 1) * size]
        plane_scatter(place, place.peers(), stack, parts, gram_ref, send_one, recv_one)
        for copy in line:
            copy.start()

    chain.spread(EARLY, chain.chunks)

    @pl.when(place.plane > 0)
    def _():
        line[0].wait_recv()

    gathers = plane_gather(place, gram_ref.at[place.me], send_two, recv_two)
    chain.step(0)
    spread.send()

    @pl.when(has)
    def _():
        fill.wait()
        for copy in copies:
            copy.start()

    for copy in gathers:
        copy.wait()

    def top():
        spread.wait()
        return top_ref[...]

    size = inverse_ref.shape[0]
    orthogonal_top(
        gram_ref[...].reshape(size, size), top, 0, inverse_ref, shifted_ref, sign_ref,
        later_steps(chain, 1, 3),
    )

    @pl.when(first)
    def _():
        for copy in line:
            copy.wait_send()

    spread.finish()

    @pl.when(has)
    def _():
        for copy in copies:
            copy.wait_send()

    for col in range(held):
        @pl.when(place.col != col)
        def _():
            remote(spot(col), spot(col), send_row.at[0], recv_row.at[col], place.row, place.col).wait_recv()

    chain.finish(True)


def first_panel(x4, collective_id):
    rows, cols = lax.axis_size("row"), lax.axis_size("col")
    row_count, tiles, _, tile = x4.shape
    width = tiles * tile
    count = 2 * cols
    pieces = (count, BAND // count, BAND)
    vmem = pl.BlockSpec(memory_space=pltpu.VMEM)
    dma = pltpu.SemaphoreType.DMA
    panel_tiles = BAND // tile
    square = jax.ShapeDtypeStruct((BAND, BAND), x4.dtype)
    return pl.pallas_call(
        functools.partial(first_kernel, rows, cols),
        out_shape=(
            square,
            square,
            jax.ShapeDtypeStruct((1, BAND), x4.dtype),
            jax.ShapeDtypeStruct((PANELS, row_count, BAND), x4.dtype),
            jax.ShapeDtypeStruct((BAND, width), x4.dtype),
        ),
        in_specs=[pl.BlockSpec(memory_space=pltpu.HBM)],
        out_specs=(vmem,) * 5,
        scratch_shapes=[
            pltpu.VMEM(pieces, x4.dtype),
            pltpu.VMEM((count - 1,) + pieces[1:], x4.dtype),
            pltpu.VMEM(pieces, x4.dtype),
            pltpu.VMEM((BAND, BAND), x4.dtype),
            dma((count - 1,)),
            dma((count - 1,)),
            dma((rows // 2 - 1,)),
            dma((1,)),
            dma((count - 1,)),
            dma((count - 1,)),
            dma((1,)),
            dma((cols - 1,)),
            dma((PANELS * panel_tiles,)),
            dma((panel_tiles, count - 1)),
            dma((panel_tiles, 2)),
        ]
        + Chain.semaphores(tiles, width // CHUNK),
        compiler_params=pltpu.CompilerParams(
            collective_id=collective_id, has_side_effects=True, vmem_limit_bytes=56 * MIB
        ),
    )(x4)


def next_kernel(rows, cols, below, *refs):
    refs = list(refs)
    take = lambda count: [refs.pop(0) for _ in range(count)]
    (
        vec_rows, applied_rows, vec_cols, applied, transform_ref, inner_ref, applied_next,
        old_ref, later_ref, x_ref,
    ) = take(10)
    inverse_ref, shifted_ref, sign_ref, panel_ref, cols_ref = take(5)
    old_high, old_low, new_high, new_low, update_ref, ahead_ref = take(6)
    gram_in, gram_sum = take(2)
    near, near_sum, parts, gram_ref, top_ref = refs[:5]
    near_send, near_recv, line_send, line_recv, send_two, recv_two = refs[5:11]
    top_line_send, top_line_recv, top_send, top_recv = refs[11:15]
    place = Place(rows, cols)
    tile = x_ref.shape[-1]
    panel_tiles = BAND // tile
    number = 2 * panel_tiles
    chain = Chain(place, 1, x_ref, cols_ref, refs[15:])
    chain.start()
    place.greet()
    chain.share()
    chain.spread(0, 2 * EARLY)
    size = BAND
    half = 0.5 * mm(transform_ref[...], inner_ref[...], 0, 0)
    ahead_ref[...] = applied_next[...] - mm(half, old_ref[...], 0, 1)
    gram_sum[...] = jnp.zeros_like(gram_sum)

    def own_rows(index, carry):
        here = pl.ds(pl.multiple_of(index * tile, tile), tile)
        vec = vec_rows[here, :]
        change = applied_rows[here, :] - mm(vec, half, 1, 0)
        panel = later_ref[here, :] - mm(vec, ahead_ref[...], 1, 0) - mm(change, old_ref[...], 1, 1)
        first = (index * rows + place.row) * tile
        panel = jnp.where(first >= below + BAND, panel, 0.0)
        panel_ref[here, :] = panel
        gram_sum[...] += mm(panel, panel, 0, 0)
        for start, value in ((0, vec), (size, change)):
            high, low = split(value)
            old_high[here, start : start + size] = high
            old_low[here, start : start + size] = low
        return carry

    lax.fori_loop(0, panel_ref.shape[0] // tile, own_rows, 0)
    height = gram_in.shape[2]
    for col in range(cols):
        for core in range(2):
            start = (2 * col + core) * height
            gram_in[col, core] = gram_sum[start : start + height, :]
    swap = remote(
        gram_in.at[place.col, 1 - place.core], near.at[0], near_send.at[0], near_recv.at[0],
        place.other, place.col,
    )
    swap.start()

    top_plane = number % rows // 2
    start = pl.multiple_of(place.core * tile, tile)
    local = number // rows * tile
    block = panel_ref.at[pl.ds(local, tile), :]
    target = top_ref.at[pl.ds(start, tile), :]
    at_top = place.plane == top_plane

    def top_line(step):
        return remote(
            block, target, top_line_send.at[step - 1], top_line_recv.at[0],
            lax.rem(place.row + 2 * step, rows), place.col,
        )

    top_near = remote(target, target, top_send.at[0], top_recv.at[0], place.other, place.col)
    top_first = remote(block, target, top_send.at[0], top_recv.at[0], place.other, place.col)

    swap.wait_recv()
    near_sum[0] = gram_in[place.col, place.core] + near[0]
    line = [
        remote(
            near_sum.at[0], parts.at[step - 1], line_send.at[step - 1], line_recv.at[step - 1],
            lax.rem(place.row + 2 * step, rows), place.col,
        )
        for step in range(1, place.planes)
    ]
    for copy in line:
        copy.start()

    @pl.when(at_top)
    def _():
        for step in range(1, place.planes):
            top_line(step).start()
        top_first.start()
        target[...] = block[...]

    chain.spread(2 * EARLY, chain.chunks)

    def own_cols(index, carry):
        here = pl.ds(pl.multiple_of(index * 2 * tile, 2 * tile), 2 * tile)
        vec = vec_cols[:, here]
        change = applied[:, here] - mm(half, vec, 0, 0)
        update_ref[:, here] = change
        for start, value in ((0, change), (size, vec)):
            high, low = split(value)
            new_high[start : start + size, here] = high
            new_low[start : start + size, here] = low
        return carry

    lax.fori_loop(0, x_ref.shape[1] // 2, own_cols, 0)
    total = near_sum[0]
    for slot, copy in enumerate(line):
        copy.wait_recv()
        total = total + parts[slot]
    piece = 2 * place.col + place.core
    gram_ref[piece] = total
    gathers = plane_gather(place, gram_ref.at[piece], send_two, recv_two)

    @pl.when(jnp.logical_not(at_top))
    def _():
        top_line(1).wait_recv()
        top_near.start()

    for copy in gathers:
        copy.wait()

    def top():
        top_near.wait_recv()
        return top_ref[...]

    orthogonal_top(
        gram_ref[...].reshape(size, size), top, 1, inverse_ref, shifted_ref, sign_ref,
        later_steps(chain, 0, 3),
    )
    swap.wait_send()
    for copy in line:
        copy.wait_send()
    top_near.wait_send()

    @pl.when(at_top)
    def _():
        for step in range(1, place.planes):
            top_line(step).wait_send()

    chain.finish()


def next_panel(operands, x4, below, collective_id):
    rows, cols = lax.axis_size("row"), lax.axis_size("col")
    row_count, tiles, _, tile = x4.shape
    width = tiles * tile
    count = 2 * cols
    piece = (BAND // count, BAND)
    planes = rows // 2
    vmem = pl.BlockSpec(memory_space=pltpu.VMEM)
    dma = pltpu.SemaphoreType.DMA
    f32, bf16 = jnp.float32, jnp.bfloat16
    shape = jax.ShapeDtypeStruct
    square = shape((BAND, BAND), f32)
    return pl.pallas_call(
        functools.partial(next_kernel, rows, cols, below),
        out_shape=(
            square,
            square,
            shape((1, BAND), f32),
            shape((row_count, BAND), f32),
            shape((BAND, width), f32),
            shape((row_count, 2 * BAND), bf16),
            shape((row_count, 2 * BAND), bf16),
            shape((2 * BAND, width), bf16),
            shape((2 * BAND, width), bf16),
            shape((BAND, width), f32),
            square,
        ),
        in_specs=[vmem] * len(operands) + [pl.BlockSpec(memory_space=pltpu.HBM)],
        out_specs=(vmem,) * 11,
        scratch_shapes=[
            pltpu.VMEM((cols, 2) + piece, f32),
            pltpu.VMEM((BAND, BAND), f32),
            pltpu.VMEM((1,) + piece, f32),
            pltpu.VMEM((1,) + piece, f32),
            pltpu.VMEM((planes - 1,) + piece, f32),
            pltpu.VMEM((count,) + piece, f32),
            pltpu.VMEM((BAND, BAND), f32),
            dma((1,)),
            dma((1,)),
            dma((planes - 1,)),
            dma((planes - 1,)),
            dma((count - 1,)),
            dma((count - 1,)),
            dma((planes - 1,)),
            dma((1,)),
            dma((1,)),
            dma((1,)),
        ]
        + Chain.semaphores(tiles, width // CHUNK),
        compiler_params=pltpu.CompilerParams(
            collective_id=collective_id, has_side_effects=True, vmem_limit_bytes=44 * MIB
        ),
    )(*operands, x4)


def split(value):
    high = value.astype(jnp.bfloat16)
    return high, (value - high.astype(jnp.float32)).astype(jnp.bfloat16)


def split_outside(value):
    high = lax.reduce_precision(value, 8, 7)
    return high.astype(jnp.bfloat16), (value - high).astype(jnp.bfloat16)


def dot(a, b):
    return jnp.dot(a, b, preferred_element_type=jnp.float32)


def apply_kernel(rows, cols, below, tiles, fixed, *refs):
    place = Place(rows, cols)
    refs = list(refs)
    take = lambda count: [refs.pop(0) for _ in range(count)]
    x_ref, left_ref, shifted_ref, sign_ref, inverse_ref, panel_ref = take(6)
    old_high, old_low, new_high, new_low = take(4) if fixed else [None] * 4
    row_ref, transform_ref, vec_ref, applied_ref, inner_ref = take(5)
    next_ref = take(1)[0] if tiles else None
    kept_ref = take(1)[0] if fixed else None
    block, part, near, pair, left_in, right_in, left_out, right_out, out_ref = take(9)
    total_ref, stack, parts = take(3)
    (
        load, near_send, near_recv, left_send, left_recv, right_send, right_recv,
        both_send, both_recv, row_send, row_recv, send_one, recv_one, send_two, recv_two,
    ) = take(15)
    next_sems = take(2) if tiles else None
    store = take(1)[0] if fixed else None
    plane, core, planes = place.plane, place.core, place.planes
    tile = x_ref.shape[-1]
    chunks = block.shape[0]
    pieces = pair.shape[0] // chunks
    depth = pair.shape[1]
    subs = chunks * pieces
    size = left_ref.shape[0] // 2

    def load_of(chunk, index):
        return pltpu.make_async_copy(
            x_ref.at[:, 2 * chunk + index, 0, :],
            block.at[chunk, :, pl.ds(index * tile, tile)],
            load.at[chunk, index],
        )

    def store_of(chunk, index):
        return pltpu.make_async_copy(
            block.at[chunk, :, pl.ds(index * tile, tile)],
            kept_ref.at[:, 2 * chunk + index, 0, :],
            store.at[chunk, index],
        )

    for chunk in range(chunks):
        for index in range(2):
            load_of(chunk, index).start()
    place.greet()

    def near_of(chunk):
        return remote(
            part.at[chunk, 1 - core],
            near.at[chunk],
            near_send.at[chunk],
            near_recv.at[chunk],
            place.other,
            place.col,
        )

    def rightward(source, index):
        return remote(
            source.at[index], left_in.at[index], right_send.at[index], left_recv.at[index],
            lax.rem(place.row + 2, rows), place.col,
        )

    def leftward(source, index):
        return remote(
            source.at[index], right_in.at[index], left_send.at[index], right_recv.at[index],
            lax.rem(place.row + rows - 2, rows), place.col,
        )

    def joined(chunk):
        near_of(chunk).wait_recv()
        for piece in range(pieces):
            pair[chunk * pieces + piece] = part[chunk, core, piece] + near[chunk, piece]

        @pl.when(plane == 0)
        def _():
            for piece in range(pieces):
                rightward(pair, chunk * pieces + piece).start()

        @pl.when(plane == planes - 1)
        def _():
            for piece in range(pieces):
                leftward(pair, chunk * pieces + piece).start()

    def product(chunk, carry):
        for index in range(2):
            load_of(chunk, index).wait()
        if fixed:
            here = pl.ds(pl.multiple_of(chunk * 2 * tile, 2 * tile), 2 * tile)
            change = dot(old_high[...], new_high[:, here]) + (
                dot(old_low[...], new_high[:, here]) + dot(old_high[...], new_low[:, here])
            )
            block[chunk] = block[chunk] - change
            for index in range(2):
                store_of(chunk, index).start()
        high, low = split(block[chunk])
        value = dot(left_ref[...], high)
        value = value[:size] + (value[size:] + dot(left_ref[:size], low))
        for index in range(2):
            for piece in range(pieces):
                part[chunk, index, piece] = value[
                    piece * depth : (piece + 1) * depth, index * tile : (index + 1) * tile
                ]
        near_of(chunk).start()

        @pl.when(chunk > 0)
        def _():
            joined(chunk - 1)

        return carry

    lax.fori_loop(0, chunks, product, 0)
    joined(chunks - 1)

    left_lag = jnp.maximum(plane - 1, 0)
    right_lag = jnp.maximum(planes - 2 - plane, 0)
    last_lag = jnp.maximum(left_lag, right_lag)
    held = cols * core + place.col
    source = held // 2 == plane
    target_row = 2 * plane + lax.rem(place.col, 2)
    to_self = target_row == place.row

    def depths(index):
        return pl.ds(pl.multiple_of(lax.rem(index, pieces) * depth, depth), depth)

    def lanes(index):
        return pl.ds(pl.multiple_of((2 * (index // pieces) + core) * tile, tile), tile)

    def row_lanes(index):
        return pl.ds(pl.multiple_of(index // pieces * tile, tile), tile)

    def both_of(index):
        spot = out_ref.at[depths(index), lanes(index)]
        return remote(spot, spot, both_send.at[index], both_recv.at[index], place.other, place.col)

    def row_of(index, step):
        return remote(
            out_ref.at[depths(index), lanes(index)],
            row_ref.at[depths(index), row_lanes(index)],
            row_send.at[index, step],
            row_recv.at[index],
            target_row,
            lax.rem(place.col + step, cols),
        )

    def chain(step, carry):
        index = step - left_lag

        @pl.when((plane > 0) & (index >= 0) & (index < subs))
        def _():
            rightward(pair, index).wait_recv()

            @pl.when(plane < planes - 1)
            def _():
                right_out[index] = left_in[index] + pair[index]
                rightward(right_out, index).start()

        other = step - right_lag

        @pl.when((plane < planes - 1) & (other >= 0) & (other < subs))
        def _():
            leftward(pair, other).wait_recv()

            @pl.when(plane > 0)
            def _():
                left_out[other] = right_in[other] + pair[other]
                leftward(left_out, other).start()

        done = step - last_lag

        @pl.when((done >= 0) & (done < subs))
        def _():
            @pl.when(plane == 0)
            def _():
                out_ref[depths(done), lanes(done)] = pair[done] + right_in[done]

            @pl.when(plane == planes - 1)
            def _():
                out_ref[depths(done), lanes(done)] = left_in[done] + pair[done]

            @pl.when((plane > 0) & (plane < planes - 1))
            def _():
                out_ref[depths(done), lanes(done)] = right_out[done] + right_in[done]

            both_of(done).start()

            @pl.when(source)
            def _():
                for step in range(1, cols):
                    row_of(done, step).start()

                @pl.when(to_self)
                def _():
                    row_ref[depths(done), row_lanes(done)] = out_ref[depths(done), lanes(done)]

                @pl.when(jnp.logical_not(to_self))
                def _():
                    row_of(done, 0).start()

        return carry

    steps = subs + planes - 2
    count = [0, 0]

    def hook():
        count[0] += 1
        if count[0] % 3 == 0 and count[1] < steps:
            chain(count[1], 0)
            count[1] += 1

    transform_ref[...] = block_transform(shifted_ref[...], sign_ref[...], hook)
    total_ref[...] = jnp.zeros_like(total_ref)
    diagonal = lax.broadcasted_iota(jnp.int32, (size, size), 0)
    lane = lax.broadcasted_iota(jnp.int32, (size, 2 * tile), 1)
    band = lax.broadcasted_iota(jnp.int32, (size, 2 * tile), 0)
    sign_column = jnp.sum(
        jnp.where(diagonal == lax.broadcasted_iota(jnp.int32, (size, size), 1), sign_ref[...], 0.0),
        axis=1,
        keepdims=True,
    )

    def finished(chunk):
        for piece in range(pieces):
            both_of(chunk * pieces + piece).wait_recv()
        here = pl.ds(pl.multiple_of(chunk * 2 * tile, 2 * tile), 2 * tile)
        second = jnp.where(lane >= tile, 1, 0)
        place_of = ((2 * chunk + second) * cols + place.col) * tile + lane - second * tile - below
        vec = mm(inverse_ref[...], jnp.where(place_of >= 0, panel_ref[:, here], 0.0), 1, 0)
        vec = vec - jnp.where(place_of == band, sign_column, 0.0)
        vec_ref[:, here] = vec
        applied = mm(transform_ref[...], out_ref[:, here], 0, 0)
        applied_ref[:, here] = applied
        total_ref[...] += mm(vec, applied, 1, 1)

    done_steps = count[1]
    early = 0
    while early < chunks and pieces * (early + 1) + planes - 2 <= done_steps + early + 1 and done_steps + early < steps:
        early += 1

    def paired(chunk, carry):
        chain(done_steps + chunk, 0)
        finished(chunk)
        return carry

    def alone(chunk, carry):
        finished(chunk)
        return carry

    lax.fori_loop(0, early, paired, 0)
    if done_steps + early < steps:
        lax.fori_loop(done_steps + early, steps, chain, 0)
    if early < chunks:
        lax.fori_loop(early, chunks, alone, 0)

    height = stack.shape[1]
    for piece in range(stack.shape[0]):
        stack[piece] = total_ref[piece * height : (piece + 1) * height, :]
    if tiles:
        spread = Spread(place, applied_ref, tiles, next_ref, *next_sems)
        spread.send()
    plane_scatter(place, place.peers()[: cols - 1], stack, parts, inner_ref, send_one, recv_one)
    gathers = plane_gather(place, inner_ref.at[place.me], send_two, recv_two)
    gets = jnp.logical_not(source & to_self)

    def drain(index, carry):
        both_of(index).wait_send()

        @pl.when(plane < planes - 1)
        def _():
            rightward(pair, index).wait_send()

        @pl.when(plane > 0)
        def _():
            leftward(pair, index).wait_send()

        @pl.when(source)
        def _():
            for step in range(1, cols):
                row_of(index, step).wait_send()

            @pl.when(jnp.logical_not(to_self))
            def _():
                row_of(index, 0).wait_send()

        @pl.when(gets)
        def _():
            row_of(index, 0).wait_recv()

        return carry

    def drain_chunk(chunk, carry):
        if fixed:
            for index in range(2):
                store_of(chunk, index).wait()
        near_of(chunk).wait_send()
        return carry

    lax.fori_loop(0, subs, drain, 0)
    lax.fori_loop(0, chunks, drain_chunk, 0)
    for copy in gathers:
        copy.wait()
    if tiles:
        spread.wait()
        spread.finish()


PIECES = 2


def apply(x4, left, shifted, signs, inverse, panel_cols, below, tiles, more, collective_id):
    rows, cols = lax.axis_size("row"), lax.axis_size("col")
    row_count, held_tiles, _, tile = x4.shape
    width = held_tiles * tile
    chunks = held_tiles // 2
    count = 2 * cols
    vmem = pl.BlockSpec(memory_space=pltpu.VMEM)
    hbm = pl.BlockSpec(memory_space=pltpu.HBM)
    dma = pltpu.SemaphoreType.DMA
    f32 = jnp.float32
    piece = (BAND // PIECES, tile)
    subs = PIECES * chunks
    sums = (count, BAND // count, BAND)
    kept = bool(more)
    square = jax.ShapeDtypeStruct((BAND, BAND), f32)
    wide = jax.ShapeDtypeStruct((BAND, width), f32)
    shapes = (
        jax.ShapeDtypeStruct((BAND, row_count), f32),
        square,
        wide,
        wide,
        jax.ShapeDtypeStruct(sums, f32),
    )
    shapes += (square,) if tiles else ()
    out = pl.pallas_call(
        functools.partial(apply_kernel, rows, cols, below, tiles, kept),
        out_shape=shapes + ((jax.ShapeDtypeStruct(x4.shape, x4.dtype),) if kept else ()),
        in_specs=[hbm] + [vmem] * (5 + len(more)),
        out_specs=(vmem,) * len(shapes) + ((hbm,) if kept else ()),
        scratch_shapes=[
            pltpu.VMEM((chunks, row_count, 2 * tile), f32),
            pltpu.VMEM((chunks, 2, PIECES) + piece, f32),
            pltpu.VMEM((chunks, PIECES) + piece, f32),
        ]
        + [pltpu.VMEM((subs,) + piece, f32)] * 5
        + [
            pltpu.VMEM((BAND, width), f32),
            pltpu.VMEM((BAND, BAND), f32),
            pltpu.VMEM(sums, f32),
            pltpu.VMEM((cols - 1,) + sums[1:], f32),
        ]
        + [dma((chunks, 2)), dma((chunks,)), dma((chunks,))]
        + [dma((subs,))] * 6
        + [dma((subs, cols)), dma((subs,))]
        + [dma((cols - 1,))] * 2
        + [dma((count - 1,))] * 2
        + ([dma((len(tiles), count - 1)), dma((len(tiles), 2))] if tiles else [])
        + ([dma((chunks, 2))] if kept else []),
        compiler_params=pltpu.CompilerParams(
            collective_id=collective_id, has_side_effects=True, vmem_limit_bytes=(60 if kept else 48) * MIB
        ),
    )(x4, left, shifted, signs, inverse, panel_cols, *more)
    out = list(out)
    out[4] = out[4].reshape(BAND, BAND)
    return out


def update_kernel(x_ref, left_high, left_low, right_high, right_low, out_ref, block, result, load, store):
    tile = x_ref.shape[-1]
    chunks = x_ref.shape[1] // 2

    def load_of(chunk, index):
        return pltpu.make_async_copy(
            x_ref.at[:, 2 * chunk + index, 0, :],
            block.at[lax.rem(chunk, 2), :, pl.ds(index * tile, tile)],
            load.at[lax.rem(chunk, 2), index],
        )

    def store_of(chunk, index):
        return pltpu.make_async_copy(
            result.at[lax.rem(chunk, 2), :, pl.ds(index * tile, tile)],
            out_ref.at[:, 2 * chunk + index, 0, :],
            store.at[lax.rem(chunk, 2), index],
        )

    for chunk in range(2):
        for index in range(2):
            load_of(chunk, index).start()

    def body(chunk, carry):
        slot = lax.rem(chunk, 2)
        for index in range(2):
            load_of(chunk, index).wait()

        @pl.when(chunk >= 2)
        def _():
            for index in range(2):
                store_of(chunk - 2, index).wait()

        here = pl.ds(pl.multiple_of(chunk * 2 * tile, 2 * tile), 2 * tile)
        value = dot(left_high[...], right_high[:, here]) + (
            dot(left_low[...], right_high[:, here]) + dot(left_high[...], right_low[:, here])
        )
        result[slot] = block[slot] - value
        for index in range(2):
            store_of(chunk, index).start()

        @pl.when(chunk + 2 < chunks)
        def _():
            for index in range(2):
                load_of(chunk + 2, index).start()

        return carry

    lax.fori_loop(0, chunks, body, 0)
    for chunk in range(chunks - 2, chunks):
        for index in range(2):
            store_of(chunk, index).wait()


def update(x4, left, right):
    row_count, tiles, _, tile = x4.shape
    vmem = pl.BlockSpec(memory_space=pltpu.VMEM)
    hbm = pl.BlockSpec(memory_space=pltpu.HBM)
    dma = pltpu.SemaphoreType.DMA
    return pl.pallas_call(
        update_kernel,
        out_shape=jax.ShapeDtypeStruct(x4.shape, x4.dtype),
        in_specs=[hbm] + [vmem] * 4,
        out_specs=hbm,
        scratch_shapes=[pltpu.VMEM((2, row_count, 2 * tile), jnp.float32)] * 2
        + [dma((2, 2)), dma((2, 2))],
        compiler_params=pltpu.CompilerParams(vmem_limit_bytes=48 * MIB),
    )(x4, *left, *right)


def on_device(matrix_tiles):
    tile_shape = matrix_tiles.shape
    block_rows, _, tile_size, block_cols = tile_shape[:4]
    row_count = block_rows * tile_size
    col_count = block_cols * tile_size
    row_devices = lax.axis_size("row")
    col_devices = lax.axis_size("col")
    row_index = lax.axis_index("row")
    panel_tiles = BAND // tile_size
    assert row_devices == 2 * col_devices and PANELS * panel_tiles <= col_devices
    x4 = matrix_tiles.reshape(row_count, block_cols, 1, tile_size)

    def positions(count, devices, index):
        place = jnp.arange(count, dtype=jnp.int32)
        return (place // tile_size * devices + index) * tile_size + place % tile_size

    global_rows = positions(row_count, row_devices, row_index)
    band = jnp.arange(BAND, dtype=jnp.int32)
    inverse, shifted, signs, rows_held, panel_cols = first_panel(x4, 0)
    panel_rows = rows_held[0]
    kept, more = x4, ()
    for panel_index in range(PANELS):
        below = (panel_index + 1) * BAND
        last = panel_index == PANELS - 1
        panel_rows = jnp.where((global_rows >= below)[:, None], panel_rows, 0.0)
        unit_rows = (global_rows[:, None] - below == band[None, :]).astype(jnp.float32)
        unit_rows_t = (band[:, None] == global_rows[None, :] - below).astype(jnp.float32)
        vec_rows = multiply(panel_rows, inverse, 1, 1) - unit_rows * signs
        vec_rows_t = multiply(inverse, panel_rows, 1, 1) - unit_rows_t * signs.reshape(BAND, 1)
        first = below // tile_size
        sums_rows, transform, vec_cols, applied, inner, *rest = apply(
            kept,
            jnp.concatenate(split_outside(vec_rows_t), 0),
            shifted,
            signs,
            inverse,
            panel_cols,
            below,
            () if last else tuple(range(first, first + panel_tiles)),
            more,
            1 + panel_index,
        )
        applied_rows = multiply(sums_rows, transform, 0, 0)
        if last:
            break
        old_shifted, old_cols = shifted, vec_cols
        (
            inverse, shifted, signs, panel_rows, panel_cols,
            old_high, old_low, new_high, new_low, update_cols, update_next,
        ) = next_panel(
            (
                vec_rows, applied_rows, vec_cols, applied, transform, inner, rest[0], shifted,
                rows_held[panel_index + 1],
            ),
            x4,
            below,
            3,
        )
        more = (old_high, old_low, new_high, new_low)
        panel_cols = (
            panel_cols - multiply(update_next, old_cols, 0, 0) - multiply(old_shifted, update_cols)
        )
    half_inner = 0.5 * multiply(transform, inner, 0, 0)
    update_rows = applied_rows - multiply(vec_rows, half_inner)
    update_cols = applied - multiply(half_inner, vec_cols, 0, 0)
    left = split_outside(jnp.concatenate([vec_rows, update_rows], 1))
    right = split_outside(jnp.concatenate([update_cols, vec_cols], 0))
    return update(rest[0], left, right).reshape(tile_shape)


def solution(mesh):
    return jax.shard_map(
        on_device,
        mesh=mesh,
        in_specs=(P(None, "row", None, None, "col", None),),
        out_specs=P(None, "row", None, None, "col", None),
        check_vma=False,
    )
```

```python
import functools

import jax
import jax.numpy as jnp
from jax import lax
from jax.experimental import pallas as pl
from jax.experimental.pallas import tpu as pltpu
from jax.sharding import PartitionSpec as P

BAND = 256
PANELS = 2
MIB = 1024 * 1024
MESH = pl.DeviceIdType.MESH

HI = lax.Precision.HIGHEST
def mm(a, b, ca, cb):
    return lax.dot_general(a, b, (((ca,), (cb,)), ((), ())), precision=HI, preferred_element_type=jnp.float32)

def base_inverse(block, hook):
    size = block.shape[0]
    wide = (8, 2 * size)
    group = 8
    places = lax.broadcasted_iota(jnp.int32, wide, 0)
    cols = lax.broadcasted_iota(jnp.int32, wide, 1)
    work = []
    for k in range(size // 8):
        unit = jnp.where(places + 8 * k == cols, 1.0, 0.0)[:, :size]
        work.append(jnp.concatenate([block[8 * k : 8 * k + 8], unit], 1))
    for start in range(0, size, group):
        own, offset = divmod(start, 8)
        rows = [jnp.broadcast_to(work[own][offset + i : offset + i + 1], wide) for i in range(group)]
        pivot = [
            [jnp.broadcast_to(rows[i][:, start + j : start + j + 1], wide) for j in range(group)]
            for i in range(group)
        ]
        first = own if offset + group < 8 else own + 1
        columns = [
            [jnp.broadcast_to(work[k][:, start + i : start + i + 1], wide) for i in range(group)]
            for k in range(first, len(work))
        ]
        scaled = []
        for i in range(group):
            inverse = 1.0 / pivot[i][i]
            scaled.append(rows[i] * inverse)
            for j in range(i + 1, group):
                ratio = pivot[i][j] * inverse
                for l in range(j, group):
                    pivot[j][l] = pivot[j][l] - ratio * pivot[i][l]
                rows[j] = rows[j] - ratio * rows[i]
                for column in columns:
                    column[j] = column[j] - ratio * column[i]
        for k, column in zip(range(first, len(work)), columns):
            change = column[0] * scaled[0]
            for i in range(1, group):
                change = change + column[i] * scaled[i]
            if k == own:
                change = jnp.where(places >= offset + group, change, 0.0)
            work[k] = work[k] - change
        for i in range(group):
            work[own] = jnp.where(places == offset + i, rows[i], work[own])
        hook()
    result = []
    for k, value in enumerate(work):
        pivots = jnp.sum(jnp.where(places + 8 * k == cols, value, 0.0), axis=1, keepdims=True)
        result.append(value[:, size:] * (1.0 / jnp.sqrt(pivots)))
    return jnp.concatenate(result, 0)


def factor_inverse(matrix, base, hook):
    size = matrix.shape[0]
    if size <= base:
        return base_inverse(matrix, hook)
    half = size // 2
    first = factor_inverse(matrix[:half, :half], base, hook)
    lower = mm(matrix[half:, :half], first, 1, 1)
    second = factor_inverse(matrix[half:, half:] - mm(lower, lower, 1, 1), base, hook)
    corner = -mm(second, mm(lower, first, 1, 0), 1, 0)
    top = jnp.concatenate([first, jnp.zeros_like(first)], 1)
    return jnp.concatenate([top, jnp.concatenate([corner, second], 1)], 0)

def orthogonal_top(gram, top, top_dim, inverse_ref, shifted_ref, sign_ref, hook):
    size = gram.shape[0]
    inverse = factor_inverse(gram, 64, hook)
    inverse_ref[...] = inverse
    basis = mm(top(), inverse, top_dim, 1)
    rows = lax.broadcasted_iota(jnp.int32, (size, size), 0)
    cols = lax.broadcasted_iota(jnp.int32, (size, size), 1)
    sign_square = jnp.where(rows == cols, jnp.where(basis >= 0, -1.0, 1.0), 0.0)
    shifted_ref[...] = basis - sign_square
    sign_ref[...] = jnp.sum(sign_square, axis=0, keepdims=True)


def block_transform(shifted, signs, hook):
    size = shifted.shape[0]
    outer = factor_inverse(mm(shifted, shifted, 0, 0), 64, hook)
    rows = lax.broadcasted_iota(jnp.int32, (size, size), 0)
    cols = lax.broadcasted_iota(jnp.int32, (size, size), 1)
    sign_column = jnp.sum(jnp.where(rows == cols, signs, 0.0), axis=1, keepdims=True)
    return -mm(outer, mm(outer, shifted * sign_column, 1, 1), 0, 0)


def mm3(a, b, ca=1, cb=0):
    def part(x, y):
        return lax.dot_general(
            x, y, (((ca,), (cb,)), ((), ())), preferred_element_type=jnp.float32
        )

    return part(a[0], b[0]) + (part(a[0], b[1]) + part(a[1], b[0]))


def multiply(first, second, first_dim=1, second_dim=0, precision=HI):
    return lax.dot_general(
        first,
        second,
        (((first_dim,), (second_dim,)), ((), ())),
        precision=precision,
        preferred_element_type=jnp.float32,
    )


def remote(source, target, send_sem, recv_sem, row, col):
    return pltpu.make_async_remote_copy(
        src_ref=source,
        dst_ref=target,
        send_sem=send_sem,
        recv_sem=recv_sem,
        device_id={"row": row, "col": col},
        device_id_type=MESH,
    )


class Place:
    def __init__(self, rows, cols):
        self.rows, self.cols, self.planes = rows, cols, rows // 2
        row = lax.axis_index("row")
        self.col = lax.axis_index("col")
        self.plane = row // 2
        self.core = row % 2
        self.row = row
        self.other = 2 * self.plane + (1 - self.core)
        self.me = self.core * cols + self.col

    def peers(self):
        found = []
        for core_step in range(2):
            for col_step in range(self.cols):
                if core_step or col_step:
                    core = lax.rem(self.core + core_step, 2)
                    col = lax.rem(self.col + col_step, self.cols)
                    found.append((2 * self.plane + core, col, core * self.cols + col))
        return found

    def greet(self, line=True):
        barrier = pltpu.get_barrier_semaphore()
        count = 0
        for row, col, _ in self.peers():
            pl.semaphore_signal(
                barrier, inc=1, device_id={"row": row, "col": col}, device_id_type=MESH
            )
            count += 1
        for step in range(1, self.planes) if line else ():
            row = lax.rem(self.row + 2 * step, self.rows)
            pl.semaphore_signal(
                barrier, inc=1, device_id={"row": row, "col": self.col}, device_id_type=MESH
            )
            count += 1
        pl.semaphore_wait(barrier, count)


def plane_scatter(place, peers, x_ref, parts, out_ref, send_sem, recv_sem):
    copies = []
    for slot, (row, col, piece) in enumerate(peers):
        copies.append(
            remote(
                x_ref.at[piece], parts.at[slot], send_sem.at[slot], recv_sem.at[slot], row, col
            )
        )
        copies[-1].start()
    total = x_ref[place.me]
    for slot, copy in enumerate(copies):
        copy.wait_recv()
        total = total + parts[slot]
    out_ref[place.me] = total
    for copy in copies:
        copy.wait_send()


def plane_gather(place, mine, send_sem, recv_sem):
    copies = []
    for slot, (row, col, _) in enumerate(place.peers()):
        copies.append(remote(mine, mine, send_sem.at[slot], recv_sem.at[slot], row, col))
        copies[-1].start()
    return copies


class Spread:
    def __init__(self, place, source_ref, tiles, target_ref, send_sem, recv_sem):
        self.place, self.source, self.tiles, self.target = place, source_ref, tiles, target_ref
        self.send_sem, self.recv_sem = send_sem, recv_sem
        self.tile = target_ref.shape[0] // 2

    def refs(self, index, core):
        start = pl.multiple_of(core * self.tile, self.tile)
        local = self.tiles[index] // self.place.cols
        return (
            self.source.at[pl.ds(start, self.tile), pl.ds(local * self.tile, self.tile)],
            self.target.at[pl.ds(start, self.tile), pl.ds(index * self.tile, self.tile)],
        )

    def holder(self, index):
        return self.place.col == self.tiles[index] % self.place.cols

    def copies(self, index):
        source, target = self.refs(index, self.place.core)
        return [
            remote(
                source,
                target,
                self.send_sem.at[index, slot],
                self.recv_sem.at[index, self.place.core],
                row,
                col,
            )
            for slot, (row, col, _) in enumerate(self.place.peers())
        ]

    def send(self):
        for index in range(len(self.tiles)):
            @pl.when(self.holder(index))
            def _():
                for copy in self.copies(index):
                    copy.start()
                source, target = self.refs(index, self.place.core)
                target[...] = source[...]

    def wait(self):
        for index in range(len(self.tiles)):
            for core in range(2):
                source, target = self.refs(index, core)

                @pl.when(jnp.logical_not(self.holder(index) & (self.place.core == core)))
                def _():
                    remote(
                        source,
                        target,
                        self.send_sem.at[index, 0],
                        self.recv_sem.at[index, core],
                        self.place.other,
                        self.place.col,
                    ).wait_recv()

    def finish(self):
        for index in range(len(self.tiles)):
            @pl.when(self.holder(index))
            def _():
                for copy in self.copies(index):
                    copy.wait_send()


class Chain:
    def __init__(self, place, source, x_ref, panel_ref, sems):
        self.place, self.source, self.x_ref, self.ref = place, source, x_ref, panel_ref
        self.load, self.sends, self.recv, self.share_send, self.share_recv = sems
        self.tile = x_ref.shape[-1]
        self.tiles = x_ref.shape[1]
        self.chunks = self.recv.shape[0]
        self.width = panel_ref.shape[1] // self.chunks
        self.at_source = place.plane == source

    def loads(self):
        start = pl.multiple_of(self.place.core * self.tile, self.tile)
        for tile in range(self.tiles):
            yield pltpu.make_async_copy(
                self.x_ref.at[pl.ds(0, self.tile), tile, 0, :],
                self.ref.at[pl.ds(start, self.tile), pl.ds(tile * self.tile, self.tile)],
                self.load.at[tile],
            )

    def part(self, chunk):
        start = pl.multiple_of(self.place.core * self.tile, self.tile)
        return self.ref.at[pl.ds(start, self.tile), pl.ds(chunk * self.width, self.width)]

    def hop(self, chunk, step, sem):
        part = self.part(chunk)
        row = lax.rem(self.place.row + 2 * step + self.place.rows, self.place.rows)
        return remote(part, part, self.sends.at[sem, chunk], self.recv.at[chunk], row, self.place.col)

    def shared(self, chunk):
        part = self.part(chunk)
        return remote(
            part,
            part,
            self.share_send.at[chunk],
            self.share_recv.at[chunk],
            self.place.other,
            self.place.col,
        )

    def start(self):
        @pl.when(self.at_source)
        def _():
            for copy in self.loads():
                copy.start()

    def share(self):
        @pl.when(self.at_source)
        def _():
            for copy in self.loads():
                copy.wait()
            for chunk in range(self.chunks):
                self.shared(chunk).start()

    def spread(self, first, last):
        @pl.when(self.at_source)
        def _():
            for chunk in range(first, min(last, self.chunks)):
                if self.source < self.place.planes - 1:
                    self.hop(chunk, 1, 0).start()
                if self.source > 0:
                    self.hop(chunk, -1, 1).start()

    def step(self, chunk):
        place = self.place
        for step, sem, away, more in (
            (1, 0, place.plane > self.source, place.plane < place.planes - 1),
            (-1, 1, place.plane < self.source, place.plane > 0),
        ):
            if step < 0 and self.source == 0 or step > 0 and self.source == place.planes - 1:
                continue

            @pl.when(away)
            def _():
                self.hop(chunk, step, sem).wait_recv()

                @pl.when(more)
                def _():
                    self.hop(chunk, step, sem).start()

                self.shared(chunk).start()

    def join(self):
        for chunk in range(self.chunks):
            self.shared(chunk).wait_recv()

    def finish(self, joined=False):
        place = self.place
        if joined:
            @pl.when(jnp.logical_not(self.at_source))
            def _():
                self.join()
        else:
            self.join()
        for chunk in range(self.chunks):
            self.shared(chunk).wait_send()
        for step, sem, sent in (
            (1, 0, (place.plane >= self.source) & (place.plane < place.planes - 1)),
            (-1, 1, (place.plane <= self.source) & (place.plane > 0)),
        ):

            @pl.when(sent)
            def _():
                for chunk in range(self.chunks):
                    self.hop(chunk, step, sem).wait_send()

    @staticmethod
    def semaphores(tiles, chunks):
        dma = pltpu.SemaphoreType.DMA
        return [dma((tiles,)), dma((2, chunks)), dma((chunks,)), dma((chunks,)), dma((chunks,))]


CHUNK = 256


def later_steps(chain, first, every):
    count = [0]

    def hook():
        count[0] += 1
        chunk = first + count[0] // every - 1
        if count[0] % every == 0 and first <= chunk < chain.chunks:
            chain.step(chunk)

    return hook


EARLY = 3


def first_kernel(rows, cols, x_ref, inverse_ref, shifted_ref, sign_ref, rows_ref, cols_ref, *refs):
    stack, parts, gram_ref, top_ref = refs[:4]
    send_one, recv_one, line_send, line_recv, send_two, recv_two = refs[4:10]
    load, send_row, recv_row, top_send, top_recv = refs[10:15]
    place = Place(rows, cols)
    tile, tiles = x_ref.shape[-1], x_ref.shape[1]
    panel_tiles = BAND // tile
    held = PANELS * panel_tiles
    chain = Chain(place, 0, x_ref, cols_ref, refs[15:])
    spread = Spread(
        place, cols_ref, tuple(range(panel_tiles, 2 * panel_tiles)), top_ref, top_send, top_recv
    )
    first = place.plane == 0

    def spot(col):
        start = pl.multiple_of(lax.rem(col, panel_tiles) * tile, tile)
        return rows_ref.at[col // panel_tiles, :, pl.ds(start, tile)]

    has = place.col < held
    own = spot(lax.rem(place.col, held))
    fill = pltpu.make_async_copy(x_ref.at[:, 0, 0, :], own, load.at[0])

    @pl.when(has)
    def _():
        fill.start()

    chain.start()
    place.greet()
    copies = [
        remote(
            own,
            own,
            send_row.at[step - 1],
            recv_row.at[lax.rem(place.col, held)],
            place.row,
            lax.rem(place.col + step, cols),
        )
        for step in range(1, cols)
    ]
    line = [
        remote(
            gram_ref.at[place.me],
            gram_ref.at[place.me],
            line_send.at[step - 1],
            line_recv.at[0],
            lax.rem(place.row + 2 * step, rows),
            place.col,
        )
        for step in range(1, place.planes)
    ]
    chain.share()
    chain.spread(0, EARLY)

    @pl.when(first)
    def _():
        chain.join()
        width = tile * tiles // 2
        offset = place.core * width
        lanes = lax.broadcasted_iota(jnp.int32, (cols_ref.shape[0], width), 1) + offset
        limit = jnp.where(place.col < panel_tiles, tile, 0)
        value = cols_ref[:, pl.ds(pl.multiple_of(offset, tile), width)]
        value = jnp.where(lanes >= limit, value, 0.0)
        gram = mm(value, value, 1, 1)
        size = stack.shape[1]
        for piece in range(stack.shape[0]):
            stack[piece] = gram[piece * size : (piece + 1) * size]
        plane_scatter(place, place.peers(), stack, parts, gram_ref, send_one, recv_one)
        for copy in line:
            copy.start()

    chain.spread(EARLY, chain.chunks)

    @pl.when(place.plane > 0)
    def _():
        line[0].wait_recv()

    gathers = plane_gather(place, gram_ref.at[place.me], send_two, recv_two)
    chain.step(0)
    spread.send()

    @pl.when(has)
    def _():
        fill.wait()
        for copy in copies:
            copy.start()

    for copy in gathers:
        copy.wait()

    def top():
        spread.wait()
        return top_ref[...]

    size = inverse_ref.shape[0]
    orthogonal_top(
        gram_ref[...].reshape(size, size), top, 0, inverse_ref, shifted_ref, sign_ref,
        later_steps(chain, 1, 3),
    )

    @pl.when(first)
    def _():
        for copy in line:
            copy.wait_send()

    spread.finish()

    @pl.when(has)
    def _():
        for copy in copies:
            copy.wait_send()

    for col in range(held):
        @pl.when(place.col != col)
        def _():
            remote(spot(col), spot(col), send_row.at[0], recv_row.at[col], place.row, place.col).wait_recv()

    chain.finish(True)


def first_panel(x4, collective_id):
    rows, cols = lax.axis_size("row"), lax.axis_size("col")
    row_count, tiles, _, tile = x4.shape
    width = tiles * tile
    count = 2 * cols
    pieces = (count, BAND // count, BAND)
    vmem = pl.BlockSpec(memory_space=pltpu.VMEM)
    dma = pltpu.SemaphoreType.DMA
    panel_tiles = BAND // tile
    square = jax.ShapeDtypeStruct((BAND, BAND), x4.dtype)
    return pl.pallas_call(
        functools.partial(first_kernel, rows, cols),
        out_shape=(
            square,
            square,
            jax.ShapeDtypeStruct((1, BAND), x4.dtype),
            jax.ShapeDtypeStruct((PANELS, row_count, BAND), x4.dtype),
            jax.ShapeDtypeStruct((BAND, width), x4.dtype),
        ),
        in_specs=[pl.BlockSpec(memory_space=pltpu.HBM)],
        out_specs=(vmem,) * 5,
        scratch_shapes=[
            pltpu.VMEM(pieces, x4.dtype),
            pltpu.VMEM((count - 1,) + pieces[1:], x4.dtype),
            pltpu.VMEM(pieces, x4.dtype),
            pltpu.VMEM((BAND, BAND), x4.dtype),
            dma((count - 1,)),
            dma((count - 1,)),
            dma((rows // 2 - 1,)),
            dma((1,)),
            dma((count - 1,)),
            dma((count - 1,)),
            dma((1,)),
            dma((cols - 1,)),
            dma((PANELS * panel_tiles,)),
            dma((panel_tiles, count - 1)),
            dma((panel_tiles, 2)),
        ]
        + Chain.semaphores(tiles, width // CHUNK),
        compiler_params=pltpu.CompilerParams(
            collective_id=collective_id, has_side_effects=True, vmem_limit_bytes=56 * MIB
        ),
    )(x4)


def next_kernel(rows, cols, below, *refs):
    refs = list(refs)
    take = lambda count: [refs.pop(0) for _ in range(count)]
    (
        vec_rows, applied_rows, vec_cols, applied, transform_ref, inner_ref, applied_next,
        old_ref, later_ref, x_ref,
    ) = take(10)
    inverse_ref, shifted_ref, sign_ref, panel_ref, cols_ref = take(5)
    old_high, old_low, new_high, new_low, update_ref, ahead_ref = take(6)
    gram_in, gram_sum = take(2)
    near, near_sum, parts, gram_ref, top_ref = refs[:5]
    near_send, near_recv, line_send, line_recv, send_two, recv_two = refs[5:11]
    top_line_send, top_line_recv, top_send, top_recv = refs[11:15]
    place = Place(rows, cols)
    tile = x_ref.shape[-1]
    panel_tiles = BAND // tile
    number = 2 * panel_tiles
    chain = Chain(place, 1, x_ref, cols_ref, refs[15:])
    chain.start()
    place.greet()
    chain.share()
    chain.spread(0, EARLY)
    half_full = 0.5 * mm(transform_ref[...], inner_ref[...], 1, 0)
    half = split(half_full)
    old = old_ref[...]
    ahead = applied_next[...] - mm(half_full, old, 0, 1)
    ahead_ref[...] = ahead
    vec = vec_rows[...]
    vec_parts = split(vec)
    change = applied_rows[...] - mm3(vec_parts, half)
    panel = later_ref[...] - mm(vec, ahead, 1, 0) - mm(change, old, 1, 1)
    lines = lax.broadcasted_iota(jnp.int32, panel.shape, 0)
    above = (below + BAND) // tile
    limit = (above // rows + jnp.where(place.row < above % rows, 1, 0)) * tile
    panel = jnp.where(lines >= limit, panel, 0.0)
    panel_ref[...] = panel
    gram_sum[...] = mm(panel, panel, 0, 0)
    change_parts = split(change)
    for start, value in ((0, vec_parts), (BAND, change_parts)):
        old_high[:, start : start + BAND] = value[0]
        old_low[:, start : start + BAND] = value[1]
    size = BAND
    height = gram_in.shape[2]
    for col in range(cols):
        for core in range(2):
            start = (2 * col + core) * height
            gram_in[col, core] = gram_sum[start : start + height, :]
    chain.step(0)
    swap = remote(
        gram_in.at[place.col, 1 - place.core], near.at[0], near_send.at[0], near_recv.at[0],
        place.other, place.col,
    )
    swap.start()

    top_plane = number % rows // 2
    start = pl.multiple_of(place.core * tile, tile)
    local = number // rows * tile
    block = panel_ref.at[pl.ds(local, tile), :]
    target = top_ref.at[pl.ds(start, tile), :]
    at_top = place.plane == top_plane

    def top_line(step):
        return remote(
            block, target, top_line_send.at[step - 1], top_line_recv.at[0],
            lax.rem(place.row + 2 * step, rows), place.col,
        )

    top_near = remote(target, target, top_send.at[0], top_recv.at[0], place.other, place.col)
    top_first = remote(block, target, top_send.at[0], top_recv.at[0], place.other, place.col)

    swap.wait_recv()
    near_sum[0] = gram_in[place.col, place.core] + near[0]
    line = [
        remote(
            near_sum.at[0], parts.at[step - 1], line_send.at[step - 1], line_recv.at[step - 1],
            lax.rem(place.row + 2 * step, rows), place.col,
        )
        for step in range(1, place.planes)
    ]
    for copy in line:
        copy.start()

    @pl.when(at_top)
    def _():
        for step in range(1, place.planes):
            top_line(step).start()
        top_first.start()
        target[...] = block[...]

    chain.spread(EARLY, chain.chunks)
    chain.step(1)
    group = 5 if x_ref.shape[1] % 10 == 0 else 1
    wide = x_ref.shape[1] // group * tile
    half_t = split(half_full.T)

    def own_cols(index, carry):
        here = pl.ds(pl.multiple_of(index * wide, wide), wide)
        vec = split(vec_cols[:, here])
        change = applied[:, here] - mm3(half_t, vec)
        update_ref[:, here] = change
        for start, value in ((0, split(change)), (size, vec)):
            new_high[start : start + size, here] = value[0]
            new_low[start : start + size, here] = value[1]
        return carry

    lax.fori_loop(0, group, own_cols, 0)
    chain.step(2)
    total = near_sum[0]
    for slot, copy in enumerate(line):
        copy.wait_recv()
        total = total + parts[slot]
    piece = 2 * place.col + place.core
    gram_ref[piece] = total
    gathers = plane_gather(place, gram_ref.at[piece], send_two, recv_two)

    @pl.when(jnp.logical_not(at_top))
    def _():
        top_line(1).wait_recv()
        top_near.start()

    for copy in gathers:
        copy.wait()

    def top():
        top_near.wait_recv()
        return top_ref[...]

    orthogonal_top(
        gram_ref[...].reshape(size, size), top, 1, inverse_ref, shifted_ref, sign_ref,
        later_steps(chain, 3, 2),
    )
    swap.wait_send()
    for copy in line:
        copy.wait_send()
    top_near.wait_send()

    @pl.when(at_top)
    def _():
        for step in range(1, place.planes):
            top_line(step).wait_send()

    chain.finish()


def next_panel(operands, x4, below, collective_id):
    rows, cols = lax.axis_size("row"), lax.axis_size("col")
    row_count, tiles, _, tile = x4.shape
    width = tiles * tile
    count = 2 * cols
    piece = (BAND // count, BAND)
    planes = rows // 2
    vmem = pl.BlockSpec(memory_space=pltpu.VMEM)
    dma = pltpu.SemaphoreType.DMA
    f32, bf16 = jnp.float32, jnp.bfloat16
    shape = jax.ShapeDtypeStruct
    square = shape((BAND, BAND), f32)
    return pl.pallas_call(
        functools.partial(next_kernel, rows, cols, below),
        out_shape=(
            square,
            square,
            shape((1, BAND), f32),
            shape((row_count, BAND), f32),
            shape((BAND, width), f32),
            shape((row_count, 2 * BAND), bf16),
            shape((row_count, 2 * BAND), bf16),
            shape((2 * BAND, width), bf16),
            shape((2 * BAND, width), bf16),
            shape((BAND, width), f32),
            square,
        ),
        in_specs=[vmem] * len(operands) + [pl.BlockSpec(memory_space=pltpu.HBM)],
        out_specs=(vmem,) * 11,
        scratch_shapes=[
            pltpu.VMEM((cols, 2) + piece, f32),
            pltpu.VMEM((BAND, BAND), f32),
            pltpu.VMEM((1,) + piece, f32),
            pltpu.VMEM((1,) + piece, f32),
            pltpu.VMEM((planes - 1,) + piece, f32),
            pltpu.VMEM((count,) + piece, f32),
            pltpu.VMEM((BAND, BAND), f32),
            dma((1,)),
            dma((1,)),
            dma((planes - 1,)),
            dma((planes - 1,)),
            dma((count - 1,)),
            dma((count - 1,)),
            dma((planes - 1,)),
            dma((1,)),
            dma((1,)),
            dma((1,)),
        ]
        + Chain.semaphores(tiles, width // CHUNK),
        compiler_params=pltpu.CompilerParams(
            collective_id=collective_id, has_side_effects=True, vmem_limit_bytes=44 * MIB
        ),
    )(*operands, x4)


def split(value):
    high = value.astype(jnp.bfloat16)
    return high, (value - high.astype(jnp.float32)).astype(jnp.bfloat16)


def split_outside(value):
    high = lax.reduce_precision(value, 8, 7)
    return high.astype(jnp.bfloat16), (value - high).astype(jnp.bfloat16)


def dot(a, b):
    return jnp.dot(a, b, preferred_element_type=jnp.float32)


def apply_kernel(rows, cols, tiles, fixed, *refs):
    place = Place(rows, cols)
    refs = list(refs)
    take = lambda count: [refs.pop(0) for _ in range(count)]
    x_ref, left_ref, shifted_ref, sign_ref, vec_ref = take(5)
    old_high, old_low, new_high, new_low = take(4) if fixed else [None] * 4
    row_ref, transform_ref, applied_ref, inner_ref = take(4)
    next_ref = take(1)[0] if tiles else None
    kept_ref = take(1)[0] if fixed else None
    block, part, near, pair, left_in, right_in, left_out, right_out, out_ref = take(9)
    total_ref, stack, parts = take(3)
    (
        load, near_send, near_recv, left_send, left_recv, right_send, right_recv,
        both_send, both_recv, row_send, row_recv, send_one, recv_one, send_two, recv_two,
    ) = take(15)
    next_sems = take(2) if tiles else None
    store = take(1)[0] if fixed else None
    plane, core, planes = place.plane, place.core, place.planes
    tile = x_ref.shape[-1]
    chunks = block.shape[0]
    pieces = pair.shape[0] // chunks
    depth = pair.shape[1]
    subs = chunks * pieces
    size = left_ref.shape[0] // 2

    def load_of(chunk, index):
        return pltpu.make_async_copy(
            x_ref.at[:, 2 * chunk + index, 0, :],
            block.at[chunk, :, pl.ds(index * tile, tile)],
            load.at[chunk, index],
        )

    def store_of(chunk, index):
        return pltpu.make_async_copy(
            block.at[chunk, :, pl.ds(index * tile, tile)],
            kept_ref.at[:, 2 * chunk + index, 0, :],
            store.at[chunk, index],
        )

    for chunk in range(chunks):
        for index in range(2):
            load_of(chunk, index).start()
    place.greet()

    def near_of(chunk):
        return remote(
            part.at[chunk, 1 - core],
            near.at[chunk],
            near_send.at[chunk],
            near_recv.at[chunk],
            place.other,
            place.col,
        )

    def rightward(source, index):
        return remote(
            source.at[index], left_in.at[index], right_send.at[index], left_recv.at[index],
            lax.rem(place.row + 2, rows), place.col,
        )

    def leftward(source, index):
        return remote(
            source.at[index], right_in.at[index], left_send.at[index], right_recv.at[index],
            lax.rem(place.row + rows - 2, rows), place.col,
        )

    def joined(chunk):
        near_of(chunk).wait_recv()
        for piece in range(pieces):
            pair[chunk * pieces + piece] = part[chunk, core, piece] + near[chunk, piece]

        @pl.when(plane == 0)
        def _():
            for piece in range(pieces):
                rightward(pair, chunk * pieces + piece).start()

        @pl.when(plane == planes - 1)
        def _():
            for piece in range(pieces):
                leftward(pair, chunk * pieces + piece).start()

    def product(chunk, carry):
        for index in range(2):
            load_of(chunk, index).wait()
        if fixed:
            here = pl.ds(pl.multiple_of(chunk * 2 * tile, 2 * tile), 2 * tile)
            change = dot(old_high[...], new_high[:, here]) + (
                dot(old_low[...], new_high[:, here]) + dot(old_high[...], new_low[:, here])
            )
            block[chunk] = block[chunk] - change
            for index in range(2):
                store_of(chunk, index).start()
        high, low = split(block[chunk])
        value = dot(left_ref[...], high)
        value = value[:size] + (value[size:] + dot(left_ref[:size], low))
        for index in range(2):
            for piece in range(pieces):
                part[chunk, index, piece] = value[
                    piece * depth : (piece + 1) * depth, index * tile : (index + 1) * tile
                ]
        near_of(chunk).start()

        @pl.when(chunk > 0)
        def _():
            joined(chunk - 1)

        for piece in range(pieces):
            chain((chunk - BEHIND) * pieces + piece, 0)
        return carry

    left_lag = HOP * jnp.maximum(plane - 1, 0)
    right_lag = HOP * jnp.maximum(planes - 2 - plane, 0)
    last_lag = jnp.maximum(left_lag, right_lag)
    held = cols * core + place.col
    source = held // 2 == plane
    target_row = 2 * plane + lax.rem(place.col, 2)
    to_self = target_row == place.row

    def depths(index):
        return pl.ds(pl.multiple_of(lax.rem(index, pieces) * depth, depth), depth)

    def lanes(index):
        return pl.ds(pl.multiple_of((2 * (index // pieces) + core) * tile, tile), tile)

    def row_lanes(index):
        return pl.ds(pl.multiple_of(index // pieces * tile, tile), tile)

    def both_of(index):
        spot = out_ref.at[depths(index), lanes(index)]
        return remote(spot, spot, both_send.at[index], both_recv.at[index], place.other, place.col)

    def row_of(index, step):
        return remote(
            out_ref.at[depths(index), lanes(index)],
            row_ref.at[depths(index), row_lanes(index)],
            row_send.at[index, step],
            row_recv.at[index],
            target_row,
            lax.rem(place.col + step, cols),
        )

    def chain(step, carry):
        index = step - left_lag

        @pl.when((plane > 0) & (index >= 0) & (index < subs))
        def _():
            rightward(pair, index).wait_recv()

            @pl.when(plane < planes - 1)
            def _():
                right_out[index] = left_in[index] + pair[index]
                rightward(right_out, index).start()

        other = step - right_lag

        @pl.when((plane < planes - 1) & (other >= 0) & (other < subs))
        def _():
            leftward(pair, other).wait_recv()

            @pl.when(plane > 0)
            def _():
                left_out[other] = right_in[other] + pair[other]
                leftward(left_out, other).start()

        done = step - last_lag

        @pl.when((done >= 0) & (done < subs))
        def _():
            @pl.when(plane == 0)
            def _():
                out_ref[depths(done), lanes(done)] = pair[done] + right_in[done]

            @pl.when(plane == planes - 1)
            def _():
                out_ref[depths(done), lanes(done)] = left_in[done] + pair[done]

            @pl.when((plane > 0) & (plane < planes - 1))
            def _():
                out_ref[depths(done), lanes(done)] = right_out[done] + right_in[done]

            both_of(done).start()

            @pl.when(source)
            def _():
                for step in range(1, cols):
                    row_of(done, step).start()

                @pl.when(to_self)
                def _():
                    row_ref[depths(done), row_lanes(done)] = out_ref[depths(done), lanes(done)]

                @pl.when(jnp.logical_not(to_self))
                def _():
                    row_of(done, 0).start()

        return carry

    lax.fori_loop(0, chunks, product, 0)
    joined(chunks - 1)
    steps = subs + HOP * (planes - 2)
    count = [0, max(chunks - BEHIND, 0) * pieces]

    def hook():
        count[0] += 1
        if count[0] % 2 == 0 and count[1] < steps:
            chain(count[1], 0)
            count[1] += 1

    transform_ref[...] = block_transform(shifted_ref[...], sign_ref[...], hook)
    if count[1] < steps:
        lax.fori_loop(count[1], steps, chain, 0)
    total_ref[...] = jnp.zeros_like(total_ref)
    transform = split(transform_ref[...])

    def finished(number, carry):
        for index in range(2 * pieces):
            both_of(2 * pieces * number + index).wait_recv()
        here = pl.ds(pl.multiple_of(number * 4 * tile, 4 * tile), 4 * tile)
        applied = mm3(transform, split(out_ref[:, here]))
        applied_ref[:, here] = applied
        total_ref[...] += mm3(split(vec_ref[:, here]), split(applied), 1, 1)
        return carry

    def finished_one(number, carry):
        for index in range(pieces):
            both_of(pieces * number + index).wait_recv()
        here = pl.ds(pl.multiple_of(number * 2 * tile, 2 * tile), 2 * tile)
        applied = mm3(transform, split(out_ref[:, here]))
        applied_ref[:, here] = applied
        total_ref[...] += mm3(split(vec_ref[:, here]), split(applied), 1, 1)
        return carry

    if chunks % 2 == 0:
        lax.fori_loop(0, chunks // 2, finished, 0)
    else:
        lax.fori_loop(0, chunks, finished_one, 0)
    height = stack.shape[1]
    for piece in range(stack.shape[0]):
        stack[piece] = total_ref[piece * height : (piece + 1) * height, :]
    if tiles:
        spread = Spread(place, applied_ref, tiles, next_ref, *next_sems)
        spread.send()
    plane_scatter(place, place.peers()[: cols - 1], stack, parts, inner_ref, send_one, recv_one)
    gathers = plane_gather(place, inner_ref.at[place.me], send_two, recv_two)
    gets = jnp.logical_not(source & to_self)

    def drain(index, carry):
        both_of(index).wait_send()

        @pl.when(plane < planes - 1)
        def _():
            rightward(pair, index).wait_send()

        @pl.when(plane > 0)
        def _():
            leftward(pair, index).wait_send()

        @pl.when(source)
        def _():
            for step in range(1, cols):
                row_of(index, step).wait_send()

            @pl.when(jnp.logical_not(to_self))
            def _():
                row_of(index, 0).wait_send()

        @pl.when(gets)
        def _():
            row_of(index, 0).wait_recv()

        return carry

    def drain_chunk(chunk, carry):
        if fixed:
            for index in range(2):
                store_of(chunk, index).wait()
        near_of(chunk).wait_send()
        return carry

    lax.fori_loop(0, subs, drain, 0)
    lax.fori_loop(0, chunks, drain_chunk, 0)
    for copy in gathers:
        copy.wait()
    if tiles:
        spread.wait()
        spread.finish()


PIECES = 2
HOP = 3
BEHIND = 3


def apply(x4, left, shifted, signs, vec_cols, tiles, more, collective_id):
    rows, cols = lax.axis_size("row"), lax.axis_size("col")
    row_count, held_tiles, _, tile = x4.shape
    width = held_tiles * tile
    chunks = held_tiles // 2
    count = 2 * cols
    vmem = pl.BlockSpec(memory_space=pltpu.VMEM)
    hbm = pl.BlockSpec(memory_space=pltpu.HBM)
    dma = pltpu.SemaphoreType.DMA
    f32 = jnp.float32
    piece = (BAND // PIECES, tile)
    subs = PIECES * chunks
    sums = (count, BAND // count, BAND)
    kept = bool(more)
    square = jax.ShapeDtypeStruct((BAND, BAND), f32)
    wide = jax.ShapeDtypeStruct((BAND, width), f32)
    shapes = (
        jax.ShapeDtypeStruct((BAND, row_count), f32),
        square,
        wide,
        jax.ShapeDtypeStruct(sums, f32),
    )
    shapes += (square,) if tiles else ()
    out = pl.pallas_call(
        functools.partial(apply_kernel, rows, cols, tiles, kept),
        out_shape=shapes + ((jax.ShapeDtypeStruct(x4.shape, x4.dtype),) if kept else ()),
        in_specs=[hbm] + [vmem] * (4 + len(more)),
        out_specs=(vmem,) * len(shapes) + ((hbm,) if kept else ()),
        scratch_shapes=[
            pltpu.VMEM((chunks, row_count, 2 * tile), f32),
            pltpu.VMEM((chunks, 2, PIECES) + piece, f32),
            pltpu.VMEM((chunks, PIECES) + piece, f32),
        ]
        + [pltpu.VMEM((subs,) + piece, f32)] * 5
        + [
            pltpu.VMEM((BAND, width), f32),
            pltpu.VMEM((BAND, BAND), f32),
            pltpu.VMEM(sums, f32),
            pltpu.VMEM((cols - 1,) + sums[1:], f32),
        ]
        + [dma((chunks, 2)), dma((chunks,)), dma((chunks,))]
        + [dma((subs,))] * 6
        + [dma((subs, cols)), dma((subs,))]
        + [dma((cols - 1,))] * 2
        + [dma((count - 1,))] * 2
        + ([dma((len(tiles), count - 1)), dma((len(tiles), 2))] if tiles else [])
        + ([dma((chunks, 2))] if kept else []),
        compiler_params=pltpu.CompilerParams(
            collective_id=collective_id, has_side_effects=True, vmem_limit_bytes=(60 if kept else 48) * MIB
        ),
    )(x4, left, shifted, signs, vec_cols, *more)
    out = list(out)
    out[3] = out[3].reshape(BAND, BAND)
    return out


def update_kernel(x_ref, left_high, left_low, right_high, right_low, out_ref, block, result, load, store):
    tile = x_ref.shape[-1]
    chunks = x_ref.shape[1] // 2

    def load_of(chunk, index):
        return pltpu.make_async_copy(
            x_ref.at[:, 2 * chunk + index, 0, :],
            block.at[lax.rem(chunk, 2), :, pl.ds(index * tile, tile)],
            load.at[lax.rem(chunk, 2), index],
        )

    def store_of(chunk, index):
        return pltpu.make_async_copy(
            result.at[lax.rem(chunk, 2), :, pl.ds(index * tile, tile)],
            out_ref.at[:, 2 * chunk + index, 0, :],
            store.at[lax.rem(chunk, 2), index],
        )

    for chunk in range(2):
        for index in range(2):
            load_of(chunk, index).start()

    def body(chunk, carry):
        slot = lax.rem(chunk, 2)
        for index in range(2):
            load_of(chunk, index).wait()

        @pl.when(chunk >= 2)
        def _():
            for index in range(2):
                store_of(chunk - 2, index).wait()

        here = pl.ds(pl.multiple_of(chunk * 2 * tile, 2 * tile), 2 * tile)
        value = dot(left_high[...], right_high[:, here]) + (
            dot(left_low[...], right_high[:, here]) + dot(left_high[...], right_low[:, here])
        )
        result[slot] = block[slot] - value
        for index in range(2):
            store_of(chunk, index).start()

        @pl.when(chunk + 2 < chunks)
        def _():
            for index in range(2):
                load_of(chunk + 2, index).start()

        return carry

    lax.fori_loop(0, chunks, body, 0)
    for chunk in range(chunks - 2, chunks):
        for index in range(2):
            store_of(chunk, index).wait()


def update(x4, left, right):
    row_count, tiles, _, tile = x4.shape
    vmem = pl.BlockSpec(memory_space=pltpu.VMEM)
    hbm = pl.BlockSpec(memory_space=pltpu.HBM)
    dma = pltpu.SemaphoreType.DMA
    return pl.pallas_call(
        update_kernel,
        out_shape=jax.ShapeDtypeStruct(x4.shape, x4.dtype),
        in_specs=[hbm] + [vmem] * 4,
        out_specs=hbm,
        scratch_shapes=[pltpu.VMEM((2, row_count, 2 * tile), jnp.float32)] * 2
        + [dma((2, 2)), dma((2, 2))],
        compiler_params=pltpu.CompilerParams(vmem_limit_bytes=48 * MIB),
    )(x4, *left, *right)


def on_device(matrix_tiles):
    tile_shape = matrix_tiles.shape
    block_rows, _, tile_size, block_cols = tile_shape[:4]
    row_count = block_rows * tile_size
    col_count = block_cols * tile_size
    row_devices = lax.axis_size("row")
    col_devices = lax.axis_size("col")
    row_index = lax.axis_index("row")
    panel_tiles = BAND // tile_size
    assert row_devices == 2 * col_devices and PANELS * panel_tiles <= col_devices
    x4 = matrix_tiles.reshape(row_count, block_cols, 1, tile_size)

    def positions(count, devices, index):
        place = jnp.arange(count, dtype=jnp.int32)
        return (place // tile_size * devices + index) * tile_size + place % tile_size

    global_rows = positions(row_count, row_devices, row_index)
    global_cols = positions(col_count, lax.axis_size("col"), lax.axis_index("col"))
    band = jnp.arange(BAND, dtype=jnp.int32)
    inverse, shifted, signs, rows_held, panel_cols = first_panel(x4, 0)
    panel_rows = rows_held[0]
    kept, more = x4, ()
    for panel_index in range(PANELS):
        below = (panel_index + 1) * BAND
        last = panel_index == PANELS - 1
        panel_rows = jnp.where((global_rows >= below)[:, None], panel_rows, 0.0)
        unit_rows = (global_rows[:, None] - below == band[None, :]).astype(jnp.float32)
        unit_rows_t = (band[:, None] == global_rows[None, :] - below).astype(jnp.float32)
        vec_rows = multiply(panel_rows, inverse, 1, 1) - unit_rows * signs
        vec_rows_t = multiply(inverse, panel_rows, 1, 1) - unit_rows_t * signs.reshape(BAND, 1)
        panel_cols = jnp.where((global_cols >= below)[None, :], panel_cols, 0.0)
        unit_cols = (band[:, None] == global_cols[None, :] - below).astype(jnp.float32)
        vec_cols = multiply(inverse, panel_cols) - unit_cols * signs.reshape(BAND, 1)
        first = below // tile_size
        sums_rows, transform, applied, inner, *rest = apply(
            kept,
            jnp.concatenate(split_outside(vec_rows_t), 0),
            shifted,
            signs,
            vec_cols,
            () if last else tuple(range(first, first + panel_tiles)),
            more,
            1 + panel_index,
        )
        applied_rows = multiply(sums_rows, transform, 0, 1)
        if last:
            break
        old_shifted, old_cols = shifted, vec_cols
        (
            inverse, shifted, signs, panel_rows, panel_cols,
            old_high, old_low, new_high, new_low, update_cols, update_next,
        ) = next_panel(
            (
                vec_rows, applied_rows, vec_cols, applied, transform, inner, rest[0], shifted,
                rows_held[panel_index + 1],
            ),
            x4,
            below,
            3,
        )
        more = (old_high, old_low, new_high, new_low)
        panel_cols = (
            panel_cols - multiply(update_next, old_cols, 0, 0) - multiply(old_shifted, update_cols)
        )
    half_inner = 0.5 * multiply(transform, inner)
    update_rows = applied_rows - multiply(vec_rows, half_inner)
    update_cols = applied - multiply(half_inner, vec_cols, 0, 0)
    left = split_outside(jnp.concatenate([vec_rows, update_rows], 1))
    right = split_outside(jnp.concatenate([update_cols, vec_cols], 0))
    return update(rest[0], left, right).reshape(tile_shape)


def solution(mesh):
    return jax.shard_map(
        on_device,
        mesh=mesh,
        in_specs=(P(None, "row", None, None, "col", None),),
        out_specs=P(None, "row", None, None, "col", None),
        check_vma=False,
    )
```

```python
import functools

import jax
import jax.numpy as jnp
from jax import lax
from jax.experimental import pallas as pl
from jax.experimental.pallas import tpu as pltpu
from jax.sharding import PartitionSpec as P

BAND = 256
PANELS = 2
MIB = 1024 * 1024
MESH = pl.DeviceIdType.MESH

HI = lax.Precision.HIGHEST
def mm(a, b, ca, cb):
    return lax.dot_general(a, b, (((ca,), (cb,)), ((), ())), precision=HI, preferred_element_type=jnp.float32)

def base_inverse(block, hook):
    size = block.shape[0]
    wide = (8, 2 * size)
    group = 8
    places = lax.broadcasted_iota(jnp.int32, wide, 0)
    cols = lax.broadcasted_iota(jnp.int32, wide, 1)
    work = []
    for k in range(size // 8):
        unit = jnp.where(places + 8 * k == cols, 1.0, 0.0)[:, :size]
        work.append(jnp.concatenate([block[8 * k : 8 * k + 8], unit], 1))
    for start in range(0, size, group):
        own, offset = divmod(start, 8)
        rows = [jnp.broadcast_to(work[own][offset + i : offset + i + 1], wide) for i in range(group)]
        pivot = [
            [jnp.broadcast_to(rows[i][:, start + j : start + j + 1], wide) for j in range(group)]
            for i in range(group)
        ]
        first = own if offset + group < 8 else own + 1
        columns = [
            [jnp.broadcast_to(work[k][:, start + i : start + i + 1], wide) for i in range(group)]
            for k in range(first, len(work))
        ]
        scaled = []
        for i in range(group):
            inverse = 1.0 / pivot[i][i]
            scaled.append(rows[i] * inverse)
            for j in range(i + 1, group):
                ratio = pivot[i][j] * inverse
                for l in range(j, group):
                    pivot[j][l] = pivot[j][l] - ratio * pivot[i][l]
                rows[j] = rows[j] - ratio * rows[i]
                for column in columns:
                    column[j] = column[j] - ratio * column[i]
        for k, column in zip(range(first, len(work)), columns):
            change = column[0] * scaled[0]
            for i in range(1, group):
                change = change + column[i] * scaled[i]
            if k == own:
                change = jnp.where(places >= offset + group, change, 0.0)
            work[k] = work[k] - change
        for i in range(group):
            work[own] = jnp.where(places == offset + i, rows[i], work[own])
        hook()
    result = []
    for k, value in enumerate(work):
        pivots = jnp.sum(jnp.where(places + 8 * k == cols, value, 0.0), axis=1, keepdims=True)
        result.append(value[:, size:] * (1.0 / jnp.sqrt(pivots)))
    return jnp.concatenate(result, 0)


def factor_inverse(matrix, base, hook):
    size = matrix.shape[0]
    if size <= base:
        return base_inverse(matrix, hook)
    half = size // 2
    first = factor_inverse(matrix[:half, :half], base, hook)
    lower = mm(matrix[half:, :half], first, 1, 1)
    second = factor_inverse(matrix[half:, half:] - mm(lower, lower, 1, 1), base, hook)
    corner = -mm(second, mm(lower, first, 1, 0), 1, 0)
    top = jnp.concatenate([first, jnp.zeros_like(first)], 1)
    return jnp.concatenate([top, jnp.concatenate([corner, second], 1)], 0)

def orthogonal_top(gram, top, top_dim, inverse_ref, shifted_ref, sign_ref, hook):
    size = gram.shape[0]
    inverse = factor_inverse(gram, 64, hook)
    inverse_ref[...] = inverse
    basis = mm(top(), inverse, top_dim, 1)
    rows = lax.broadcasted_iota(jnp.int32, (size, size), 0)
    cols = lax.broadcasted_iota(jnp.int32, (size, size), 1)
    sign_square = jnp.where(rows == cols, jnp.where(basis >= 0, -1.0, 1.0), 0.0)
    shifted_ref[...] = basis - sign_square
    sign_ref[...] = jnp.sum(sign_square, axis=0, keepdims=True)


def block_transform(shifted, signs, hook):
    size = shifted.shape[0]
    outer = factor_inverse(mm(shifted, shifted, 0, 0), 64, hook)
    rows = lax.broadcasted_iota(jnp.int32, (size, size), 0)
    cols = lax.broadcasted_iota(jnp.int32, (size, size), 1)
    sign_column = jnp.sum(jnp.where(rows == cols, signs, 0.0), axis=1, keepdims=True)
    return -mm(outer, mm(outer, shifted * sign_column, 1, 1), 0, 0)


def mm3(a, b, ca=1, cb=0):
    def part(x, y):
        return lax.dot_general(
            x, y, (((ca,), (cb,)), ((), ())), preferred_element_type=jnp.float32
        )

    return part(a[0], b[0]) + (part(a[0], b[1]) + part(a[1], b[0]))


def multiply(first, second, first_dim=1, second_dim=0, precision=HI):
    return lax.dot_general(
        first,
        second,
        (((first_dim,), (second_dim,)), ((), ())),
        precision=precision,
        preferred_element_type=jnp.float32,
    )


def remote(source, target, send_sem, recv_sem, row, col):
    return pltpu.make_async_remote_copy(
        src_ref=source,
        dst_ref=target,
        send_sem=send_sem,
        recv_sem=recv_sem,
        device_id={"row": row, "col": col},
        device_id_type=MESH,
    )


class Place:
    def __init__(self, rows, cols):
        self.rows, self.cols, self.planes = rows, cols, rows // 2
        row = lax.axis_index("row")
        self.col = lax.axis_index("col")
        self.plane = row // 2
        self.core = row % 2
        self.row = row
        self.other = 2 * self.plane + (1 - self.core)
        self.me = self.core * cols + self.col

    def peers(self):
        found = []
        for core_step in range(2):
            for col_step in range(self.cols):
                if core_step or col_step:
                    core = lax.rem(self.core + core_step, 2)
                    col = lax.rem(self.col + col_step, self.cols)
                    found.append((2 * self.plane + core, col, core * self.cols + col))
        return found

    def greet(self, line=True):
        barrier = pltpu.get_barrier_semaphore()
        count = 0
        for row, col, _ in self.peers():
            pl.semaphore_signal(
                barrier, inc=1, device_id={"row": row, "col": col}, device_id_type=MESH
            )
            count += 1
        for step in range(1, self.planes) if line else ():
            row = lax.rem(self.row + 2 * step, self.rows)
            pl.semaphore_signal(
                barrier, inc=1, device_id={"row": row, "col": self.col}, device_id_type=MESH
            )
            count += 1
        pl.semaphore_wait(barrier, count)


def plane_scatter(place, peers, x_ref, parts, out_ref, send_sem, recv_sem):
    copies = []
    for slot, (row, col, piece) in enumerate(peers):
        copies.append(
            remote(
                x_ref.at[piece], parts.at[slot], send_sem.at[slot], recv_sem.at[slot], row, col
            )
        )
        copies[-1].start()
    total = x_ref[place.me]
    for slot, copy in enumerate(copies):
        copy.wait_recv()
        total = total + parts[slot]
    out_ref[place.me] = total
    for copy in copies:
        copy.wait_send()


def plane_gather(place, mine, send_sem, recv_sem):
    copies = []
    for slot, (row, col, _) in enumerate(place.peers()):
        copies.append(remote(mine, mine, send_sem.at[slot], recv_sem.at[slot], row, col))
        copies[-1].start()
    return copies


class Spread:
    def __init__(self, place, source_ref, tiles, target_ref, send_sem, recv_sem):
        self.place, self.source, self.tiles, self.target = place, source_ref, tiles, target_ref
        self.send_sem, self.recv_sem = send_sem, recv_sem
        self.tile = target_ref.shape[0] // 2

    def refs(self, index, core):
        start = pl.multiple_of(core * self.tile, self.tile)
        local = self.tiles[index] // self.place.cols
        return (
            self.source.at[pl.ds(start, self.tile), pl.ds(local * self.tile, self.tile)],
            self.target.at[pl.ds(start, self.tile), pl.ds(index * self.tile, self.tile)],
        )

    def holder(self, index):
        return self.place.col == self.tiles[index] % self.place.cols

    def copies(self, index):
        source, target = self.refs(index, self.place.core)
        return [
            remote(
                source,
                target,
                self.send_sem.at[index, slot],
                self.recv_sem.at[index, self.place.core],
                row,
                col,
            )
            for slot, (row, col, _) in enumerate(self.place.peers())
        ]

    def send(self):
        for index in range(len(self.tiles)):
            @pl.when(self.holder(index))
            def _():
                for copy in self.copies(index):
                    copy.start()
                source, target = self.refs(index, self.place.core)
                target[...] = source[...]

    def wait(self):
        for index in range(len(self.tiles)):
            for core in range(2):
                source, target = self.refs(index, core)

                @pl.when(jnp.logical_not(self.holder(index) & (self.place.core == core)))
                def _():
                    remote(
                        source,
                        target,
                        self.send_sem.at[index, 0],
                        self.recv_sem.at[index, core],
                        self.place.other,
                        self.place.col,
                    ).wait_recv()

    def finish(self):
        for index in range(len(self.tiles)):
            @pl.when(self.holder(index))
            def _():
                for copy in self.copies(index):
                    copy.wait_send()


class Chain:
    def __init__(self, place, source, x_ref, panel_ref, sems):
        self.place, self.source, self.x_ref, self.ref = place, source, x_ref, panel_ref
        self.load, self.sends, self.recv, self.share_send, self.share_recv = sems
        self.tile = x_ref.shape[-1]
        self.tiles = x_ref.shape[1]
        self.chunks = self.recv.shape[0]
        self.width = panel_ref.shape[1] // self.chunks
        self.at_source = place.plane == source

    def loads(self):
        start = pl.multiple_of(self.place.core * self.tile, self.tile)
        for tile in range(self.tiles):
            yield pltpu.make_async_copy(
                self.x_ref.at[pl.ds(0, self.tile), tile, 0, :],
                self.ref.at[pl.ds(start, self.tile), pl.ds(tile * self.tile, self.tile)],
                self.load.at[tile],
            )

    def part(self, chunk):
        start = pl.multiple_of(self.place.core * self.tile, self.tile)
        return self.ref.at[pl.ds(start, self.tile), pl.ds(chunk * self.width, self.width)]

    def hop(self, chunk, step, sem):
        part = self.part(chunk)
        row = lax.rem(self.place.row + 2 * step + self.place.rows, self.place.rows)
        return remote(part, part, self.sends.at[sem, chunk], self.recv.at[chunk], row, self.place.col)

    def shared(self, chunk):
        part = self.part(chunk)
        return remote(
            part,
            part,
            self.share_send.at[chunk],
            self.share_recv.at[chunk],
            self.place.other,
            self.place.col,
        )

    def start(self):
        @pl.when(self.at_source)
        def _():
            for copy in self.loads():
                copy.start()

    def share(self):
        @pl.when(self.at_source)
        def _():
            for copy in self.loads():
                copy.wait()
            for chunk in range(self.chunks):
                self.shared(chunk).start()

    def spread(self, first, last):
        @pl.when(self.at_source)
        def _():
            for chunk in range(first, min(last, self.chunks)):
                if self.source < self.place.planes - 1:
                    self.hop(chunk, 1, 0).start()
                if self.source > 0:
                    self.hop(chunk, -1, 1).start()

    def step(self, chunk):
        place = self.place
        for step, sem, away, more in (
            (1, 0, place.plane > self.source, place.plane < place.planes - 1),
            (-1, 1, place.plane < self.source, place.plane > 0),
        ):
            if step < 0 and self.source == 0 or step > 0 and self.source == place.planes - 1:
                continue

            @pl.when(away)
            def _():
                self.hop(chunk, step, sem).wait_recv()

                @pl.when(more)
                def _():
                    self.hop(chunk, step, sem).start()

                self.shared(chunk).start()

    def join(self):
        for chunk in range(self.chunks):
            self.shared(chunk).wait_recv()

    def finish(self, joined=False):
        place = self.place
        if joined:
            @pl.when(jnp.logical_not(self.at_source))
            def _():
                self.join()
        else:
            self.join()
        for chunk in range(self.chunks):
            self.shared(chunk).wait_send()
        for step, sem, sent in (
            (1, 0, (place.plane >= self.source) & (place.plane < place.planes - 1)),
            (-1, 1, (place.plane <= self.source) & (place.plane > 0)),
        ):

            @pl.when(sent)
            def _():
                for chunk in range(self.chunks):
                    self.hop(chunk, step, sem).wait_send()

    @staticmethod
    def semaphores(tiles, chunks):
        dma = pltpu.SemaphoreType.DMA
        return [dma((tiles,)), dma((2, chunks)), dma((chunks,)), dma((chunks,)), dma((chunks,))]


CHUNK = 256


def later_steps(chain, first, every):
    count = [0]

    def hook():
        count[0] += 1
        chunk = first + count[0] // every - 1
        if count[0] % every == 0 and first <= chunk < chain.chunks:
            chain.step(chunk)

    return hook


EARLY = 3


def first_kernel(rows, cols, x_ref, inverse_ref, shifted_ref, sign_ref, rows_ref, cols_ref, *refs):
    stack, parts, gram_ref, top_ref = refs[:4]
    send_one, recv_one, line_send, line_recv, send_two, recv_two = refs[4:10]
    load, send_row, recv_row, top_send, top_recv = refs[10:15]
    place = Place(rows, cols)
    tile, tiles = x_ref.shape[-1], x_ref.shape[1]
    panel_tiles = BAND // tile
    held = PANELS * panel_tiles
    chain = Chain(place, 0, x_ref, cols_ref, refs[15:])
    spread = Spread(
        place, cols_ref, tuple(range(panel_tiles, 2 * panel_tiles)), top_ref, top_send, top_recv
    )
    first = place.plane == 0

    def spot(col):
        start = pl.multiple_of(lax.rem(col, panel_tiles) * tile, tile)
        return rows_ref.at[col // panel_tiles, :, pl.ds(start, tile)]

    has = place.col < held
    own = spot(lax.rem(place.col, held))
    fill = pltpu.make_async_copy(x_ref.at[:, 0, 0, :], own, load.at[0])

    @pl.when(has)
    def _():
        fill.start()

    chain.start()
    place.greet()
    copies = [
        remote(
            own,
            own,
            send_row.at[step - 1],
            recv_row.at[lax.rem(place.col, held)],
            place.row,
            lax.rem(place.col + step, cols),
        )
        for step in range(1, cols)
    ]
    line = [
        remote(
            gram_ref.at[place.me],
            gram_ref.at[place.me],
            line_send.at[step - 1],
            line_recv.at[0],
            lax.rem(place.row + 2 * step, rows),
            place.col,
        )
        for step in range(1, place.planes)
    ]
    chain.share()
    chain.spread(0, EARLY)

    @pl.when(first)
    def _():
        chain.join()
        width = tile * tiles // 2
        offset = place.core * width
        lanes = lax.broadcasted_iota(jnp.int32, (cols_ref.shape[0], width), 1) + offset
        limit = jnp.where(place.col < panel_tiles, tile, 0)
        value = cols_ref[:, pl.ds(pl.multiple_of(offset, tile), width)]
        value = jnp.where(lanes >= limit, value, 0.0)
        gram = mm(value, value, 1, 1)
        size = stack.shape[1]
        for piece in range(stack.shape[0]):
            stack[piece] = gram[piece * size : (piece + 1) * size]
        plane_scatter(place, place.peers(), stack, parts, gram_ref, send_one, recv_one)
        for copy in line:
            copy.start()

    chain.spread(EARLY, chain.chunks)

    for chunk in range(EARLY):
        @pl.when(place.plane <= EARLY - chunk)
        def _():
            chain.step(chunk)

    @pl.when(place.plane > 0)
    def _():
        line[0].wait_recv()

    gathers = plane_gather(place, gram_ref.at[place.me], send_two, recv_two)
    for chunk in range(EARLY):
        @pl.when(place.plane > EARLY - chunk)
        def _():
            chain.step(chunk)

    spread.send()

    @pl.when(has)
    def _():
        fill.wait()
        for copy in copies:
            copy.start()

    for copy in gathers:
        copy.wait()

    def top():
        spread.wait()
        return top_ref[...]

    size = inverse_ref.shape[0]
    orthogonal_top(
        gram_ref[...].reshape(size, size), top, 0, inverse_ref, shifted_ref, sign_ref,
        later_steps(chain, EARLY, 2),
    )

    @pl.when(first)
    def _():
        for copy in line:
            copy.wait_send()

    spread.finish()

    @pl.when(has)
    def _():
        for copy in copies:
            copy.wait_send()

    for col in range(held):
        @pl.when(place.col != col)
        def _():
            remote(spot(col), spot(col), send_row.at[0], recv_row.at[col], place.row, place.col).wait_recv()

    chain.finish(True)


def first_panel(x4, collective_id):
    rows, cols = lax.axis_size("row"), lax.axis_size("col")
    row_count, tiles, _, tile = x4.shape
    width = tiles * tile
    count = 2 * cols
    pieces = (count, BAND // count, BAND)
    vmem = pl.BlockSpec(memory_space=pltpu.VMEM)
    dma = pltpu.SemaphoreType.DMA
    panel_tiles = BAND // tile
    square = jax.ShapeDtypeStruct((BAND, BAND), x4.dtype)
    return pl.pallas_call(
        functools.partial(first_kernel, rows, cols),
        out_shape=(
            square,
            square,
            jax.ShapeDtypeStruct((1, BAND), x4.dtype),
            jax.ShapeDtypeStruct((PANELS, row_count, BAND), x4.dtype),
            jax.ShapeDtypeStruct((BAND, width), x4.dtype),
        ),
        in_specs=[pl.BlockSpec(memory_space=pltpu.HBM)],
        out_specs=(vmem,) * 5,
        scratch_shapes=[
            pltpu.VMEM(pieces, x4.dtype),
            pltpu.VMEM((count - 1,) + pieces[1:], x4.dtype),
            pltpu.VMEM(pieces, x4.dtype),
            pltpu.VMEM((BAND, BAND), x4.dtype),
            dma((count - 1,)),
            dma((count - 1,)),
            dma((rows // 2 - 1,)),
            dma((1,)),
            dma((count - 1,)),
            dma((count - 1,)),
            dma((1,)),
            dma((cols - 1,)),
            dma((PANELS * panel_tiles,)),
            dma((panel_tiles, count - 1)),
            dma((panel_tiles, 2)),
        ]
        + Chain.semaphores(tiles, width // CHUNK),
        compiler_params=pltpu.CompilerParams(
            collective_id=collective_id, has_side_effects=True, vmem_limit_bytes=56 * MIB
        ),
    )(x4)


def next_kernel(rows, cols, below, *refs):
    refs = list(refs)
    take = lambda count: [refs.pop(0) for _ in range(count)]
    (
        vec_rows, applied_rows, vec_cols, applied, transform_ref, inner_ref, applied_next,
        old_ref, later_ref, x_ref,
    ) = take(10)
    inverse_ref, shifted_ref, sign_ref, panel_ref, cols_ref = take(5)
    old_high, old_low, new_high, new_low, update_ref, ahead_ref = take(6)
    gram_in, gram_sum = take(2)
    near, near_sum, parts, gram_ref, top_ref = refs[:5]
    near_send, near_recv, line_send, line_recv, send_two, recv_two = refs[5:11]
    top_line_send, top_line_recv, top_send, top_recv = refs[11:15]
    place = Place(rows, cols)
    tile = x_ref.shape[-1]
    panel_tiles = BAND // tile
    number = 2 * panel_tiles
    chain = Chain(place, 1, x_ref, cols_ref, refs[15:])
    chain.start()
    place.greet()
    chain.share()
    chain.spread(0, EARLY)
    half_full = 0.5 * mm(transform_ref[...], inner_ref[...], 1, 0)
    half = split(half_full)
    old = old_ref[...]
    ahead = applied_next[...] - mm(half_full, old, 0, 1)
    ahead_ref[...] = ahead
    vec = vec_rows[...]
    vec_parts = split(vec)
    change = applied_rows[...] - mm3(vec_parts, half)
    panel = later_ref[1] - mm(vec, ahead, 1, 0) - mm(change, old, 1, 1)
    lines = lax.broadcasted_iota(jnp.int32, panel.shape, 0)
    above = (below + BAND) // tile
    limit = (above // rows + jnp.where(place.row < above % rows, 1, 0)) * tile
    panel = jnp.where(lines >= limit, panel, 0.0)
    panel_ref[...] = panel
    gram_sum[...] = mm(panel, panel, 0, 0)
    change_parts = split(change)
    for start, value in ((0, vec_parts), (BAND, change_parts)):
        old_high[:, start : start + BAND] = value[0]
        old_low[:, start : start + BAND] = value[1]
    size = BAND
    height = gram_in.shape[2]
    for col in range(cols):
        for core in range(2):
            start = (2 * col + core) * height
            gram_in[col, core] = gram_sum[start : start + height, :]
    chain.step(0)
    swap = remote(
        gram_in.at[place.col, 1 - place.core], near.at[0], near_send.at[0], near_recv.at[0],
        place.other, place.col,
    )
    swap.start()

    top_plane = number % rows // 2
    start = pl.multiple_of(place.core * tile, tile)
    local = number // rows * tile
    block = panel_ref.at[pl.ds(local, tile), :]
    target = top_ref.at[pl.ds(start, tile), :]
    at_top = place.plane == top_plane

    def top_line(step):
        return remote(
            block, target, top_line_send.at[step - 1], top_line_recv.at[0],
            lax.rem(place.row + 2 * step, rows), place.col,
        )

    top_near = remote(target, target, top_send.at[0], top_recv.at[0], place.other, place.col)
    top_first = remote(block, target, top_send.at[0], top_recv.at[0], place.other, place.col)

    swap.wait_recv()
    near_sum[0] = gram_in[place.col, place.core] + near[0]
    line = [
        remote(
            near_sum.at[0], parts.at[step - 1], line_send.at[step - 1], line_recv.at[step - 1],
            lax.rem(place.row + 2 * step, rows), place.col,
        )
        for step in range(1, place.planes)
    ]
    for copy in line:
        copy.start()

    @pl.when(at_top)
    def _():
        for step in range(1, place.planes):
            top_line(step).start()
        top_first.start()
        target[...] = block[...]

    chain.spread(EARLY, chain.chunks)
    chain.step(1)
    group = 5 if x_ref.shape[1] % 10 == 0 else 1
    wide = x_ref.shape[1] // group * tile
    half_t = split(half_full.T)

    def own_cols(index, carry):
        here = pl.ds(pl.multiple_of(index * wide, wide), wide)
        vec = split(vec_cols[:, here])
        change = applied[:, here] - mm3(half_t, vec)
        update_ref[:, here] = change
        for start, value in ((0, split(change)), (size, vec)):
            new_high[start : start + size, here] = value[0]
            new_low[start : start + size, here] = value[1]
        return carry

    lax.fori_loop(0, group, own_cols, 0)
    chain.step(2)
    total = near_sum[0]
    for slot, copy in enumerate(line):
        copy.wait_recv()
        total = total + parts[slot]
    piece = 2 * place.col + place.core
    gram_ref[piece] = total
    gathers = plane_gather(place, gram_ref.at[piece], send_two, recv_two)

    @pl.when(jnp.logical_not(at_top))
    def _():
        top_line(1).wait_recv()
        top_near.start()

    ready = min(6, chain.chunks)
    for chunk in range(3, ready):
        chain.step(chunk)
    for copy in gathers:
        copy.wait()

    def top():
        top_near.wait_recv()
        return top_ref[...]

    orthogonal_top(
        gram_ref[...].reshape(size, size), top, 1, inverse_ref, shifted_ref, sign_ref,
        later_steps(chain, ready, 2),
    )
    swap.wait_send()
    for copy in line:
        copy.wait_send()
    top_near.wait_send()

    @pl.when(at_top)
    def _():
        for step in range(1, place.planes):
            top_line(step).wait_send()

    chain.finish()


def next_panel(operands, x4, below, collective_id):
    rows, cols = lax.axis_size("row"), lax.axis_size("col")
    row_count, tiles, _, tile = x4.shape
    width = tiles * tile
    count = 2 * cols
    piece = (BAND // count, BAND)
    planes = rows // 2
    vmem = pl.BlockSpec(memory_space=pltpu.VMEM)
    dma = pltpu.SemaphoreType.DMA
    f32, bf16 = jnp.float32, jnp.bfloat16
    shape = jax.ShapeDtypeStruct
    square = shape((BAND, BAND), f32)
    return pl.pallas_call(
        functools.partial(next_kernel, rows, cols, below),
        out_shape=(
            square,
            square,
            shape((1, BAND), f32),
            shape((row_count, BAND), f32),
            shape((BAND, width), f32),
            shape((row_count, 2 * BAND), bf16),
            shape((row_count, 2 * BAND), bf16),
            shape((2 * BAND, width), bf16),
            shape((2 * BAND, width), bf16),
            shape((BAND, width), f32),
            square,
        ),
        in_specs=[vmem] * len(operands) + [pl.BlockSpec(memory_space=pltpu.HBM)],
        out_specs=(vmem,) * 11,
        scratch_shapes=[
            pltpu.VMEM((cols, 2) + piece, f32),
            pltpu.VMEM((BAND, BAND), f32),
            pltpu.VMEM((1,) + piece, f32),
            pltpu.VMEM((1,) + piece, f32),
            pltpu.VMEM((planes - 1,) + piece, f32),
            pltpu.VMEM((count,) + piece, f32),
            pltpu.VMEM((BAND, BAND), f32),
            dma((1,)),
            dma((1,)),
            dma((planes - 1,)),
            dma((planes - 1,)),
            dma((count - 1,)),
            dma((count - 1,)),
            dma((planes - 1,)),
            dma((1,)),
            dma((1,)),
            dma((1,)),
        ]
        + Chain.semaphores(tiles, width // CHUNK),
        compiler_params=pltpu.CompilerParams(
            collective_id=collective_id, has_side_effects=True, vmem_limit_bytes=44 * MIB
        ),
    )(*operands, x4)


def split(value):
    high = value.astype(jnp.bfloat16)
    return high, (value - high.astype(jnp.float32)).astype(jnp.bfloat16)


def split_outside(value):
    high = lax.reduce_precision(value, 8, 7)
    return high.astype(jnp.bfloat16), (value - high).astype(jnp.bfloat16)


def dot(a, b):
    return jnp.dot(a, b, preferred_element_type=jnp.float32)


def apply_kernel(rows, cols, tiles, fixed, *refs):
    place = Place(rows, cols)
    refs = list(refs)
    take = lambda count: [refs.pop(0) for _ in range(count)]
    x_ref, left_ref, shifted_ref, sign_ref, vec_ref = take(5)
    old_high, old_low, new_high, new_low = take(4) if fixed else [None] * 4
    applied_row_ref, transform_ref, applied_ref, inner_ref = take(4)
    next_ref = take(1)[0] if tiles else None
    kept_ref = take(1)[0] if fixed else None
    block, part, near, pair, left_in, right_in, left_out, right_out, out_ref, row_ref = take(10)
    total_ref, stack, parts = take(3)
    (
        load, near_send, near_recv, left_send, left_recv, right_send, right_recv,
        both_send, both_recv, row_send, row_recv, send_one, recv_one, send_two, recv_two,
    ) = take(15)
    next_sems = take(2) if tiles else None
    store = take(1)[0] if fixed else None
    plane, core, planes = place.plane, place.core, place.planes
    tile = x_ref.shape[-1]
    chunks = block.shape[0]
    pieces = pair.shape[0] // chunks
    depth = pair.shape[1]
    subs = chunks * pieces
    size = left_ref.shape[0] // 2

    def load_of(chunk, index):
        return pltpu.make_async_copy(
            x_ref.at[:, 2 * chunk + index, 0, :],
            block.at[chunk, :, pl.ds(index * tile, tile)],
            load.at[chunk, index],
        )

    def store_of(chunk, index):
        return pltpu.make_async_copy(
            block.at[chunk, :, pl.ds(index * tile, tile)],
            kept_ref.at[:, 2 * chunk + index, 0, :],
            store.at[chunk, index],
        )

    for chunk in range(chunks):
        for index in range(2):
            load_of(chunk, index).start()
    place.greet()

    def near_of(chunk):
        return remote(
            part.at[chunk, 1 - core],
            near.at[chunk],
            near_send.at[chunk],
            near_recv.at[chunk],
            place.other,
            place.col,
        )

    def rightward(source, index):
        return remote(
            source.at[index], left_in.at[index], right_send.at[index], left_recv.at[index],
            lax.rem(place.row + 2, rows), place.col,
        )

    def leftward(source, index):
        return remote(
            source.at[index], right_in.at[index], left_send.at[index], right_recv.at[index],
            lax.rem(place.row + rows - 2, rows), place.col,
        )

    def joined(chunk):
        near_of(chunk).wait_recv()
        for piece in range(pieces):
            pair[chunk * pieces + piece] = part[chunk, core, piece] + near[chunk, piece]

        @pl.when(plane == 0)
        def _():
            for piece in range(pieces):
                rightward(pair, chunk * pieces + piece).start()

        @pl.when(plane == planes - 1)
        def _():
            for piece in range(pieces):
                leftward(pair, chunk * pieces + piece).start()

    def product(chunk, carry):
        for index in range(2):
            load_of(chunk, index).wait()
        if fixed:
            here = pl.ds(pl.multiple_of(chunk * 2 * tile, 2 * tile), 2 * tile)
            change = dot(old_high[...], new_high[:, here]) + (
                dot(old_low[...], new_high[:, here]) + dot(old_high[...], new_low[:, here])
            )
            block[chunk] = block[chunk] - change
            for index in range(2):
                store_of(chunk, index).start()
        high, low = split(block[chunk])
        value = dot(left_ref[...], high)
        value = value[:size] + (value[size:] + dot(left_ref[:size], low))
        for index in range(2):
            for piece in range(pieces):
                part[chunk, index, piece] = value[
                    piece * depth : (piece + 1) * depth, index * tile : (index + 1) * tile
                ]
        near_of(chunk).start()

        @pl.when(chunk > 0)
        def _():
            joined(chunk - 1)

        for piece in range(pieces):
            chain((chunk - BEHIND) * pieces + piece, 0)
        return carry

    left_lag = HOP * jnp.maximum(plane - 1, 0)
    right_lag = HOP * jnp.maximum(planes - 2 - plane, 0)
    last_lag = jnp.maximum(left_lag, right_lag)
    held = cols * core + place.col
    source = held // 2 == plane
    target_row = 2 * plane + lax.rem(place.col, 2)
    to_self = target_row == place.row

    def depths(index):
        return pl.ds(pl.multiple_of(lax.rem(index, pieces) * depth, depth), depth)

    def lanes(index):
        return pl.ds(pl.multiple_of((2 * (index // pieces) + core) * tile, tile), tile)

    def row_lanes(index):
        return pl.ds(pl.multiple_of(index // pieces * tile, tile), tile)

    def both_of(index):
        spot = out_ref.at[depths(index), lanes(index)]
        return remote(spot, spot, both_send.at[index], both_recv.at[index], place.other, place.col)

    def row_of(index, step):
        return remote(
            out_ref.at[depths(index), lanes(index)],
            row_ref.at[depths(index), row_lanes(index)],
            row_send.at[index, step],
            row_recv.at[index],
            target_row,
            lax.rem(place.col + step, cols),
        )

    def chain(step, carry):
        index = step - left_lag

        @pl.when((plane > 0) & (index >= 0) & (index < subs))
        def _():
            rightward(pair, index).wait_recv()

            @pl.when(plane < planes - 1)
            def _():
                right_out[index] = left_in[index] + pair[index]
                rightward(right_out, index).start()

        other = step - right_lag

        @pl.when((plane < planes - 1) & (other >= 0) & (other < subs))
        def _():
            leftward(pair, other).wait_recv()

            @pl.when(plane > 0)
            def _():
                left_out[other] = right_in[other] + pair[other]
                leftward(left_out, other).start()

        done = step - last_lag

        @pl.when((done >= 0) & (done < subs))
        def _():
            @pl.when(plane == 0)
            def _():
                out_ref[depths(done), lanes(done)] = pair[done] + right_in[done]

            @pl.when(plane == planes - 1)
            def _():
                out_ref[depths(done), lanes(done)] = left_in[done] + pair[done]

            @pl.when((plane > 0) & (plane < planes - 1))
            def _():
                out_ref[depths(done), lanes(done)] = right_out[done] + right_in[done]

            both_of(done).start()

            @pl.when(source)
            def _():
                for step in range(1, cols):
                    row_of(done, step).start()

                @pl.when(to_self)
                def _():
                    row_ref[depths(done), row_lanes(done)] = out_ref[depths(done), lanes(done)]

                @pl.when(jnp.logical_not(to_self))
                def _():
                    row_of(done, 0).start()

        return carry

    lax.fori_loop(0, chunks, product, 0)
    joined(chunks - 1)
    steps = subs + HOP * (planes - 2)
    count = [0, max(chunks - BEHIND, 0) * pieces]

    def hook():
        count[0] += 1
        if count[0] % 2 == 0 and count[1] < steps:
            chain(count[1], 0)
            count[1] += 1

    transform_ref[...] = block_transform(shifted_ref[...], sign_ref[...], hook)
    if count[1] < steps:
        lax.fori_loop(count[1], steps, chain, 0)
    total_ref[...] = jnp.zeros_like(total_ref)
    transform = split(transform_ref[...])

    def finished(number, carry):
        for index in range(2 * pieces):
            both_of(2 * pieces * number + index).wait_recv()
        here = pl.ds(pl.multiple_of(number * 4 * tile, 4 * tile), 4 * tile)
        applied = mm3(transform, split(out_ref[:, here]))
        applied_ref[:, here] = applied
        total_ref[...] += mm3(split(vec_ref[:, here]), split(applied), 1, 1)
        return carry

    def finished_one(number, carry):
        for index in range(pieces):
            both_of(pieces * number + index).wait_recv()
        here = pl.ds(pl.multiple_of(number * 2 * tile, 2 * tile), 2 * tile)
        applied = mm3(transform, split(out_ref[:, here]))
        applied_ref[:, here] = applied
        total_ref[...] += mm3(split(vec_ref[:, here]), split(applied), 1, 1)
        return carry

    if chunks % 2 == 0:
        lax.fori_loop(0, chunks // 2, finished, 0)
    else:
        lax.fori_loop(0, chunks, finished_one, 0)
    height = stack.shape[1]
    for piece in range(stack.shape[0]):
        stack[piece] = total_ref[piece * height : (piece + 1) * height, :]
    if tiles:
        spread = Spread(place, applied_ref, tiles, next_ref, *next_sems)
        spread.send()
    plane_scatter(place, place.peers()[: cols - 1], stack, parts, inner_ref, send_one, recv_one)
    gathers = plane_gather(place, inner_ref.at[place.me], send_two, recv_two)
    gets = jnp.logical_not(source & to_self)

    def drain(index, carry):
        both_of(index).wait_send()

        @pl.when(plane < planes - 1)
        def _():
            rightward(pair, index).wait_send()

        @pl.when(plane > 0)
        def _():
            leftward(pair, index).wait_send()

        @pl.when(source)
        def _():
            for step in range(1, cols):
                row_of(index, step).wait_send()

            @pl.when(jnp.logical_not(to_self))
            def _():
                row_of(index, 0).wait_send()

        @pl.when(gets)
        def _():
            row_of(index, 0).wait_recv()

        return carry

    def drain_chunk(chunk, carry):
        if fixed:
            for index in range(2):
                store_of(chunk, index).wait()
        near_of(chunk).wait_send()
        return carry

    lax.fori_loop(0, subs, drain, 0)
    lax.fori_loop(0, chunks, drain_chunk, 0)
    applied_row_ref[...] = mm3(split(row_ref[...].T), split(transform_ref[...]), 1, 1)
    for copy in gathers:
        copy.wait()
    if tiles:
        spread.wait()
        spread.finish()


PIECES = 2
HOP = 3
BEHIND = 3


def apply(x4, left, shifted, signs, vec_cols, tiles, more, collective_id):
    rows, cols = lax.axis_size("row"), lax.axis_size("col")
    row_count, held_tiles, _, tile = x4.shape
    width = held_tiles * tile
    chunks = held_tiles // 2
    count = 2 * cols
    vmem = pl.BlockSpec(memory_space=pltpu.VMEM)
    hbm = pl.BlockSpec(memory_space=pltpu.HBM)
    dma = pltpu.SemaphoreType.DMA
    f32 = jnp.float32
    piece = (BAND // PIECES, tile)
    subs = PIECES * chunks
    sums = (count, BAND // count, BAND)
    kept = bool(more)
    square = jax.ShapeDtypeStruct((BAND, BAND), f32)
    wide = jax.ShapeDtypeStruct((BAND, width), f32)
    shapes = (
        jax.ShapeDtypeStruct((row_count, BAND), f32),
        square,
        wide,
        jax.ShapeDtypeStruct(sums, f32),
    )
    shapes += (square,) if tiles else ()
    out = pl.pallas_call(
        functools.partial(apply_kernel, rows, cols, tiles, kept),
        out_shape=shapes + ((jax.ShapeDtypeStruct(x4.shape, x4.dtype),) if kept else ()),
        in_specs=[hbm] + [vmem] * (4 + len(more)),
        out_specs=(vmem,) * len(shapes) + ((hbm,) if kept else ()),
        scratch_shapes=[
            pltpu.VMEM((chunks, row_count, 2 * tile), f32),
            pltpu.VMEM((chunks, 2, PIECES) + piece, f32),
            pltpu.VMEM((chunks, PIECES) + piece, f32),
        ]
        + [pltpu.VMEM((subs,) + piece, f32)] * 5
        + [
            pltpu.VMEM((BAND, width), f32),
            pltpu.VMEM((BAND, row_count), f32),
            pltpu.VMEM((BAND, BAND), f32),
            pltpu.VMEM(sums, f32),
            pltpu.VMEM((cols - 1,) + sums[1:], f32),
        ]
        + [dma((chunks, 2)), dma((chunks,)), dma((chunks,))]
        + [dma((subs,))] * 6
        + [dma((subs, cols)), dma((subs,))]
        + [dma((cols - 1,))] * 2
        + [dma((count - 1,))] * 2
        + ([dma((len(tiles), count - 1)), dma((len(tiles), 2))] if tiles else [])
        + ([dma((chunks, 2))] if kept else []),
        compiler_params=pltpu.CompilerParams(
            collective_id=collective_id, has_side_effects=True, vmem_limit_bytes=(60 if kept else 48) * MIB
        ),
    )(x4, left, shifted, signs, vec_cols, *more)
    out = list(out)
    out[3] = out[3].reshape(BAND, BAND)
    return out


def update_kernel(x_ref, left_high, left_low, right_high, right_low, out_ref, block, result, load, store):
    tile = x_ref.shape[-1]
    chunks = x_ref.shape[1] // 2

    def load_of(chunk, index):
        return pltpu.make_async_copy(
            x_ref.at[:, 2 * chunk + index, 0, :],
            block.at[lax.rem(chunk, 2), :, pl.ds(index * tile, tile)],
            load.at[lax.rem(chunk, 2), index],
        )

    def store_of(chunk, index):
        return pltpu.make_async_copy(
            result.at[lax.rem(chunk, 2), :, pl.ds(index * tile, tile)],
            out_ref.at[:, 2 * chunk + index, 0, :],
            store.at[lax.rem(chunk, 2), index],
        )

    for chunk in range(2):
        for index in range(2):
            load_of(chunk, index).start()

    def body(chunk, carry):
        slot = lax.rem(chunk, 2)
        for index in range(2):
            load_of(chunk, index).wait()

        @pl.when(chunk >= 2)
        def _():
            for index in range(2):
                store_of(chunk - 2, index).wait()

        here = pl.ds(pl.multiple_of(chunk * 2 * tile, 2 * tile), 2 * tile)
        value = dot(left_high[...], right_high[:, here]) + (
            dot(left_low[...], right_high[:, here]) + dot(left_high[...], right_low[:, here])
        )
        result[slot] = block[slot] - value
        for index in range(2):
            store_of(chunk, index).start()

        @pl.when(chunk + 2 < chunks)
        def _():
            for index in range(2):
                load_of(chunk + 2, index).start()

        return carry

    lax.fori_loop(0, chunks, body, 0)
    for chunk in range(chunks - 2, chunks):
        for index in range(2):
            store_of(chunk, index).wait()


def update(x4, left, right):
    row_count, tiles, _, tile = x4.shape
    vmem = pl.BlockSpec(memory_space=pltpu.VMEM)
    hbm = pl.BlockSpec(memory_space=pltpu.HBM)
    dma = pltpu.SemaphoreType.DMA
    return pl.pallas_call(
        update_kernel,
        out_shape=jax.ShapeDtypeStruct(x4.shape, x4.dtype),
        in_specs=[hbm] + [vmem] * 4,
        out_specs=hbm,
        scratch_shapes=[pltpu.VMEM((2, row_count, 2 * tile), jnp.float32)] * 2
        + [dma((2, 2)), dma((2, 2))],
        compiler_params=pltpu.CompilerParams(vmem_limit_bytes=48 * MIB),
    )(x4, *left, *right)


def on_device(matrix_tiles):
    tile_shape = matrix_tiles.shape
    block_rows, _, tile_size, block_cols = tile_shape[:4]
    row_count = block_rows * tile_size
    col_count = block_cols * tile_size
    row_devices = lax.axis_size("row")
    col_devices = lax.axis_size("col")
    row_index = lax.axis_index("row")
    panel_tiles = BAND // tile_size
    assert row_devices == 2 * col_devices and PANELS * panel_tiles <= col_devices
    x4 = matrix_tiles.reshape(row_count, block_cols, 1, tile_size)

    def positions(count, devices, index):
        place = jnp.arange(count, dtype=jnp.int32)
        return (place // tile_size * devices + index) * tile_size + place % tile_size

    global_rows = positions(row_count, row_devices, row_index)
    global_cols = positions(col_count, lax.axis_size("col"), lax.axis_index("col"))
    band = jnp.arange(BAND, dtype=jnp.int32)
    inverse, shifted, signs, rows_held, panel_cols = first_panel(x4, 0)
    panel_rows = rows_held[0]
    kept, more = x4, ()
    for panel_index in range(PANELS):
        below = (panel_index + 1) * BAND
        last = panel_index == PANELS - 1
        panel_rows = jnp.where((global_rows >= below)[:, None], panel_rows, 0.0)
        unit_rows = (global_rows[:, None] - below == band[None, :]).astype(jnp.float32)
        unit_rows_t = (band[:, None] == global_rows[None, :] - below).astype(jnp.float32)
        vec_rows = multiply(panel_rows, inverse, 1, 1) - unit_rows * signs
        vec_rows_t = multiply(inverse, panel_rows, 1, 1) - unit_rows_t * signs.reshape(BAND, 1)
        panel_cols = jnp.where((global_cols >= below)[None, :], panel_cols, 0.0)
        unit_cols = (band[:, None] == global_cols[None, :] - below).astype(jnp.float32)
        vec_cols = multiply(inverse, panel_cols) - unit_cols * signs.reshape(BAND, 1)
        first = below // tile_size
        applied_rows, transform, applied, inner, *rest = apply(
            kept,
            jnp.concatenate(split_outside(vec_rows_t), 0),
            shifted,
            signs,
            vec_cols,
            () if last else tuple(range(first, first + panel_tiles)),
            more,
            1 + panel_index,
        )
        if last:
            break
        old_shifted, old_cols = shifted, vec_cols
        (
            inverse, shifted, signs, panel_rows, panel_cols,
            old_high, old_low, new_high, new_low, update_cols, update_next,
        ) = next_panel(
            (
                vec_rows, applied_rows, vec_cols, applied, transform, inner, rest[0], shifted,
                rows_held,
            ),
            x4,
            below,
            3,
        )
        more = (old_high, old_low, new_high, new_low)
        panel_cols = (
            panel_cols - multiply(update_next, old_cols, 0, 0) - multiply(old_shifted, update_cols)
        )
    half_inner = 0.5 * multiply(transform, inner)
    update_rows = applied_rows - multiply(vec_rows, half_inner)
    update_cols = applied - multiply(half_inner, vec_cols, 0, 0)
    left = split_outside(jnp.concatenate([vec_rows, update_rows], 1))
    right = split_outside(jnp.concatenate([update_cols, vec_cols], 0))
    return update(rest[0], left, right).reshape(tile_shape)


def solution(mesh):
    return jax.shard_map(
        on_device,
        mesh=mesh,
        in_specs=(P(None, "row", None, None, "col", None),),
        out_specs=P(None, "row", None, None, "col", None),
        check_vma=False,
    )
```

```python
import functools

import jax
import jax.numpy as jnp
from jax import lax
from jax.experimental import pallas as pl
from jax.experimental.pallas import tpu as pltpu
from jax.sharding import PartitionSpec as P

BAND = 256
PANELS = 2
MIB = 1024 * 1024
MESH = pl.DeviceIdType.MESH

HI = lax.Precision.HIGHEST
def mm(a, b, ca, cb):
    return lax.dot_general(a, b, (((ca,), (cb,)), ((), ())), precision=HI, preferred_element_type=jnp.float32)

def base_inverse(block, hook):
    size = block.shape[0]
    wide = (8, 2 * size)
    group = 8
    places = lax.broadcasted_iota(jnp.int32, wide, 0)
    cols = lax.broadcasted_iota(jnp.int32, wide, 1)
    work = []
    for k in range(size // 8):
        unit = jnp.where(places + 8 * k == cols, 1.0, 0.0)[:, :size]
        work.append(jnp.concatenate([block[8 * k : 8 * k + 8], unit], 1))
    for start in range(0, size, group):
        own, offset = divmod(start, 8)
        rows = [jnp.broadcast_to(work[own][offset + i : offset + i + 1], wide) for i in range(group)]
        pivot = [
            [jnp.broadcast_to(rows[i][:, start + j : start + j + 1], wide) for j in range(group)]
            for i in range(group)
        ]
        first = own if offset + group < 8 else own + 1
        columns = [
            [jnp.broadcast_to(work[k][:, start + i : start + i + 1], wide) for i in range(group)]
            for k in range(first, len(work))
        ]
        scaled = []
        for i in range(group):
            inverse = 1.0 / pivot[i][i]
            scaled.append(rows[i] * inverse)
            for j in range(i + 1, group):
                ratio = pivot[i][j] * inverse
                for l in range(j, group):
                    pivot[j][l] = pivot[j][l] - ratio * pivot[i][l]
                rows[j] = rows[j] - ratio * rows[i]
                for column in columns:
                    column[j] = column[j] - ratio * column[i]
        for k, column in zip(range(first, len(work)), columns):
            change = column[0] * scaled[0]
            for i in range(1, group):
                change = change + column[i] * scaled[i]
            if k == own:
                change = jnp.where(places >= offset + group, change, 0.0)
            work[k] = work[k] - change
        for i in range(group):
            work[own] = jnp.where(places == offset + i, rows[i], work[own])
        hook()
    result = []
    for k, value in enumerate(work):
        pivots = jnp.sum(jnp.where(places + 8 * k == cols, value, 0.0), axis=1, keepdims=True)
        result.append(value[:, size:] * (1.0 / jnp.sqrt(pivots)))
    return jnp.concatenate(result, 0)


def factor_inverse(matrix, base, hook):
    size = matrix.shape[0]
    if size <= base:
        return base_inverse(matrix, hook)
    half = size // 2
    first = factor_inverse(matrix[:half, :half], base, hook)
    lower = mm(matrix[half:, :half], first, 1, 1)
    second = factor_inverse(matrix[half:, half:] - mm(lower, lower, 1, 1), base, hook)
    corner = -mm(second, mm(lower, first, 1, 0), 1, 0)
    top = jnp.concatenate([first, jnp.zeros_like(first)], 1)
    return jnp.concatenate([top, jnp.concatenate([corner, second], 1)], 0)

def orthogonal_top(gram, top, top_dim, inverse_ref, shifted_ref, sign_ref, hook):
    size = gram.shape[0]
    inverse = factor_inverse(gram, 64, hook)
    inverse_ref[...] = inverse
    basis = mm(top(), inverse, top_dim, 1)
    rows = lax.broadcasted_iota(jnp.int32, (size, size), 0)
    cols = lax.broadcasted_iota(jnp.int32, (size, size), 1)
    sign_square = jnp.where(rows == cols, jnp.where(basis >= 0, -1.0, 1.0), 0.0)
    shifted_ref[...] = basis - sign_square
    sign_ref[...] = jnp.sum(sign_square, axis=0, keepdims=True)


def block_transform(shifted, signs, hook):
    size = shifted.shape[0]
    outer = factor_inverse(mm(shifted, shifted, 0, 0), 64, hook)
    rows = lax.broadcasted_iota(jnp.int32, (size, size), 0)
    cols = lax.broadcasted_iota(jnp.int32, (size, size), 1)
    sign_column = jnp.sum(jnp.where(rows == cols, signs, 0.0), axis=1, keepdims=True)
    return -mm(outer, mm(outer, shifted * sign_column, 1, 1), 0, 0)


def mm3(a, b, ca=1, cb=0):
    def part(x, y):
        return lax.dot_general(
            x, y, (((ca,), (cb,)), ((), ())), preferred_element_type=jnp.float32
        )

    return part(a[0], b[0]) + (part(a[0], b[1]) + part(a[1], b[0]))


def multiply(first, second, first_dim=1, second_dim=0, precision=HI):
    return lax.dot_general(
        first,
        second,
        (((first_dim,), (second_dim,)), ((), ())),
        precision=precision,
        preferred_element_type=jnp.float32,
    )


def remote(source, target, send_sem, recv_sem, row, col):
    return pltpu.make_async_remote_copy(
        src_ref=source,
        dst_ref=target,
        send_sem=send_sem,
        recv_sem=recv_sem,
        device_id={"row": row, "col": col},
        device_id_type=MESH,
    )


class Place:
    def __init__(self, rows, cols):
        self.rows, self.cols, self.planes = rows, cols, rows // 2
        row = lax.axis_index("row")
        self.col = lax.axis_index("col")
        self.plane = row // 2
        self.core = row % 2
        self.row = row
        self.other = 2 * self.plane + (1 - self.core)
        self.me = self.core * cols + self.col

    def peers(self):
        found = []
        for core_step in range(2):
            for col_step in range(self.cols):
                if core_step or col_step:
                    core = lax.rem(self.core + core_step, 2)
                    col = lax.rem(self.col + col_step, self.cols)
                    found.append((2 * self.plane + core, col, core * self.cols + col))
        return found

    def greet(self, line=True):
        barrier = pltpu.get_barrier_semaphore()
        count = 0
        for row, col, _ in self.peers():
            pl.semaphore_signal(
                barrier, inc=1, device_id={"row": row, "col": col}, device_id_type=MESH
            )
            count += 1
        for step in range(1, self.planes) if line else ():
            row = lax.rem(self.row + 2 * step, self.rows)
            pl.semaphore_signal(
                barrier, inc=1, device_id={"row": row, "col": self.col}, device_id_type=MESH
            )
            count += 1
        pl.semaphore_wait(barrier, count)


def plane_scatter(place, peers, x_ref, parts, out_ref, send_sem, recv_sem):
    copies = []
    for slot, (row, col, piece) in enumerate(peers):
        copies.append(
            remote(
                x_ref.at[piece], parts.at[slot], send_sem.at[slot], recv_sem.at[slot], row, col
            )
        )
        copies[-1].start()
    total = x_ref[place.me]
    for slot, copy in enumerate(copies):
        copy.wait_recv()
        total = total + parts[slot]
    out_ref[place.me] = total
    for copy in copies:
        copy.wait_send()


def plane_gather(place, mine, send_sem, recv_sem):
    copies = []
    for slot, (row, col, _) in enumerate(place.peers()):
        copies.append(remote(mine, mine, send_sem.at[slot], recv_sem.at[slot], row, col))
        copies[-1].start()
    return copies


class Spread:
    def __init__(self, place, source_ref, tiles, target_ref, send_sem, recv_sem):
        self.place, self.source, self.tiles, self.target = place, source_ref, tiles, target_ref
        self.send_sem, self.recv_sem = send_sem, recv_sem
        self.tile = target_ref.shape[0] // 2

    def refs(self, index, core):
        start = pl.multiple_of(core * self.tile, self.tile)
        local = self.tiles[index] // self.place.cols
        return (
            self.source.at[pl.ds(start, self.tile), pl.ds(local * self.tile, self.tile)],
            self.target.at[pl.ds(start, self.tile), pl.ds(index * self.tile, self.tile)],
        )

    def holder(self, index):
        return self.place.col == self.tiles[index] % self.place.cols

    def copies(self, index):
        source, target = self.refs(index, self.place.core)
        return [
            remote(
                source,
                target,
                self.send_sem.at[index, slot],
                self.recv_sem.at[index, self.place.core],
                row,
                col,
            )
            for slot, (row, col, _) in enumerate(self.place.peers())
        ]

    def send(self):
        for index in range(len(self.tiles)):
            @pl.when(self.holder(index))
            def _():
                for copy in self.copies(index):
                    copy.start()
                source, target = self.refs(index, self.place.core)
                target[...] = source[...]

    def wait(self):
        for index in range(len(self.tiles)):
            for core in range(2):
                source, target = self.refs(index, core)

                @pl.when(jnp.logical_not(self.holder(index) & (self.place.core == core)))
                def _():
                    remote(
                        source,
                        target,
                        self.send_sem.at[index, 0],
                        self.recv_sem.at[index, core],
                        self.place.other,
                        self.place.col,
                    ).wait_recv()

    def finish(self):
        for index in range(len(self.tiles)):
            @pl.when(self.holder(index))
            def _():
                for copy in self.copies(index):
                    copy.wait_send()


class Chain:
    def __init__(self, place, source, x_ref, panel_ref, sems):
        self.place, self.source, self.x_ref, self.ref = place, source, x_ref, panel_ref
        self.load, self.sends, self.recv, self.share_send, self.share_recv = sems
        self.tile = x_ref.shape[-1]
        self.tiles = x_ref.shape[1]
        self.chunks = self.recv.shape[0]
        self.width = panel_ref.shape[1] // self.chunks
        self.at_source = place.plane == source

    def loads(self):
        start = pl.multiple_of(self.place.core * self.tile, self.tile)
        for tile in range(self.tiles):
            yield pltpu.make_async_copy(
                self.x_ref.at[pl.ds(0, self.tile), tile, 0, :],
                self.ref.at[pl.ds(start, self.tile), pl.ds(tile * self.tile, self.tile)],
                self.load.at[tile],
            )

    def part(self, chunk):
        start = pl.multiple_of(self.place.core * self.tile, self.tile)
        here = chunk * self.width
        if not isinstance(here, int):
            here = pl.multiple_of(here, self.width)
        return self.ref.at[pl.ds(start, self.tile), pl.ds(here, self.width)]

    def hop(self, chunk, step, sem):
        part = self.part(chunk)
        row = lax.rem(self.place.row + 2 * step + self.place.rows, self.place.rows)
        return remote(part, part, self.sends.at[sem, chunk], self.recv.at[chunk], row, self.place.col)

    def shared(self, chunk):
        part = self.part(chunk)
        return remote(
            part,
            part,
            self.share_send.at[chunk],
            self.share_recv.at[chunk],
            self.place.other,
            self.place.col,
        )

    def start(self):
        @pl.when(self.at_source)
        def _():
            for copy in self.loads():
                copy.start()

    def share(self):
        @pl.when(self.at_source)
        def _():
            for copy in self.loads():
                copy.wait()
            for chunk in range(self.chunks):
                self.shared(chunk).start()

    def spread(self, first, last):
        @pl.when(self.at_source)
        def _():
            for chunk in range(first, min(last, self.chunks)):
                if self.source < self.place.planes - 1:
                    self.hop(chunk, 1, 0).start()
                if self.source > 0:
                    self.hop(chunk, -1, 1).start()

    def step(self, chunk):
        place = self.place
        for step, sem, away, more in (
            (1, 0, place.plane > self.source, place.plane < place.planes - 1),
            (-1, 1, place.plane < self.source, place.plane > 0),
        ):
            if step < 0 and self.source == 0 or step > 0 and self.source == place.planes - 1:
                continue

            @pl.when(away)
            def _():
                self.hop(chunk, step, sem).wait_recv()

                @pl.when(more)
                def _():
                    self.hop(chunk, step, sem).start()

                self.shared(chunk).start()

    def join(self):
        for chunk in range(self.chunks):
            self.shared(chunk).wait_recv()

    def late_step(self, chunk):
        index = chunk - jnp.where(jnp.abs(self.place.plane - self.source) > 1, 1, 0)

        @pl.when((index >= 0) & (index < self.chunks))
        def _():
            self.step(index)

    def finish(self, joined=False):
        place = self.place
        if joined:
            @pl.when(jnp.logical_not(self.at_source))
            def _():
                self.join()
        else:
            self.join()
        for chunk in range(self.chunks):
            self.shared(chunk).wait_send()
        for step, sem, sent in (
            (1, 0, (place.plane >= self.source) & (place.plane < place.planes - 1)),
            (-1, 1, (place.plane <= self.source) & (place.plane > 0)),
        ):

            @pl.when(sent)
            def _():
                for chunk in range(self.chunks):
                    self.hop(chunk, step, sem).wait_send()

    @staticmethod
    def semaphores(tiles, chunks):
        dma = pltpu.SemaphoreType.DMA
        return [dma((tiles,)), dma((2, chunks)), dma((chunks,)), dma((chunks,)), dma((chunks,))]


CHUNK = 256


def later_steps(chain, first, every, late=False):
    count = [0]

    def hook():
        count[0] += 1
        chunk = first + count[0] // every - 1
        if count[0] % every == 0 and first <= chunk < chain.chunks + late:
            if late:
                chain.late_step(chunk)
            else:
                chain.step(chunk)

    return hook


EARLY = 3
PARTS = 4


def first_kernel(rows, cols, x_ref, inverse_ref, shifted_ref, sign_ref, rows_ref, cols_ref, *refs):
    stack, parts, gram_ref, top_ref = refs[:4]
    send_one, recv_one, line_send, line_recv, send_two, recv_two = refs[4:10]
    load, send_row, recv_row, top_send, top_recv = refs[10:15]
    place = Place(rows, cols)
    tile, tiles = x_ref.shape[-1], x_ref.shape[1]
    panel_tiles = BAND // tile
    held = PANELS * panel_tiles
    chain = Chain(place, 0, x_ref, cols_ref, refs[15:])
    spread = Spread(
        place, cols_ref, tuple(range(panel_tiles, 2 * panel_tiles)), top_ref, top_send, top_recv
    )
    first = place.plane == 0

    share = rows_ref.shape[1] // PARTS

    def spot(col, index):
        start = pl.multiple_of(lax.rem(col, panel_tiles) * tile, tile)
        return rows_ref.at[col // panel_tiles, pl.ds(index * share, share), pl.ds(start, tile)]

    has = place.col < held
    holder = lax.rem(place.col, held)
    begin = pl.multiple_of(lax.rem(holder, panel_tiles) * tile, tile)
    fill = pltpu.make_async_copy(
        x_ref.at[:, 0, 0, :], rows_ref.at[holder // panel_tiles, :, pl.ds(begin, tile)], load.at[0]
    )

    @pl.when(has)
    def _():
        fill.start()

    chain.start()
    place.greet()
    def row_copies(first, last):
        return [
            remote(
                spot(holder, index),
                spot(holder, index),
                send_row.at[index, step - 1],
                recv_row.at[index, holder],
                place.row,
                lax.rem(place.col + step, cols),
            )
            for index in range(first, last)
            for step in range(1, cols)
        ]

    line = [
        remote(
            gram_ref.at[place.me],
            gram_ref.at[place.me],
            line_send.at[step - 1],
            line_recv.at[0],
            lax.rem(place.row + 2 * step, rows),
            place.col,
        )
        for step in range(1, place.planes)
    ]
    chain.share()
    chain.spread(0, EARLY)

    @pl.when(has)
    def _():
        fill.wait()
        for copy in row_copies(0, 1):
            copy.start()

        @pl.when(place.plane > 0)
        def _():
            for copy in row_copies(1, 2):
                copy.start()

    @pl.when(first)
    def _():
        chain.join()
        width = tile * tiles // 2
        offset = place.core * width
        lanes = lax.broadcasted_iota(jnp.int32, (cols_ref.shape[0], width), 1) + offset
        limit = jnp.where(place.col < panel_tiles, tile, 0)
        value = cols_ref[:, pl.ds(pl.multiple_of(offset, tile), width)]
        value = jnp.where(lanes >= limit, value, 0.0)
        gram = mm(value, value, 1, 1)
        size = stack.shape[1]
        for piece in range(stack.shape[0]):
            stack[piece] = gram[piece * size : (piece + 1) * size]
        plane_scatter(place, place.peers(), stack, parts, gram_ref, send_one, recv_one)
        for copy in line:
            copy.start()

    chain.spread(EARLY, chain.chunks)

    for chunk in range(EARLY):
        @pl.when(place.plane <= EARLY - chunk)
        def _():
            chain.step(chunk)

    @pl.when(place.plane > 0)
    def _():
        line[0].wait_recv()

    gathers = plane_gather(place, gram_ref.at[place.me], send_two, recv_two)
    for chunk in range(EARLY):
        @pl.when(place.plane > EARLY - chunk)
        def _():
            chain.step(chunk)

    spread.send()

    @pl.when(has)
    def _():
        @pl.when(first)
        def _():
            for copy in row_copies(1, 2):
                copy.start()

        for copy in row_copies(2, PARTS):
            copy.start()

    for copy in gathers:
        copy.wait()

    def top():
        spread.wait()
        return top_ref[...]

    size = inverse_ref.shape[0]
    orthogonal_top(
        gram_ref[...].reshape(size, size), top, 0, inverse_ref, shifted_ref, sign_ref,
        later_steps(chain, EARLY, 2),
    )

    @pl.when(first)
    def _():
        for copy in line:
            copy.wait_send()

    spread.finish()

    @pl.when(has)
    def _():
        for copy in row_copies(0, PARTS):
            copy.wait_send()

    for col in range(held):
        @pl.when(place.col != col)
        def _():
            for index in range(PARTS):
                remote(
                    spot(col, index), spot(col, index), send_row.at[index, 0],
                    recv_row.at[index, col], place.row, place.col,
                ).wait_recv()

    chain.finish(True)


def first_panel(x4, collective_id):
    rows, cols = lax.axis_size("row"), lax.axis_size("col")
    row_count, tiles, _, tile = x4.shape
    width = tiles * tile
    count = 2 * cols
    pieces = (count, BAND // count, BAND)
    vmem = pl.BlockSpec(memory_space=pltpu.VMEM)
    dma = pltpu.SemaphoreType.DMA
    panel_tiles = BAND // tile
    square = jax.ShapeDtypeStruct((BAND, BAND), x4.dtype)
    return pl.pallas_call(
        functools.partial(first_kernel, rows, cols),
        out_shape=(
            square,
            square,
            jax.ShapeDtypeStruct((1, BAND), x4.dtype),
            jax.ShapeDtypeStruct((PANELS, row_count, BAND), x4.dtype),
            jax.ShapeDtypeStruct((BAND, width), x4.dtype),
        ),
        in_specs=[pl.BlockSpec(memory_space=pltpu.HBM)],
        out_specs=(vmem,) * 5,
        scratch_shapes=[
            pltpu.VMEM(pieces, x4.dtype),
            pltpu.VMEM((count - 1,) + pieces[1:], x4.dtype),
            pltpu.VMEM(pieces, x4.dtype),
            pltpu.VMEM((BAND, BAND), x4.dtype),
            dma((count - 1,)),
            dma((count - 1,)),
            dma((rows // 2 - 1,)),
            dma((1,)),
            dma((count - 1,)),
            dma((count - 1,)),
            dma((1,)),
            dma((PARTS, cols - 1)),
            dma((PARTS, PANELS * panel_tiles)),
            dma((panel_tiles, count - 1)),
            dma((panel_tiles, 2)),
        ]
        + Chain.semaphores(tiles, width // CHUNK),
        compiler_params=pltpu.CompilerParams(
            collective_id=collective_id, has_side_effects=True, vmem_limit_bytes=56 * MIB
        ),
    )(x4)


def next_kernel(rows, cols, below, *refs):
    refs = list(refs)
    take = lambda count: [refs.pop(0) for _ in range(count)]
    (
        vec_rows, applied_rows, vec_cols, applied, transform_ref, inner_ref, applied_next,
        old_ref, later_ref, x_ref,
    ) = take(10)
    inverse_ref, shifted_ref, sign_ref, panel_ref, cols_ref = take(5)
    old_high, old_low, new_high, new_low, update_ref, ahead_ref = take(6)
    gram_in, gram_sum = take(2)
    near, near_sum, parts, gram_ref, top_ref = refs[:5]
    near_send, near_recv, line_send, line_recv, send_two, recv_two = refs[5:11]
    top_line_send, top_line_recv, top_send, top_recv = refs[11:15]
    place = Place(rows, cols)
    tile = x_ref.shape[-1]
    panel_tiles = BAND // tile
    number = 2 * panel_tiles
    chain = Chain(place, 1, x_ref, cols_ref, refs[15:])
    chain.start()
    place.greet()
    chain.share()
    chain.spread(0, EARLY + 2)
    half_full = 0.5 * mm(transform_ref[...], inner_ref[...], 1, 0)
    half = split(half_full)
    old = old_ref[...]
    ahead = applied_next[...] - mm(half_full, old, 0, 1)
    ahead_ref[...] = ahead
    chain.late_step(0)
    vec = vec_rows[...]
    vec_parts = split(vec)
    change = applied_rows[...] - mm3(vec_parts, half)
    panel = later_ref[1] - mm(vec, ahead, 1, 0) - mm(change, old, 1, 1)
    lines = lax.broadcasted_iota(jnp.int32, panel.shape, 0)
    above = (below + BAND) // tile
    limit = (above // rows + jnp.where(place.row < above % rows, 1, 0)) * tile
    panel = jnp.where(lines >= limit, panel, 0.0)
    panel_ref[...] = panel
    gram_sum[...] = mm(panel, panel, 0, 0)
    change_parts = split(change)
    for start, value in ((0, vec_parts), (BAND, change_parts)):
        old_high[:, start : start + BAND] = value[0]
        old_low[:, start : start + BAND] = value[1]
    size = BAND
    height = gram_in.shape[2]
    for col in range(cols):
        for core in range(2):
            start = (2 * col + core) * height
            gram_in[col, core] = gram_sum[start : start + height, :]
    chain.late_step(1)
    swap = remote(
        gram_in.at[place.col, 1 - place.core], near.at[0], near_send.at[0], near_recv.at[0],
        place.other, place.col,
    )
    swap.start()

    top_plane = number % rows // 2
    start = pl.multiple_of(place.core * tile, tile)
    local = number // rows * tile
    block = panel_ref.at[pl.ds(local, tile), :]
    target = top_ref.at[pl.ds(start, tile), :]
    at_top = place.plane == top_plane

    def top_line(step):
        return remote(
            block, target, top_line_send.at[step - 1], top_line_recv.at[0],
            lax.rem(place.row + 2 * step, rows), place.col,
        )

    top_near = remote(target, target, top_send.at[0], top_recv.at[0], place.other, place.col)
    top_first = remote(block, target, top_send.at[0], top_recv.at[0], place.other, place.col)

    swap.wait_recv()
    near_sum[0] = gram_in[place.col, place.core] + near[0]
    line = [
        remote(
            near_sum.at[0], parts.at[step - 1], line_send.at[step - 1], line_recv.at[step - 1],
            lax.rem(place.row + 2 * step, rows), place.col,
        )
        for step in range(1, place.planes)
    ]
    for copy in line:
        copy.start()

    @pl.when(at_top)
    def _():
        for step in range(1, place.planes):
            top_line(step).start()
        top_first.start()
        target[...] = block[...]

    chain.spread(EARLY + 2, chain.chunks)
    chain.late_step(2)
    group = 5 if x_ref.shape[1] % 10 == 0 else 1
    wide = x_ref.shape[1] // group * tile
    half_t = split(half_full.T)

    def own_cols(index, carry):
        here = pl.ds(pl.multiple_of(index * wide, wide), wide)
        vec = split(vec_cols[:, here])
        change = applied[:, here] - mm3(half_t, vec)
        update_ref[:, here] = change
        for start, value in ((0, split(change)), (size, vec)):
            new_high[start : start + size, here] = value[0]
            new_low[start : start + size, here] = value[1]
        return carry

    lax.fori_loop(0, group, own_cols, 0)
    chain.late_step(3)
    total = near_sum[0]
    for slot, copy in enumerate(line):
        copy.wait_recv()
        total = total + parts[slot]
    piece = 2 * place.col + place.core
    gram_ref[piece] = total
    gathers = plane_gather(place, gram_ref.at[piece], send_two, recv_two)

    @pl.when(jnp.logical_not(at_top))
    def _():
        top_line(1).wait_recv()
        top_near.start()

    for chunk in range(4, 6):
        chain.late_step(chunk)
    for copy in gathers:
        copy.wait()

    def top():
        top_near.wait_recv()
        return top_ref[...]

    orthogonal_top(
        gram_ref[...].reshape(size, size), top, 1, inverse_ref, shifted_ref, sign_ref,
        later_steps(chain, 6, 2, True),
    )
    swap.wait_send()
    for copy in line:
        copy.wait_send()
    top_near.wait_send()

    @pl.when(at_top)
    def _():
        for step in range(1, place.planes):
            top_line(step).wait_send()

    chain.finish()


def next_panel(operands, x4, below, collective_id):
    rows, cols = lax.axis_size("row"), lax.axis_size("col")
    row_count, tiles, _, tile = x4.shape
    width = tiles * tile
    count = 2 * cols
    piece = (BAND // count, BAND)
    planes = rows // 2
    vmem = pl.BlockSpec(memory_space=pltpu.VMEM)
    dma = pltpu.SemaphoreType.DMA
    f32, bf16 = jnp.float32, jnp.bfloat16
    shape = jax.ShapeDtypeStruct
    square = shape((BAND, BAND), f32)
    return pl.pallas_call(
        functools.partial(next_kernel, rows, cols, below),
        out_shape=(
            square,
            square,
            shape((1, BAND), f32),
            shape((row_count, BAND), f32),
            shape((BAND, width), f32),
            shape((row_count, 2 * BAND), bf16),
            shape((row_count, 2 * BAND), bf16),
            shape((2 * BAND, width), bf16),
            shape((2 * BAND, width), bf16),
            shape((BAND, width), f32),
            square,
        ),
        in_specs=[vmem] * len(operands) + [pl.BlockSpec(memory_space=pltpu.HBM)],
        out_specs=(vmem,) * 11,
        scratch_shapes=[
            pltpu.VMEM((cols, 2) + piece, f32),
            pltpu.VMEM((BAND, BAND), f32),
            pltpu.VMEM((1,) + piece, f32),
            pltpu.VMEM((1,) + piece, f32),
            pltpu.VMEM((planes - 1,) + piece, f32),
            pltpu.VMEM((count,) + piece, f32),
            pltpu.VMEM((BAND, BAND), f32),
            dma((1,)),
            dma((1,)),
            dma((planes - 1,)),
            dma((planes - 1,)),
            dma((count - 1,)),
            dma((count - 1,)),
            dma((planes - 1,)),
            dma((1,)),
            dma((1,)),
            dma((1,)),
        ]
        + Chain.semaphores(tiles, width // CHUNK),
        compiler_params=pltpu.CompilerParams(
            collective_id=collective_id, has_side_effects=True, vmem_limit_bytes=44 * MIB
        ),
    )(*operands, x4)


def split(value):
    high = value.astype(jnp.bfloat16)
    return high, (value - high.astype(jnp.float32)).astype(jnp.bfloat16)


def split_outside(value):
    high = lax.reduce_precision(value, 8, 7)
    return high.astype(jnp.bfloat16), (value - high).astype(jnp.bfloat16)


def dot(a, b):
    return jnp.dot(a, b, preferred_element_type=jnp.float32)


def apply_kernel(rows, cols, tiles, fixed, *refs):
    place = Place(rows, cols)
    refs = list(refs)
    take = lambda count: [refs.pop(0) for _ in range(count)]
    x_ref, left_ref, shifted_ref, sign_ref, vec_ref = take(5)
    old_high, old_low, new_high, new_low = take(4) if fixed else [None] * 4
    applied_row_ref, transform_ref, applied_ref, inner_ref = take(4)
    next_ref = take(1)[0] if tiles else None
    kept_ref = take(1)[0] if fixed else None
    block, part, near, pair, left_in, right_in, left_out, right_out, out_ref, row_ref = take(10)
    total_ref, stack, parts = take(3)
    (
        load, near_send, near_recv, left_send, left_recv, right_send, right_recv,
        both_send, both_recv, row_send, row_recv, send_one, recv_one, send_two, recv_two,
    ) = take(15)
    next_sems = take(2) if tiles else None
    store = take(1)[0] if fixed else None
    plane, core, planes = place.plane, place.core, place.planes
    tile = x_ref.shape[-1]
    chunks = block.shape[0]
    pieces = pair.shape[0] // chunks
    depth = pair.shape[1]
    subs = chunks * pieces
    size = left_ref.shape[0] // 2

    def load_of(chunk, index):
        return pltpu.make_async_copy(
            x_ref.at[:, 2 * chunk + index, 0, :],
            block.at[chunk, :, pl.ds(index * tile, tile)],
            load.at[chunk, index],
        )

    def store_of(chunk, index):
        return pltpu.make_async_copy(
            block.at[chunk, :, pl.ds(index * tile, tile)],
            kept_ref.at[:, 2 * chunk + index, 0, :],
            store.at[chunk, index],
        )

    for chunk in range(chunks):
        for index in range(2):
            load_of(chunk, index).start()
    place.greet()

    def near_of(chunk):
        return remote(
            part.at[chunk, 1 - core],
            near.at[chunk],
            near_send.at[chunk],
            near_recv.at[chunk],
            place.other,
            place.col,
        )

    def rightward(source, index):
        return remote(
            source.at[index], left_in.at[index], right_send.at[index], left_recv.at[index],
            lax.rem(place.row + 2, rows), place.col,
        )

    def leftward(source, index):
        return remote(
            source.at[index], right_in.at[index], left_send.at[index], right_recv.at[index],
            lax.rem(place.row + rows - 2, rows), place.col,
        )

    def joined(chunk):
        near_of(chunk).wait_recv()
        for piece in range(pieces):
            pair[chunk * pieces + piece] = part[chunk, core, piece] + near[chunk, piece]

        @pl.when(plane == 0)
        def _():
            for piece in range(pieces):
                rightward(pair, chunk * pieces + piece).start()

        @pl.when(plane == planes - 1)
        def _():
            for piece in range(pieces):
                leftward(pair, chunk * pieces + piece).start()

    def product(chunk, carry):
        for index in range(2):
            load_of(chunk, index).wait()
        if fixed:
            here = pl.ds(pl.multiple_of(chunk * 2 * tile, 2 * tile), 2 * tile)
            change = dot(old_high[...], new_high[:, here]) + (
                dot(old_low[...], new_high[:, here]) + dot(old_high[...], new_low[:, here])
            )
            block[chunk] = block[chunk] - change
            for index in range(2):
                store_of(chunk, index).start()
        high, low = split(block[chunk])
        value = dot(left_ref[...], high)
        value = value[:size] + (value[size:] + dot(left_ref[:size], low))
        for index in range(2):
            for piece in range(pieces):
                part[chunk, index, piece] = value[
                    piece * depth : (piece + 1) * depth, index * tile : (index + 1) * tile
                ]
        near_of(chunk).start()

        @pl.when(chunk > 0)
        def _():
            joined(chunk - 1)

        for piece in range(pieces):
            chain((chunk - BEHIND) * pieces + piece, 0)
        return carry

    left_lag = HOP * jnp.maximum(plane - 1, 0)
    right_lag = HOP * jnp.maximum(planes - 2 - plane, 0)
    last_lag = jnp.maximum(left_lag, right_lag)
    held = cols * core + place.col
    source = held // 2 == plane
    target_row = 2 * plane + lax.rem(place.col, 2)
    to_self = target_row == place.row
    square = cols == 4
    beside = place.col + 1 - 2 * lax.rem(place.col, 2)
    across = lax.rem(place.col + 2, 4)
    targets = (place.col, beside, across) if square else tuple(
        lax.rem(place.col + step, cols) for step in range(cols)
    )
    relays = (lax.rem(place.row, cols) == across) if square else None

    def depths(index):
        return pl.ds(pl.multiple_of(lax.rem(index, pieces) * depth, depth), depth)

    def lanes(index):
        return pl.ds(pl.multiple_of((2 * (index // pieces) + core) * tile, tile), tile)

    def row_lanes(index):
        return pl.ds(pl.multiple_of(index // pieces * tile, tile), tile)

    def both_of(index):
        spot = out_ref.at[depths(index), lanes(index)]
        return remote(spot, spot, both_send.at[index], both_recv.at[index], place.other, place.col)

    def row_of(index, step):
        return remote(
            out_ref.at[depths(index), lanes(index)],
            row_ref.at[depths(index), row_lanes(index)],
            row_send.at[index, step],
            row_recv.at[index],
            target_row,
            targets[step],
        )

    def relay_of(index):
        spot = row_ref.at[depths(index), row_lanes(index)]
        return remote(spot, spot, row_send.at[index, 3], row_recv.at[index], place.row, beside)

    def relay(index):
        @pl.when(relays & (index >= 0) & (index < subs))
        def _():
            relay_of(index).wait_recv()
            relay_of(index).start()

    def chain(step, carry):
        index = step - left_lag

        @pl.when((plane > 0) & (index >= 0) & (index < subs))
        def _():
            rightward(pair, index).wait_recv()

            @pl.when(plane < planes - 1)
            def _():
                right_out[index] = left_in[index] + pair[index]
                rightward(right_out, index).start()

        other = step - right_lag

        @pl.when((plane < planes - 1) & (other >= 0) & (other < subs))
        def _():
            leftward(pair, other).wait_recv()

            @pl.when(plane > 0)
            def _():
                left_out[other] = right_in[other] + pair[other]
                leftward(left_out, other).start()

        done = step - last_lag

        @pl.when((done >= 0) & (done < subs))
        def _():
            @pl.when(plane == 0)
            def _():
                out_ref[depths(done), lanes(done)] = pair[done] + right_in[done]

            @pl.when(plane == planes - 1)
            def _():
                out_ref[depths(done), lanes(done)] = left_in[done] + pair[done]

            @pl.when((plane > 0) & (plane < planes - 1))
            def _():
                out_ref[depths(done), lanes(done)] = right_out[done] + right_in[done]

            both_of(done).start()

            @pl.when(source)
            def _():
                for step in range(1, len(targets)):
                    row_of(done, step).start()

                @pl.when(to_self)
                def _():
                    row_ref[depths(done), row_lanes(done)] = out_ref[depths(done), lanes(done)]

                @pl.when(jnp.logical_not(to_self))
                def _():
                    row_of(done, 0).start()

        if square:
            relay(done - HOP)
        return carry

    lax.fori_loop(0, chunks, product, 0)
    joined(chunks - 1)
    steps = subs + HOP * (planes - 2 + square)
    count = [0, max(chunks - BEHIND, 0) * pieces]

    def hook():
        count[0] += 1
        if count[0] % 2 == 0 and count[1] < steps:
            chain(count[1], 0)
            count[1] += 1

    transform_ref[...] = block_transform(shifted_ref[...], sign_ref[...], hook)
    if count[1] < steps:
        lax.fori_loop(count[1], steps, chain, 0)
    total_ref[...] = jnp.zeros_like(total_ref)
    transform = split(transform_ref[...])

    def finished(number, carry):
        for index in range(2 * pieces):
            both_of(2 * pieces * number + index).wait_recv()
        here = pl.ds(pl.multiple_of(number * 4 * tile, 4 * tile), 4 * tile)
        applied = mm3(transform, split(out_ref[:, here]))
        applied_ref[:, here] = applied
        total_ref[...] += mm3(split(vec_ref[:, here]), split(applied), 1, 1)
        return carry

    def finished_one(number, carry):
        for index in range(pieces):
            both_of(pieces * number + index).wait_recv()
        here = pl.ds(pl.multiple_of(number * 2 * tile, 2 * tile), 2 * tile)
        applied = mm3(transform, split(out_ref[:, here]))
        applied_ref[:, here] = applied
        total_ref[...] += mm3(split(vec_ref[:, here]), split(applied), 1, 1)
        return carry

    if chunks % 2 == 0:
        lax.fori_loop(0, chunks // 2, finished, 0)
    else:
        lax.fori_loop(0, chunks, finished_one, 0)
    height = stack.shape[1]
    for piece in range(stack.shape[0]):
        stack[piece] = total_ref[piece * height : (piece + 1) * height, :]
    if tiles:
        spread = Spread(place, applied_ref, tiles, next_ref, *next_sems)
        spread.send()
    plane_scatter(place, place.peers()[: cols - 1], stack, parts, inner_ref, send_one, recv_one)
    gathers = plane_gather(place, inner_ref.at[place.me], send_two, recv_two)
    gets = jnp.logical_not(source & to_self)
    if square:
        gets = gets & jnp.logical_not(relays)

    def drain(index, carry):
        both_of(index).wait_send()

        @pl.when(plane < planes - 1)
        def _():
            rightward(pair, index).wait_send()

        @pl.when(plane > 0)
        def _():
            leftward(pair, index).wait_send()

        @pl.when(source)
        def _():
            for step in range(1, len(targets)):
                row_of(index, step).wait_send()

            @pl.when(jnp.logical_not(to_self))
            def _():
                row_of(index, 0).wait_send()

        @pl.when(gets)
        def _():
            row_of(index, 0).wait_recv()

        if square:
            @pl.when(relays)
            def _():
                relay_of(index).wait_send()

        return carry

    def drain_chunk(chunk, carry):
        if fixed:
            for index in range(2):
                store_of(chunk, index).wait()
        near_of(chunk).wait_send()
        return carry

    lax.fori_loop(0, subs, drain, 0)
    lax.fori_loop(0, chunks, drain_chunk, 0)
    applied_row_ref[...] = mm3(split(row_ref[...].T), split(transform_ref[...]), 1, 1)
    for copy in gathers:
        copy.wait()
    if tiles:
        spread.wait()
        spread.finish()


PIECES = 2
HOP = 3
BEHIND = 3


def apply(x4, left, shifted, signs, vec_cols, tiles, more, collective_id):
    rows, cols = lax.axis_size("row"), lax.axis_size("col")
    row_count, held_tiles, _, tile = x4.shape
    width = held_tiles * tile
    chunks = held_tiles // 2
    count = 2 * cols
    vmem = pl.BlockSpec(memory_space=pltpu.VMEM)
    hbm = pl.BlockSpec(memory_space=pltpu.HBM)
    dma = pltpu.SemaphoreType.DMA
    f32 = jnp.float32
    piece = (BAND // PIECES, tile)
    subs = PIECES * chunks
    sums = (count, BAND // count, BAND)
    kept = bool(more)
    square = jax.ShapeDtypeStruct((BAND, BAND), f32)
    wide = jax.ShapeDtypeStruct((BAND, width), f32)
    shapes = (
        jax.ShapeDtypeStruct((row_count, BAND), f32),
        square,
        wide,
        jax.ShapeDtypeStruct(sums, f32),
    )
    shapes += (square,) if tiles else ()
    out = pl.pallas_call(
        functools.partial(apply_kernel, rows, cols, tiles, kept),
        out_shape=shapes + ((jax.ShapeDtypeStruct(x4.shape, x4.dtype),) if kept else ()),
        in_specs=[hbm] + [vmem] * (4 + len(more)),
        out_specs=(vmem,) * len(shapes) + ((hbm,) if kept else ()),
        scratch_shapes=[
            pltpu.VMEM((chunks, row_count, 2 * tile), f32),
            pltpu.VMEM((chunks, 2, PIECES) + piece, f32),
            pltpu.VMEM((chunks, PIECES) + piece, f32),
        ]
        + [pltpu.VMEM((subs,) + piece, f32)] * 5
        + [
            pltpu.VMEM((BAND, width), f32),
            pltpu.VMEM((BAND, row_count), f32),
            pltpu.VMEM((BAND, BAND), f32),
            pltpu.VMEM(sums, f32),
            pltpu.VMEM((cols - 1,) + sums[1:], f32),
        ]
        + [dma((chunks, 2)), dma((chunks,)), dma((chunks,))]
        + [dma((subs,))] * 6
        + [dma((subs, cols)), dma((subs,))]
        + [dma((cols - 1,))] * 2
        + [dma((count - 1,))] * 2
        + ([dma((len(tiles), count - 1)), dma((len(tiles), 2))] if tiles else [])
        + ([dma((chunks, 2))] if kept else []),
        compiler_params=pltpu.CompilerParams(
            collective_id=collective_id, has_side_effects=True, vmem_limit_bytes=(60 if kept else 48) * MIB
        ),
    )(x4, left, shifted, signs, vec_cols, *more)
    out = list(out)
    out[3] = out[3].reshape(BAND, BAND)
    return out


def update_kernel(x_ref, left_high, left_low, right_high, right_low, out_ref, block, result, load, store):
    tile = x_ref.shape[-1]
    chunks = x_ref.shape[1] // 2

    def load_of(chunk, index):
        return pltpu.make_async_copy(
            x_ref.at[:, 2 * chunk + index, 0, :],
            block.at[lax.rem(chunk, 2), :, pl.ds(index * tile, tile)],
            load.at[lax.rem(chunk, 2), index],
        )

    def store_of(chunk, index):
        return pltpu.make_async_copy(
            result.at[lax.rem(chunk, 2), :, pl.ds(index * tile, tile)],
            out_ref.at[:, 2 * chunk + index, 0, :],
            store.at[lax.rem(chunk, 2), index],
        )

    for chunk in range(2):
        for index in range(2):
            load_of(chunk, index).start()

    def body(chunk, carry):
        slot = lax.rem(chunk, 2)
        for index in range(2):
            load_of(chunk, index).wait()

        @pl.when(chunk >= 2)
        def _():
            for index in range(2):
                store_of(chunk - 2, index).wait()

        here = pl.ds(pl.multiple_of(chunk * 2 * tile, 2 * tile), 2 * tile)
        value = dot(left_high[...], right_high[:, here]) + (
            dot(left_low[...], right_high[:, here]) + dot(left_high[...], right_low[:, here])
        )
        result[slot] = block[slot] - value
        for index in range(2):
            store_of(chunk, index).start()

        @pl.when(chunk + 2 < chunks)
        def _():
            for index in range(2):
                load_of(chunk + 2, index).start()

        return carry

    lax.fori_loop(0, chunks, body, 0)
    for chunk in range(chunks - 2, chunks):
        for index in range(2):
            store_of(chunk, index).wait()


def update(x4, left, right):
    row_count, tiles, _, tile = x4.shape
    vmem = pl.BlockSpec(memory_space=pltpu.VMEM)
    hbm = pl.BlockSpec(memory_space=pltpu.HBM)
    dma = pltpu.SemaphoreType.DMA
    return pl.pallas_call(
        update_kernel,
        out_shape=jax.ShapeDtypeStruct(x4.shape, x4.dtype),
        in_specs=[hbm] + [vmem] * 4,
        out_specs=hbm,
        scratch_shapes=[pltpu.VMEM((2, row_count, 2 * tile), jnp.float32)] * 2
        + [dma((2, 2)), dma((2, 2))],
        compiler_params=pltpu.CompilerParams(vmem_limit_bytes=48 * MIB),
    )(x4, *left, *right)


def on_device(matrix_tiles):
    tile_shape = matrix_tiles.shape
    block_rows, _, tile_size, block_cols = tile_shape[:4]
    row_count = block_rows * tile_size
    col_count = block_cols * tile_size
    row_devices = lax.axis_size("row")
    col_devices = lax.axis_size("col")
    row_index = lax.axis_index("row")
    panel_tiles = BAND // tile_size
    assert row_devices == 2 * col_devices and PANELS * panel_tiles <= col_devices
    x4 = matrix_tiles.reshape(row_count, block_cols, 1, tile_size)

    def positions(count, devices, index):
        place = jnp.arange(count, dtype=jnp.int32)
        return (place // tile_size * devices + index) * tile_size + place % tile_size

    global_rows = positions(row_count, row_devices, row_index)
    global_cols = positions(col_count, lax.axis_size("col"), lax.axis_index("col"))
    band = jnp.arange(BAND, dtype=jnp.int32)
    inverse, shifted, signs, rows_held, panel_cols = first_panel(x4, 0)
    panel_rows = rows_held[0]
    kept, more = x4, ()
    for panel_index in range(PANELS):
        below = (panel_index + 1) * BAND
        last = panel_index == PANELS - 1
        panel_rows = jnp.where((global_rows >= below)[:, None], panel_rows, 0.0)
        unit_rows = (global_rows[:, None] - below == band[None, :]).astype(jnp.float32)
        unit_rows_t = (band[:, None] == global_rows[None, :] - below).astype(jnp.float32)
        vec_rows = multiply(panel_rows, inverse, 1, 1) - unit_rows * signs
        vec_rows_t = multiply(inverse, panel_rows, 1, 1) - unit_rows_t * signs.reshape(BAND, 1)
        panel_cols = jnp.where((global_cols >= below)[None, :], panel_cols, 0.0)
        unit_cols = (band[:, None] == global_cols[None, :] - below).astype(jnp.float32)
        vec_cols = multiply(inverse, panel_cols) - unit_cols * signs.reshape(BAND, 1)
        first = below // tile_size
        applied_rows, transform, applied, inner, *rest = apply(
            kept,
            jnp.concatenate(split_outside(vec_rows_t), 0),
            shifted,
            signs,
            vec_cols,
            () if last else tuple(range(first, first + panel_tiles)),
            more,
            1 + panel_index,
        )
        if last:
            break
        old_shifted, old_cols = shifted, vec_cols
        (
            inverse, shifted, signs, panel_rows, panel_cols,
            old_high, old_low, new_high, new_low, update_cols, update_next,
        ) = next_panel(
            (
                vec_rows, applied_rows, vec_cols, applied, transform, inner, rest[0], shifted,
                rows_held,
            ),
            x4,
            below,
            3,
        )
        more = (old_high, old_low, new_high, new_low)
        panel_cols = (
            panel_cols - multiply(update_next, old_cols, 0, 0) - multiply(old_shifted, update_cols)
        )
    half_inner = 0.5 * multiply(transform, inner)
    update_rows = applied_rows - multiply(vec_rows, half_inner)
    update_cols = applied - multiply(half_inner, vec_cols, 0, 0)
    left = split_outside(jnp.concatenate([vec_rows, update_rows], 1))
    right = split_outside(jnp.concatenate([update_cols, vec_cols], 0))
    return update(rest[0], left, right).reshape(tile_shape)


def solution(mesh):
    return jax.shard_map(
        on_device,
        mesh=mesh,
        in_specs=(P(None, "row", None, None, "col", None),),
        out_specs=P(None, "row", None, None, "col", None),
        check_vma=False,
    )
```

```python
import functools

import jax
import jax.numpy as jnp
from jax import lax
from jax.experimental import pallas as pl
from jax.experimental.pallas import tpu as pltpu
from jax.sharding import PartitionSpec as P

BAND = 256
PANELS = 2
MIB = 1024 * 1024
MESH = pl.DeviceIdType.MESH

HI = lax.Precision.HIGHEST
def mm(a, b, ca, cb):
    return lax.dot_general(a, b, (((ca,), (cb,)), ((), ())), precision=HI, preferred_element_type=jnp.float32)

def base_inverse(block, hook):
    size = block.shape[0]
    wide = (8, 2 * size)
    group = 8
    places = lax.broadcasted_iota(jnp.int32, wide, 0)
    cols = lax.broadcasted_iota(jnp.int32, wide, 1)
    work = []
    for k in range(size // 8):
        unit = jnp.where(places + 8 * k == cols, 1.0, 0.0)[:, :size]
        work.append(jnp.concatenate([block[8 * k : 8 * k + 8], unit], 1))
    for start in range(0, size, group):
        own, offset = divmod(start, 8)
        rows = [jnp.broadcast_to(work[own][offset + i : offset + i + 1], wide) for i in range(group)]
        pivot = [
            [jnp.broadcast_to(rows[i][:, start + j : start + j + 1], wide) for j in range(group)]
            for i in range(group)
        ]
        first = own if offset + group < 8 else own + 1
        columns = [
            [jnp.broadcast_to(work[k][:, start + i : start + i + 1], wide) for i in range(group)]
            for k in range(first, len(work))
        ]
        scaled = []
        for i in range(group):
            inverse = 1.0 / pivot[i][i]
            scaled.append(rows[i] * inverse)
            for j in range(i + 1, group):
                ratio = pivot[i][j] * inverse
                for l in range(j, group):
                    pivot[j][l] = pivot[j][l] - ratio * pivot[i][l]
                rows[j] = rows[j] - ratio * rows[i]
                for column in columns:
                    column[j] = column[j] - ratio * column[i]
        for k, column in zip(range(first, len(work)), columns):
            change = column[0] * scaled[0]
            for i in range(1, group):
                change = change + column[i] * scaled[i]
            if k == own:
                change = jnp.where(places >= offset + group, change, 0.0)
            work[k] = work[k] - change
        for i in range(group):
            work[own] = jnp.where(places == offset + i, rows[i], work[own])
        hook()
    result = []
    for k, value in enumerate(work):
        pivots = jnp.sum(jnp.where(places + 8 * k == cols, value, 0.0), axis=1, keepdims=True)
        result.append(value[:, size:] * (1.0 / jnp.sqrt(pivots)))
    return jnp.concatenate(result, 0)


def factor_inverse(matrix, base, hook):
    size = matrix.shape[0]
    if size <= base:
        return base_inverse(matrix, hook)
    half = size // 2
    first = factor_inverse(matrix[:half, :half], base, hook)
    lower = mm(matrix[half:, :half], first, 1, 1)
    second = factor_inverse(matrix[half:, half:] - mm(lower, lower, 1, 1), base, hook)
    corner = -mm(second, mm(lower, first, 1, 0), 1, 0)
    top = jnp.concatenate([first, jnp.zeros_like(first)], 1)
    return jnp.concatenate([top, jnp.concatenate([corner, second], 1)], 0)

def orthogonal_top(gram, top, top_dim, inverse_ref, shifted_ref, sign_ref, hook):
    size = gram.shape[0]
    inverse = factor_inverse(gram, 64, hook)
    inverse_ref[...] = inverse
    basis = mm(top(), inverse, top_dim, 1)
    rows = lax.broadcasted_iota(jnp.int32, (size, size), 0)
    cols = lax.broadcasted_iota(jnp.int32, (size, size), 1)
    sign_square = jnp.where(rows == cols, jnp.where(basis >= 0, -1.0, 1.0), 0.0)
    shifted_ref[...] = basis - sign_square
    sign_ref[...] = jnp.sum(sign_square, axis=0, keepdims=True)


def block_transform(shifted, signs, hook):
    size = shifted.shape[0]
    outer = factor_inverse(mm(shifted, shifted, 0, 0), 64, hook)
    rows = lax.broadcasted_iota(jnp.int32, (size, size), 0)
    cols = lax.broadcasted_iota(jnp.int32, (size, size), 1)
    sign_column = jnp.sum(jnp.where(rows == cols, signs, 0.0), axis=1, keepdims=True)
    parts = split(outer)
    return -mm3(parts, split(mm3(parts, split(shifted * sign_column), 1, 1)), 0, 0)


def mm3(a, b, ca=1, cb=0):
    def part(x, y):
        return lax.dot_general(
            x, y, (((ca,), (cb,)), ((), ())), preferred_element_type=jnp.float32
        )

    return part(a[0], b[0]) + (part(a[0], b[1]) + part(a[1], b[0]))


def multiply(first, second, first_dim=1, second_dim=0, precision=HI):
    return lax.dot_general(
        first,
        second,
        (((first_dim,), (second_dim,)), ((), ())),
        precision=precision,
        preferred_element_type=jnp.float32,
    )


def remote(source, target, send_sem, recv_sem, row, col):
    return pltpu.make_async_remote_copy(
        src_ref=source,
        dst_ref=target,
        send_sem=send_sem,
        recv_sem=recv_sem,
        device_id={"row": row, "col": col},
        device_id_type=MESH,
    )


class Place:
    def __init__(self, rows, cols):
        self.rows, self.cols, self.planes = rows, cols, rows // 2
        row = lax.axis_index("row")
        self.col = lax.axis_index("col")
        self.plane = row // 2
        self.core = row % 2
        self.row = row
        self.other = 2 * self.plane + (1 - self.core)
        self.me = self.core * cols + self.col

    def peers(self):
        found = []
        for core_step in range(2):
            for col_step in range(self.cols):
                if core_step or col_step:
                    core = lax.rem(self.core + core_step, 2)
                    col = lax.rem(self.col + col_step, self.cols)
                    found.append((2 * self.plane + core, col, core * self.cols + col))
        return found

    def greet(self, line=True):
        barrier = pltpu.get_barrier_semaphore()
        count = 0
        for row, col, _ in self.peers():
            pl.semaphore_signal(
                barrier, inc=1, device_id={"row": row, "col": col}, device_id_type=MESH
            )
            count += 1
        for step in range(1, self.planes) if line else ():
            row = lax.rem(self.row + 2 * step, self.rows)
            pl.semaphore_signal(
                barrier, inc=1, device_id={"row": row, "col": self.col}, device_id_type=MESH
            )
            count += 1
        pl.semaphore_wait(barrier, count)


def plane_scatter(place, peers, x_ref, parts, out_ref, send_sem, recv_sem):
    copies = []
    for slot, (row, col, piece) in enumerate(peers):
        copies.append(
            remote(
                x_ref.at[piece], parts.at[slot], send_sem.at[slot], recv_sem.at[slot], row, col
            )
        )
        copies[-1].start()
    total = x_ref[place.me]
    for slot, copy in enumerate(copies):
        copy.wait_recv()
        total = total + parts[slot]
    out_ref[place.me] = total
    for copy in copies:
        copy.wait_send()


def plane_gather(place, mine, send_sem, recv_sem):
    copies = []
    for slot, (row, col, _) in enumerate(place.peers()):
        copies.append(remote(mine, mine, send_sem.at[slot], recv_sem.at[slot], row, col))
        copies[-1].start()
    return copies


class Spread:
    def __init__(self, place, source_ref, tiles, target_ref, send_sem, recv_sem):
        self.place, self.source, self.tiles, self.target = place, source_ref, tiles, target_ref
        self.send_sem, self.recv_sem = send_sem, recv_sem
        self.tile = target_ref.shape[0] // 2

    def refs(self, index, core):
        start = pl.multiple_of(core * self.tile, self.tile)
        local = self.tiles[index] // self.place.cols
        return (
            self.source.at[pl.ds(start, self.tile), pl.ds(local * self.tile, self.tile)],
            self.target.at[pl.ds(start, self.tile), pl.ds(index * self.tile, self.tile)],
        )

    def holder(self, index):
        return self.place.col == self.tiles[index] % self.place.cols

    def copies(self, index):
        source, target = self.refs(index, self.place.core)
        return [
            remote(
                source,
                target,
                self.send_sem.at[index, slot],
                self.recv_sem.at[index, self.place.core],
                row,
                col,
            )
            for slot, (row, col, _) in enumerate(self.place.peers())
        ]

    def send(self):
        for index in range(len(self.tiles)):
            @pl.when(self.holder(index))
            def _():
                for copy in self.copies(index):
                    copy.start()
                source, target = self.refs(index, self.place.core)
                target[...] = source[...]

    def wait(self):
        for index in range(len(self.tiles)):
            for core in range(2):
                source, target = self.refs(index, core)

                @pl.when(jnp.logical_not(self.holder(index) & (self.place.core == core)))
                def _():
                    remote(
                        source,
                        target,
                        self.send_sem.at[index, 0],
                        self.recv_sem.at[index, core],
                        self.place.other,
                        self.place.col,
                    ).wait_recv()

    def finish(self):
        for index in range(len(self.tiles)):
            @pl.when(self.holder(index))
            def _():
                for copy in self.copies(index):
                    copy.wait_send()


class Chain:
    def __init__(self, place, source, x_ref, panel_ref, sems):
        self.place, self.source, self.x_ref, self.ref = place, source, x_ref, panel_ref
        self.load, self.sends, self.recv, self.share_send, self.share_recv = sems
        self.tile = x_ref.shape[-1]
        self.tiles = x_ref.shape[1]
        self.chunks = self.recv.shape[0]
        self.width = panel_ref.shape[1] // self.chunks
        self.at_source = place.plane == source

    def loads(self):
        start = pl.multiple_of(self.place.core * self.tile, self.tile)
        for tile in range(self.tiles):
            yield pltpu.make_async_copy(
                self.x_ref.at[pl.ds(0, self.tile), tile, 0, :],
                self.ref.at[pl.ds(start, self.tile), pl.ds(tile * self.tile, self.tile)],
                self.load.at[tile],
            )

    def part(self, chunk):
        start = pl.multiple_of(self.place.core * self.tile, self.tile)
        here = chunk * self.width
        if not isinstance(here, int):
            here = pl.multiple_of(here, self.width)
        return self.ref.at[pl.ds(start, self.tile), pl.ds(here, self.width)]

    def hop(self, chunk, step, sem):
        part = self.part(chunk)
        row = lax.rem(self.place.row + 2 * step + self.place.rows, self.place.rows)
        return remote(part, part, self.sends.at[sem, chunk], self.recv.at[chunk], row, self.place.col)

    def shared(self, chunk):
        part = self.part(chunk)
        return remote(
            part,
            part,
            self.share_send.at[chunk],
            self.share_recv.at[chunk],
            self.place.other,
            self.place.col,
        )

    def start(self):
        @pl.when(self.at_source)
        def _():
            for copy in self.loads():
                copy.start()

    def share(self):
        @pl.when(self.at_source)
        def _():
            for copy in self.loads():
                copy.wait()
            for chunk in range(self.chunks):
                self.shared(chunk).start()

    def spread(self, first, last):
        @pl.when(self.at_source)
        def _():
            for chunk in range(first, min(last, self.chunks)):
                if self.source < self.place.planes - 1:
                    self.hop(chunk, 1, 0).start()
                if self.source > 0:
                    self.hop(chunk, -1, 1).start()

    def step(self, chunk):
        place = self.place
        for step, sem, away, more in (
            (1, 0, place.plane > self.source, place.plane < place.planes - 1),
            (-1, 1, place.plane < self.source, place.plane > 0),
        ):
            if step < 0 and self.source == 0 or step > 0 and self.source == place.planes - 1:
                continue

            @pl.when(away)
            def _():
                self.hop(chunk, step, sem).wait_recv()

                @pl.when(more)
                def _():
                    self.hop(chunk, step, sem).start()

                self.shared(chunk).start()

    def join(self):
        for chunk in range(self.chunks):
            self.shared(chunk).wait_recv()

    def ends(self):
        place = self.place
        last = (place.plane == 0) | (place.plane == place.planes - 1)
        return last & jnp.logical_not(self.at_source)

    def middle_step(self, chunk):
        @pl.when(jnp.logical_not(self.ends()))
        def _():
            self.step(chunk)

    def end_steps(self, first):
        @pl.when(self.ends())
        def _():
            for chunk in range(first, self.chunks):
                self.step(chunk)

    def late_step(self, chunk):
        index = chunk - jnp.where(jnp.abs(self.place.plane - self.source) > 1, 1, 0)

        @pl.when((index >= 0) & (index < self.chunks) & jnp.logical_not(self.ends()))
        def _():
            self.step(index)

    def finish(self, joined=False):
        place = self.place
        if joined:
            @pl.when(jnp.logical_not(self.at_source))
            def _():
                self.join()
        else:
            self.join()
        for chunk in range(self.chunks):
            self.shared(chunk).wait_send()
        for step, sem, sent in (
            (1, 0, (place.plane >= self.source) & (place.plane < place.planes - 1)),
            (-1, 1, (place.plane <= self.source) & (place.plane > 0)),
        ):

            @pl.when(sent)
            def _():
                for chunk in range(self.chunks):
                    self.hop(chunk, step, sem).wait_send()

    @staticmethod
    def semaphores(tiles, chunks):
        dma = pltpu.SemaphoreType.DMA
        return [dma((tiles,)), dma((2, chunks)), dma((chunks,)), dma((chunks,)), dma((chunks,))]


CHUNK = 256


def later_steps(chain, first, every, late=False):
    count = [0]

    def hook():
        count[0] += 1
        chunk = first + count[0] // every - 1
        if count[0] % every == 0 and first <= chunk < chain.chunks + late:
            if late:
                chain.late_step(chunk)
            else:
                chain.middle_step(chunk)

    return hook


EARLY = 3
PARTS = 4


def first_kernel(rows, cols, x_ref, inverse_ref, shifted_ref, sign_ref, rows_ref, cols_ref, *refs):
    stack, parts, gram_ref, top_ref = refs[:4]
    send_one, recv_one, line_send, line_recv, send_two, recv_two = refs[4:10]
    load, send_row, recv_row, top_send, top_recv = refs[10:15]
    place = Place(rows, cols)
    tile, tiles = x_ref.shape[-1], x_ref.shape[1]
    panel_tiles = BAND // tile
    held = PANELS * panel_tiles
    chain = Chain(place, 0, x_ref, cols_ref, refs[15:])
    spread = Spread(
        place, cols_ref, tuple(range(panel_tiles, 2 * panel_tiles)), top_ref, top_send, top_recv
    )
    first = place.plane == 0

    share = rows_ref.shape[1] // PARTS

    def spot(col, index):
        start = pl.multiple_of(lax.rem(col, panel_tiles) * tile, tile)
        return rows_ref.at[col // panel_tiles, pl.ds(index * share, share), pl.ds(start, tile)]

    has = place.col < held
    holder = lax.rem(place.col, held)
    begin = pl.multiple_of(lax.rem(holder, panel_tiles) * tile, tile)
    fill = pltpu.make_async_copy(
        x_ref.at[:, 0, 0, :], rows_ref.at[holder // panel_tiles, :, pl.ds(begin, tile)], load.at[0]
    )

    @pl.when(has)
    def _():
        fill.start()

    chain.start()
    place.greet()
    def row_copies(first, last):
        return [
            remote(
                spot(holder, index),
                spot(holder, index),
                send_row.at[index, step - 1],
                recv_row.at[index, holder],
                place.row,
                lax.rem(place.col + step, cols),
            )
            for index in range(first, last)
            for step in range(1, cols)
        ]

    line = [
        remote(
            gram_ref.at[place.me],
            gram_ref.at[place.me],
            line_send.at[step - 1],
            line_recv.at[0],
            lax.rem(place.row + 2 * step, rows),
            place.col,
        )
        for step in range(1, place.planes)
    ]
    chain.share()
    chain.spread(0, EARLY)

    @pl.when(has)
    def _():
        fill.wait()
        for copy in row_copies(0, 1):
            copy.start()

        @pl.when(place.plane > 0)
        def _():
            for copy in row_copies(1, 2):
                copy.start()

    @pl.when(first)
    def _():
        chain.join()
        width = tile * tiles // 2
        offset = place.core * width
        lanes = lax.broadcasted_iota(jnp.int32, (cols_ref.shape[0], width), 1) + offset
        limit = jnp.where(place.col < panel_tiles, tile, 0)
        value = cols_ref[:, pl.ds(pl.multiple_of(offset, tile), width)]
        value = jnp.where(lanes >= limit, value, 0.0)
        gram = mm(value, value, 1, 1)
        size = stack.shape[1]
        for piece in range(stack.shape[0]):
            stack[piece] = gram[piece * size : (piece + 1) * size]
        plane_scatter(place, place.peers(), stack, parts, gram_ref, send_one, recv_one)
        for copy in line:
            copy.start()

    chain.spread(EARLY, chain.chunks)

    for chunk in range(EARLY):
        @pl.when(place.plane <= EARLY - chunk)
        def _():
            chain.middle_step(chunk)

    @pl.when(place.plane > 0)
    def _():
        line[0].wait_recv()

    gathers = plane_gather(place, gram_ref.at[place.me], send_two, recv_two)
    for chunk in range(EARLY):
        @pl.when(place.plane > EARLY - chunk)
        def _():
            chain.middle_step(chunk)

    @pl.when(chain.ends())
    def _():
        chain.step(0)

    spread.send()

    @pl.when(has)
    def _():
        @pl.when(first)
        def _():
            for copy in row_copies(1, 2):
                copy.start()

        for copy in row_copies(2, PARTS):
            copy.start()

    for copy in gathers:
        copy.wait()

    def top():
        spread.wait()
        return top_ref[...]

    size = inverse_ref.shape[0]
    orthogonal_top(
        gram_ref[...].reshape(size, size), top, 0, inverse_ref, shifted_ref, sign_ref,
        later_steps(chain, EARLY, 3),
    )
    chain.end_steps(1)

    @pl.when(first)
    def _():
        for copy in line:
            copy.wait_send()

    spread.finish()

    @pl.when(has)
    def _():
        for copy in row_copies(0, PARTS):
            copy.wait_send()

    for col in range(held):
        @pl.when(place.col != col)
        def _():
            for index in range(PARTS):
                remote(
                    spot(col, index), spot(col, index), send_row.at[index, 0],
                    recv_row.at[index, col], place.row, place.col,
                ).wait_recv()

    chain.finish(True)


def first_panel(x4, collective_id):
    rows, cols = lax.axis_size("row"), lax.axis_size("col")
    row_count, tiles, _, tile = x4.shape
    width = tiles * tile
    count = 2 * cols
    pieces = (count, BAND // count, BAND)
    vmem = pl.BlockSpec(memory_space=pltpu.VMEM)
    dma = pltpu.SemaphoreType.DMA
    panel_tiles = BAND // tile
    square = jax.ShapeDtypeStruct((BAND, BAND), x4.dtype)
    return pl.pallas_call(
        functools.partial(first_kernel, rows, cols),
        out_shape=(
            square,
            square,
            jax.ShapeDtypeStruct((1, BAND), x4.dtype),
            jax.ShapeDtypeStruct((PANELS, row_count, BAND), x4.dtype),
            jax.ShapeDtypeStruct((BAND, width), x4.dtype),
        ),
        in_specs=[pl.BlockSpec(memory_space=pltpu.HBM)],
        out_specs=(vmem,) * 5,
        scratch_shapes=[
            pltpu.VMEM(pieces, x4.dtype),
            pltpu.VMEM((count - 1,) + pieces[1:], x4.dtype),
            pltpu.VMEM(pieces, x4.dtype),
            pltpu.VMEM((BAND, BAND), x4.dtype),
            dma((count - 1,)),
            dma((count - 1,)),
            dma((rows // 2 - 1,)),
            dma((1,)),
            dma((count - 1,)),
            dma((count - 1,)),
            dma((1,)),
            dma((PARTS, cols - 1)),
            dma((PARTS, PANELS * panel_tiles)),
            dma((panel_tiles, count - 1)),
            dma((panel_tiles, 2)),
        ]
        + Chain.semaphores(tiles, width // CHUNK),
        compiler_params=pltpu.CompilerParams(
            collective_id=collective_id, has_side_effects=True, vmem_limit_bytes=56 * MIB
        ),
    )(x4)


def next_kernel(rows, cols, below, *refs):
    refs = list(refs)
    take = lambda count: [refs.pop(0) for _ in range(count)]
    (
        vec_rows, applied_rows, vec_cols, applied, transform_ref, inner_ref, applied_next,
        old_ref, later_ref, x_ref,
    ) = take(10)
    inverse_ref, shifted_ref, sign_ref, panel_ref, cols_ref = take(5)
    old_high, old_low, new_high, new_low, update_ref, ahead_ref = take(6)
    gram_in, gram_sum = take(2)
    near, near_sum, parts, gram_ref, top_ref = refs[:5]
    near_send, near_recv, line_send, line_recv, send_two, recv_two = refs[5:11]
    top_line_send, top_line_recv, top_send, top_recv = refs[11:15]
    place = Place(rows, cols)
    tile = x_ref.shape[-1]
    panel_tiles = BAND // tile
    number = 2 * panel_tiles
    chain = Chain(place, 1, x_ref, cols_ref, refs[15:])
    chain.start()
    place.greet()
    chain.share()
    chain.spread(0, EARLY + 2)
    half_full = 0.5 * mm(transform_ref[...], inner_ref[...], 1, 0)
    half = split(half_full)
    old = old_ref[...]
    ahead = applied_next[...] - mm(half_full, old, 0, 1)
    ahead_ref[...] = ahead
    chain.late_step(0)
    vec = vec_rows[...]
    vec_parts = split(vec)
    change = applied_rows[...] - mm3(vec_parts, half)
    panel = later_ref[1] - mm(vec, ahead, 1, 0) - mm(change, old, 1, 1)
    lines = lax.broadcasted_iota(jnp.int32, panel.shape, 0)
    above = (below + BAND) // tile
    limit = (above // rows + jnp.where(place.row < above % rows, 1, 0)) * tile
    panel = jnp.where(lines >= limit, panel, 0.0)
    panel_ref[...] = panel
    gram_sum[...] = mm(panel, panel, 0, 0)
    change_parts = split(change)
    for start, value in ((0, vec_parts), (BAND, change_parts)):
        old_high[:, start : start + BAND] = value[0]
        old_low[:, start : start + BAND] = value[1]
    size = BAND
    height = gram_in.shape[2]
    for col in range(cols):
        for core in range(2):
            start = (2 * col + core) * height
            gram_in[col, core] = gram_sum[start : start + height, :]
    chain.late_step(1)
    swap = remote(
        gram_in.at[place.col, 1 - place.core], near.at[0], near_send.at[0], near_recv.at[0],
        place.other, place.col,
    )
    swap.start()

    top_plane = number % rows // 2
    start = pl.multiple_of(place.core * tile, tile)
    local = number // rows * tile
    block = panel_ref.at[pl.ds(local, tile), :]
    target = top_ref.at[pl.ds(start, tile), :]
    at_top = place.plane == top_plane

    def top_line(step):
        return remote(
            block, target, top_line_send.at[step - 1], top_line_recv.at[0],
            lax.rem(place.row + 2 * step, rows), place.col,
        )

    top_near = remote(target, target, top_send.at[0], top_recv.at[0], place.other, place.col)
    top_first = remote(block, target, top_send.at[0], top_recv.at[0], place.other, place.col)

    swap.wait_recv()
    near_sum[0] = gram_in[place.col, place.core] + near[0]
    line = [
        remote(
            near_sum.at[0], parts.at[step - 1], line_send.at[step - 1], line_recv.at[step - 1],
            lax.rem(place.row + 2 * step, rows), place.col,
        )
        for step in range(1, place.planes)
    ]
    for copy in line:
        copy.start()

    @pl.when(at_top)
    def _():
        for step in range(1, place.planes):
            top_line(step).start()
        top_first.start()
        target[...] = block[...]

    chain.spread(EARLY + 2, chain.chunks)
    chain.late_step(2)
    group = 5 if x_ref.shape[1] % 10 == 0 else 1
    wide = x_ref.shape[1] // group * tile
    half_t = split(half_full.T)

    def own_cols(index, carry):
        here = pl.ds(pl.multiple_of(index * wide, wide), wide)
        vec = split(vec_cols[:, here])
        change = applied[:, here] - mm3(half_t, vec)
        update_ref[:, here] = change
        for start, value in ((0, split(change)), (size, vec)):
            new_high[start : start + size, here] = value[0]
            new_low[start : start + size, here] = value[1]
        return carry

    lax.fori_loop(0, group, own_cols, 0)
    chain.late_step(3)
    total = near_sum[0]
    for slot, copy in enumerate(line):
        copy.wait_recv()
        total = total + parts[slot]
    piece = 2 * place.col + place.core
    gram_ref[piece] = total
    gathers = plane_gather(place, gram_ref.at[piece], send_two, recv_two)

    @pl.when(jnp.logical_not(at_top))
    def _():
        top_line(1).wait_recv()
        top_near.start()

    for chunk in range(4, 6):
        chain.late_step(chunk)
    for copy in gathers:
        copy.wait()

    def top():
        top_near.wait_recv()
        return top_ref[...]

    orthogonal_top(
        gram_ref[...].reshape(size, size), top, 1, inverse_ref, shifted_ref, sign_ref,
        later_steps(chain, 6, 2, True),
    )
    chain.end_steps(0)
    swap.wait_send()
    for copy in line:
        copy.wait_send()
    top_near.wait_send()

    @pl.when(at_top)
    def _():
        for step in range(1, place.planes):
            top_line(step).wait_send()

    chain.finish()


def next_panel(operands, x4, below, collective_id):
    rows, cols = lax.axis_size("row"), lax.axis_size("col")
    row_count, tiles, _, tile = x4.shape
    width = tiles * tile
    count = 2 * cols
    piece = (BAND // count, BAND)
    planes = rows // 2
    vmem = pl.BlockSpec(memory_space=pltpu.VMEM)
    dma = pltpu.SemaphoreType.DMA
    f32, bf16 = jnp.float32, jnp.bfloat16
    shape = jax.ShapeDtypeStruct
    square = shape((BAND, BAND), f32)
    return pl.pallas_call(
        functools.partial(next_kernel, rows, cols, below),
        out_shape=(
            square,
            square,
            shape((1, BAND), f32),
            shape((row_count, BAND), f32),
            shape((BAND, width), f32),
            shape((row_count, 2 * BAND), bf16),
            shape((row_count, 2 * BAND), bf16),
            shape((2 * BAND, width), bf16),
            shape((2 * BAND, width), bf16),
            shape((BAND, width), f32),
            square,
        ),
        in_specs=[vmem] * len(operands) + [pl.BlockSpec(memory_space=pltpu.HBM)],
        out_specs=(vmem,) * 11,
        scratch_shapes=[
            pltpu.VMEM((cols, 2) + piece, f32),
            pltpu.VMEM((BAND, BAND), f32),
            pltpu.VMEM((1,) + piece, f32),
            pltpu.VMEM((1,) + piece, f32),
            pltpu.VMEM((planes - 1,) + piece, f32),
            pltpu.VMEM((count,) + piece, f32),
            pltpu.VMEM((BAND, BAND), f32),
            dma((1,)),
            dma((1,)),
            dma((planes - 1,)),
            dma((planes - 1,)),
            dma((count - 1,)),
            dma((count - 1,)),
            dma((planes - 1,)),
            dma((1,)),
            dma((1,)),
            dma((1,)),
        ]
        + Chain.semaphores(tiles, width // CHUNK),
        compiler_params=pltpu.CompilerParams(
            collective_id=collective_id, has_side_effects=True, vmem_limit_bytes=44 * MIB
        ),
    )(*operands, x4)


def split(value):
    high = value.astype(jnp.bfloat16)
    return high, (value - high.astype(jnp.float32)).astype(jnp.bfloat16)


def split_outside(value):
    high = lax.reduce_precision(value, 8, 7)
    return high.astype(jnp.bfloat16), (value - high).astype(jnp.bfloat16)


def dot(a, b):
    return jnp.dot(a, b, preferred_element_type=jnp.float32)


def apply_kernel(rows, cols, tiles, fixed, *refs):
    place = Place(rows, cols)
    refs = list(refs)
    take = lambda count: [refs.pop(0) for _ in range(count)]
    x_ref, left_ref, shifted_ref, sign_ref, vec_ref = take(5)
    old_high, old_low, new_high, new_low = take(4) if fixed else [None] * 4
    applied_row_ref, transform_ref, applied_ref, inner_ref = take(4)
    next_ref = take(1)[0] if tiles else None
    kept_ref = take(1)[0] if fixed else None
    block, part, near, pair, left_in, right_in, left_out, right_out, out_ref, row_ref = take(10)
    total_ref, stack, parts = take(3)
    (
        load, near_send, near_recv, left_send, left_recv, right_send, right_recv,
        both_send, both_recv, row_send, row_recv, send_one, recv_one, send_two, recv_two,
    ) = take(15)
    next_sems = take(2) if tiles else None
    store = take(1)[0] if fixed else None
    plane, core, planes = place.plane, place.core, place.planes
    tile = x_ref.shape[-1]
    chunks = block.shape[0]
    pieces = pair.shape[0] // chunks
    depth = pair.shape[1]
    subs = chunks * pieces
    size = left_ref.shape[0] // 2

    def load_of(chunk, index):
        return pltpu.make_async_copy(
            x_ref.at[:, 2 * chunk + index, 0, :],
            block.at[chunk, :, pl.ds(index * tile, tile)],
            load.at[chunk, index],
        )

    def store_of(chunk, index):
        return pltpu.make_async_copy(
            block.at[chunk, :, pl.ds(index * tile, tile)],
            kept_ref.at[:, 2 * chunk + index, 0, :],
            store.at[chunk, index],
        )

    for chunk in range(chunks):
        for index in range(2):
            load_of(chunk, index).start()
    place.greet()

    def near_of(chunk):
        return remote(
            part.at[chunk, 1 - core],
            near.at[chunk],
            near_send.at[chunk],
            near_recv.at[chunk],
            place.other,
            place.col,
        )

    def rightward(source, index):
        return remote(
            source.at[index], left_in.at[index], right_send.at[index], left_recv.at[index],
            lax.rem(place.row + 2, rows), place.col,
        )

    def leftward(source, index):
        return remote(
            source.at[index], right_in.at[index], left_send.at[index], right_recv.at[index],
            lax.rem(place.row + rows - 2, rows), place.col,
        )

    def joined(chunk):
        near_of(chunk).wait_recv()
        for piece in range(pieces):
            pair[chunk * pieces + piece] = part[chunk, core, piece] + near[chunk, piece]

        @pl.when(plane == 0)
        def _():
            for piece in range(pieces):
                rightward(pair, chunk * pieces + piece).start()

        @pl.when(plane == planes - 1)
        def _():
            for piece in range(pieces):
                leftward(pair, chunk * pieces + piece).start()

    def product(chunk, carry):
        for index in range(2):
            load_of(chunk, index).wait()
        if fixed:
            here = pl.ds(pl.multiple_of(chunk * 2 * tile, 2 * tile), 2 * tile)
            change = dot(old_high[...], new_high[:, here]) + (
                dot(old_low[...], new_high[:, here]) + dot(old_high[...], new_low[:, here])
            )
            block[chunk] = block[chunk] - change
            for index in range(2):
                store_of(chunk, index).start()
        high, low = split(block[chunk])
        value = dot(left_ref[...], high)
        value = value[:size] + (value[size:] + dot(left_ref[:size], low))
        for index in range(2):
            for piece in range(pieces):
                part[chunk, index, piece] = value[
                    piece * depth : (piece + 1) * depth, index * tile : (index + 1) * tile
                ]
        near_of(chunk).start()

        @pl.when(chunk > 0)
        def _():
            joined(chunk - 1)

        for piece in range(pieces):
            chain((chunk - BEHIND) * pieces + piece, 0)
        return carry

    left_lag = HOP * jnp.maximum(plane - 1, 0)
    right_lag = HOP * jnp.maximum(planes - 2 - plane, 0)
    last_lag = jnp.maximum(left_lag, right_lag)
    held = cols * core + place.col
    source = held // 2 == plane
    target_row = 2 * plane + lax.rem(place.col, 2)
    to_self = target_row == place.row
    square = cols == 4
    beside = place.col + 1 - 2 * lax.rem(place.col, 2)
    across = lax.rem(place.col + 2, 4)
    targets = (place.col, beside, across) if square else tuple(
        lax.rem(place.col + step, cols) for step in range(cols)
    )
    relays = (lax.rem(place.row, cols) == across) if square else None

    def depths(index):
        return pl.ds(pl.multiple_of(lax.rem(index, pieces) * depth, depth), depth)

    def lanes(index):
        return pl.ds(pl.multiple_of((2 * (index // pieces) + core) * tile, tile), tile)

    def row_lanes(index):
        return pl.ds(pl.multiple_of(index // pieces * tile, tile), tile)

    def both_of(index):
        spot = out_ref.at[depths(index), lanes(index)]
        return remote(spot, spot, both_send.at[index], both_recv.at[index], place.other, place.col)

    def row_of(index, step):
        return remote(
            out_ref.at[depths(index), lanes(index)],
            row_ref.at[depths(index), row_lanes(index)],
            row_send.at[index, step],
            row_recv.at[index],
            target_row,
            targets[step],
        )

    def relay_of(index):
        spot = row_ref.at[depths(index), row_lanes(index)]
        return remote(spot, spot, row_send.at[index, 3], row_recv.at[index], place.row, beside)

    def relay(index):
        @pl.when(relays & (index >= 0) & (index < subs))
        def _():
            relay_of(index).wait_recv()
            relay_of(index).start()

    def chain(step, carry):
        index = step - left_lag

        @pl.when((plane > 0) & (index >= 0) & (index < subs))
        def _():
            rightward(pair, index).wait_recv()

            @pl.when(plane < planes - 1)
            def _():
                right_out[index] = left_in[index] + pair[index]
                rightward(right_out, index).start()

        other = step - right_lag

        @pl.when((plane < planes - 1) & (other >= 0) & (other < subs))
        def _():
            leftward(pair, other).wait_recv()

            @pl.when(plane > 0)
            def _():
                left_out[other] = right_in[other] + pair[other]
                leftward(left_out, other).start()

        done = step - last_lag

        @pl.when((done >= 0) & (done < subs))
        def _():
            @pl.when(plane == 0)
            def _():
                out_ref[depths(done), lanes(done)] = pair[done] + right_in[done]

            @pl.when(plane == planes - 1)
            def _():
                out_ref[depths(done), lanes(done)] = left_in[done] + pair[done]

            @pl.when((plane > 0) & (plane < planes - 1))
            def _():
                out_ref[depths(done), lanes(done)] = right_out[done] + right_in[done]

            both_of(done).start()

            @pl.when(source)
            def _():
                for step in range(1, len(targets)):
                    row_of(done, step).start()

                @pl.when(to_self)
                def _():
                    row_ref[depths(done), row_lanes(done)] = out_ref[depths(done), lanes(done)]

                @pl.when(jnp.logical_not(to_self))
                def _():
                    row_of(done, 0).start()

        if square:
            relay(done - HOP)
        return carry

    lax.fori_loop(0, chunks, product, 0)
    joined(chunks - 1)
    steps = subs + HOP * (planes - 2 + square)
    count = [0, max(chunks - BEHIND, 0) * pieces]

    def hook():
        count[0] += 1
        if count[0] % 2 == 0 and count[1] < steps:
            chain(count[1], 0)
            count[1] += 1

    transform_ref[...] = block_transform(shifted_ref[...], sign_ref[...], hook)
    if count[1] < steps:
        lax.fori_loop(count[1], steps, chain, 0)
    total_ref[...] = jnp.zeros_like(total_ref)
    transform = split(transform_ref[...])

    def finished(number, carry):
        for index in range(2 * pieces):
            both_of(2 * pieces * number + index).wait_recv()
        here = pl.ds(pl.multiple_of(number * 4 * tile, 4 * tile), 4 * tile)
        applied = mm3(transform, split(out_ref[:, here]))
        applied_ref[:, here] = applied
        total_ref[...] += mm3(split(vec_ref[:, here]), split(applied), 1, 1)
        return carry

    def finished_one(number, carry):
        for index in range(pieces):
            both_of(pieces * number + index).wait_recv()
        here = pl.ds(pl.multiple_of(number * 2 * tile, 2 * tile), 2 * tile)
        applied = mm3(transform, split(out_ref[:, here]))
        applied_ref[:, here] = applied
        total_ref[...] += mm3(split(vec_ref[:, here]), split(applied), 1, 1)
        return carry

    if chunks % 2 == 0:
        lax.fori_loop(0, chunks // 2, finished, 0)
    else:
        lax.fori_loop(0, chunks, finished_one, 0)
    height = stack.shape[1]
    for piece in range(stack.shape[0]):
        stack[piece] = total_ref[piece * height : (piece + 1) * height, :]
    if tiles:
        spread = Spread(place, applied_ref, tiles, next_ref, *next_sems)
        spread.send()
    plane_scatter(place, place.peers()[: cols - 1], stack, parts, inner_ref, send_one, recv_one)
    gathers = plane_gather(place, inner_ref.at[place.me], send_two, recv_two)
    gets = jnp.logical_not(source & to_self)
    if square:
        gets = gets & jnp.logical_not(relays)

    def drain(index, carry):
        both_of(index).wait_send()

        @pl.when(plane < planes - 1)
        def _():
            rightward(pair, index).wait_send()

        @pl.when(plane > 0)
        def _():
            leftward(pair, index).wait_send()

        @pl.when(source)
        def _():
            for step in range(1, len(targets)):
                row_of(index, step).wait_send()

            @pl.when(jnp.logical_not(to_self))
            def _():
                row_of(index, 0).wait_send()

        @pl.when(gets)
        def _():
            row_of(index, 0).wait_recv()

        if square:
            @pl.when(relays)
            def _():
                relay_of(index).wait_send()

        return carry

    def drain_chunk(chunk, carry):
        if fixed:
            for index in range(2):
                store_of(chunk, index).wait()
        near_of(chunk).wait_send()
        return carry

    lax.fori_loop(0, subs, drain, 0)
    lax.fori_loop(0, chunks, drain_chunk, 0)
    applied_row_ref[...] = mm3(split(row_ref[...].T), split(transform_ref[...]), 1, 1)
    for copy in gathers:
        copy.wait()
    if tiles:
        spread.wait()
        spread.finish()


PIECES = 2
HOP = 3
BEHIND = 3


def apply(x4, left, shifted, signs, vec_cols, tiles, more, collective_id):
    rows, cols = lax.axis_size("row"), lax.axis_size("col")
    row_count, held_tiles, _, tile = x4.shape
    width = held_tiles * tile
    chunks = held_tiles // 2
    count = 2 * cols
    vmem = pl.BlockSpec(memory_space=pltpu.VMEM)
    hbm = pl.BlockSpec(memory_space=pltpu.HBM)
    dma = pltpu.SemaphoreType.DMA
    f32 = jnp.float32
    piece = (BAND // PIECES, tile)
    subs = PIECES * chunks
    sums = (count, BAND // count, BAND)
    kept = bool(more)
    square = jax.ShapeDtypeStruct((BAND, BAND), f32)
    wide = jax.ShapeDtypeStruct((BAND, width), f32)
    shapes = (
        jax.ShapeDtypeStruct((row_count, BAND), f32),
        square,
        wide,
        jax.ShapeDtypeStruct(sums, f32),
    )
    shapes += (square,) if tiles else ()
    out = pl.pallas_call(
        functools.partial(apply_kernel, rows, cols, tiles, kept),
        out_shape=shapes + ((jax.ShapeDtypeStruct(x4.shape, x4.dtype),) if kept else ()),
        in_specs=[hbm] + [vmem] * (4 + len(more)),
        out_specs=(vmem,) * len(shapes) + ((hbm,) if kept else ()),
        scratch_shapes=[
            pltpu.VMEM((chunks, row_count, 2 * tile), f32),
            pltpu.VMEM((chunks, 2, PIECES) + piece, f32),
            pltpu.VMEM((chunks, PIECES) + piece, f32),
        ]
        + [pltpu.VMEM((subs,) + piece, f32)] * 5
        + [
            pltpu.VMEM((BAND, width), f32),
            pltpu.VMEM((BAND, row_count), f32),
            pltpu.VMEM((BAND, BAND), f32),
            pltpu.VMEM(sums, f32),
            pltpu.VMEM((cols - 1,) + sums[1:], f32),
        ]
        + [dma((chunks, 2)), dma((chunks,)), dma((chunks,))]
        + [dma((subs,))] * 6
        + [dma((subs, cols)), dma((subs,))]
        + [dma((cols - 1,))] * 2
        + [dma((count - 1,))] * 2
        + ([dma((len(tiles), count - 1)), dma((len(tiles), 2))] if tiles else [])
        + ([dma((chunks, 2))] if kept else []),
        compiler_params=pltpu.CompilerParams(
            collective_id=collective_id, has_side_effects=True, vmem_limit_bytes=(60 if kept else 48) * MIB
        ),
    )(x4, left, shifted, signs, vec_cols, *more)
    out = list(out)
    out[3] = out[3].reshape(BAND, BAND)
    return out


def update_kernel(x_ref, left_high, left_low, right_high, right_low, out_ref, block, result, load, store):
    tile = x_ref.shape[-1]
    chunks = x_ref.shape[1] // 2

    def load_of(chunk, index):
        return pltpu.make_async_copy(
            x_ref.at[:, 2 * chunk + index, 0, :],
            block.at[lax.rem(chunk, 2), :, pl.ds(index * tile, tile)],
            load.at[lax.rem(chunk, 2), index],
        )

    def store_of(chunk, index):
        return pltpu.make_async_copy(
            result.at[lax.rem(chunk, 2), :, pl.ds(index * tile, tile)],
            out_ref.at[:, 2 * chunk + index, 0, :],
            store.at[lax.rem(chunk, 2), index],
        )

    for chunk in range(2):
        for index in range(2):
            load_of(chunk, index).start()

    def body(chunk, carry):
        slot = lax.rem(chunk, 2)
        for index in range(2):
            load_of(chunk, index).wait()

        @pl.when(chunk >= 2)
        def _():
            for index in range(2):
                store_of(chunk - 2, index).wait()

        here = pl.ds(pl.multiple_of(chunk * 2 * tile, 2 * tile), 2 * tile)
        value = dot(left_high[...], right_high[:, here]) + (
            dot(left_low[...], right_high[:, here]) + dot(left_high[...], right_low[:, here])
        )
        result[slot] = block[slot] - value
        for index in range(2):
            store_of(chunk, index).start()

        @pl.when(chunk + 2 < chunks)
        def _():
            for index in range(2):
                load_of(chunk + 2, index).start()

        return carry

    lax.fori_loop(0, chunks, body, 0)
    for chunk in range(chunks - 2, chunks):
        for index in range(2):
            store_of(chunk, index).wait()


def update(x4, left, right):
    row_count, tiles, _, tile = x4.shape
    vmem = pl.BlockSpec(memory_space=pltpu.VMEM)
    hbm = pl.BlockSpec(memory_space=pltpu.HBM)
    dma = pltpu.SemaphoreType.DMA
    return pl.pallas_call(
        update_kernel,
        out_shape=jax.ShapeDtypeStruct(x4.shape, x4.dtype),
        in_specs=[hbm] + [vmem] * 4,
        out_specs=hbm,
        scratch_shapes=[pltpu.VMEM((2, row_count, 2 * tile), jnp.float32)] * 2
        + [dma((2, 2)), dma((2, 2))],
        compiler_params=pltpu.CompilerParams(vmem_limit_bytes=48 * MIB),
    )(x4, *left, *right)


def on_device(matrix_tiles):
    tile_shape = matrix_tiles.shape
    block_rows, _, tile_size, block_cols = tile_shape[:4]
    row_count = block_rows * tile_size
    col_count = block_cols * tile_size
    row_devices = lax.axis_size("row")
    col_devices = lax.axis_size("col")
    row_index = lax.axis_index("row")
    panel_tiles = BAND // tile_size
    assert row_devices == 2 * col_devices and PANELS * panel_tiles <= col_devices
    x4 = matrix_tiles.reshape(row_count, block_cols, 1, tile_size)

    def positions(count, devices, index):
        place = jnp.arange(count, dtype=jnp.int32)
        return (place // tile_size * devices + index) * tile_size + place % tile_size

    global_rows = positions(row_count, row_devices, row_index)
    global_cols = positions(col_count, lax.axis_size("col"), lax.axis_index("col"))
    band = jnp.arange(BAND, dtype=jnp.int32)
    inverse, shifted, signs, rows_held, panel_cols = first_panel(x4, 0)
    panel_rows = rows_held[0]
    kept, more = x4, ()
    for panel_index in range(PANELS):
        below = (panel_index + 1) * BAND
        last = panel_index == PANELS - 1
        panel_rows = jnp.where((global_rows >= below)[:, None], panel_rows, 0.0)
        unit_rows = (global_rows[:, None] - below == band[None, :]).astype(jnp.float32)
        unit_rows_t = (band[:, None] == global_rows[None, :] - below).astype(jnp.float32)
        vec_rows = multiply(panel_rows, inverse, 1, 1) - unit_rows * signs
        vec_rows_t = multiply(inverse, panel_rows, 1, 1) - unit_rows_t * signs.reshape(BAND, 1)
        panel_cols = jnp.where((global_cols >= below)[None, :], panel_cols, 0.0)
        unit_cols = (band[:, None] == global_cols[None, :] - below).astype(jnp.float32)
        vec_cols = multiply(inverse, panel_cols) - unit_cols * signs.reshape(BAND, 1)
        first = below // tile_size
        applied_rows, transform, applied, inner, *rest = apply(
            kept,
            jnp.concatenate(split_outside(vec_rows_t), 0),
            shifted,
            signs,
            vec_cols,
            () if last else tuple(range(first, first + panel_tiles)),
            more,
            1 + panel_index,
        )
        if last:
            break
        old_shifted, old_cols = shifted, vec_cols
        (
            inverse, shifted, signs, panel_rows, panel_cols,
            old_high, old_low, new_high, new_low, update_cols, update_next,
        ) = next_panel(
            (
                vec_rows, applied_rows, vec_cols, applied, transform, inner, rest[0], shifted,
                rows_held,
            ),
            x4,
            below,
            3,
        )
        more = (old_high, old_low, new_high, new_low)
        panel_cols = (
            panel_cols - multiply(update_next, old_cols, 0, 0) - multiply(old_shifted, update_cols)
        )
    half_inner = 0.5 * multiply(transform, inner)
    update_rows = applied_rows - multiply(vec_rows, half_inner)
    update_cols = applied - multiply(half_inner, vec_cols, 0, 0)
    left = split_outside(jnp.concatenate([vec_rows, update_rows], 1))
    right = split_outside(jnp.concatenate([update_cols, vec_cols], 0))
    return update(rest[0], left, right).reshape(tile_shape)


def solution(mesh):
    return jax.shard_map(
        on_device,
        mesh=mesh,
        in_specs=(P(None, "row", None, None, "col", None),),
        out_specs=P(None, "row", None, None, "col", None),
        check_vma=False,
    )
```

```python
import functools

import jax
import jax.numpy as jnp
from jax import lax
from jax.experimental import pallas as pl
from jax.experimental.pallas import tpu as pltpu
from jax.sharding import PartitionSpec as P

BAND = 256
PANELS = 2
MIB = 1024 * 1024
MESH = pl.DeviceIdType.MESH

HI = lax.Precision.HIGHEST
def mm(a, b, ca, cb):
    return lax.dot_general(a, b, (((ca,), (cb,)), ((), ())), precision=HI, preferred_element_type=jnp.float32)

def base_inverse(block, hook):
    size = block.shape[0]
    wide = (8, 2 * size)
    group = 8
    places = lax.broadcasted_iota(jnp.int32, wide, 0)
    cols = lax.broadcasted_iota(jnp.int32, wide, 1)
    work = []
    for k in range(size // 8):
        unit = jnp.where(places + 8 * k == cols, 1.0, 0.0)[:, :size]
        work.append(jnp.concatenate([block[8 * k : 8 * k + 8], unit], 1))
    for start in range(0, size, group):
        own, offset = divmod(start, 8)
        rows = [jnp.broadcast_to(work[own][offset + i : offset + i + 1], wide) for i in range(group)]
        pivot = [
            [jnp.broadcast_to(rows[i][:, start + j : start + j + 1], wide) for j in range(group)]
            for i in range(group)
        ]
        first = own if offset + group < 8 else own + 1
        columns = [
            [jnp.broadcast_to(work[k][:, start + i : start + i + 1], wide) for i in range(group)]
            for k in range(first, len(work))
        ]
        scaled = []
        for i in range(group):
            inverse = 1.0 / pivot[i][i]
            scaled.append(rows[i] * inverse)
            for j in range(i + 1, group):
                ratio = pivot[i][j] * inverse
                for l in range(j, group):
                    pivot[j][l] = pivot[j][l] - ratio * pivot[i][l]
                rows[j] = rows[j] - ratio * rows[i]
                for column in columns:
                    column[j] = column[j] - ratio * column[i]
        for k, column in zip(range(first, len(work)), columns):
            change = column[0] * scaled[0]
            for i in range(1, group):
                change = change + column[i] * scaled[i]
            if k == own:
                change = jnp.where(places >= offset + group, change, 0.0)
            work[k] = work[k] - change
        for i in range(group):
            work[own] = jnp.where(places == offset + i, rows[i], work[own])
        hook()
    result = []
    for k, value in enumerate(work):
        pivots = jnp.sum(jnp.where(places + 8 * k == cols, value, 0.0), axis=1, keepdims=True)
        result.append(value[:, size:] * (1.0 / jnp.sqrt(pivots)))
    return jnp.concatenate(result, 0)


def factor_inverse(matrix, base, hook):
    size = matrix.shape[0]
    if size <= base:
        return base_inverse(matrix, hook)
    half = size // 2
    first = factor_inverse(matrix[:half, :half], base, hook)
    lower = mm(matrix[half:, :half], first, 1, 1)
    second = factor_inverse(matrix[half:, half:] - mm(lower, lower, 1, 1), base, hook)
    corner = -mm(second, mm(lower, first, 1, 0), 1, 0)
    top = jnp.concatenate([first, jnp.zeros_like(first)], 1)
    return jnp.concatenate([top, jnp.concatenate([corner, second], 1)], 0)

def orthogonal_top(gram, top, top_dim, inverse_ref, shifted_ref, sign_ref, hook):
    size = gram.shape[0]
    inverse = factor_inverse(gram, 64, hook)
    inverse_ref[...] = inverse
    basis = mm(top(), inverse, top_dim, 1)
    rows = lax.broadcasted_iota(jnp.int32, (size, size), 0)
    cols = lax.broadcasted_iota(jnp.int32, (size, size), 1)
    sign_square = jnp.where(rows == cols, jnp.where(basis >= 0, -1.0, 1.0), 0.0)
    shifted_ref[...] = basis - sign_square
    sign_ref[...] = jnp.sum(sign_square, axis=0, keepdims=True)


def block_transform(shifted, signs, hook):
    size = shifted.shape[0]
    outer = factor_inverse(mm(shifted, shifted, 0, 0), 64, hook)
    rows = lax.broadcasted_iota(jnp.int32, (size, size), 0)
    cols = lax.broadcasted_iota(jnp.int32, (size, size), 1)
    sign_column = jnp.sum(jnp.where(rows == cols, signs, 0.0), axis=1, keepdims=True)
    parts = split(outer)
    return -mm3(parts, split(mm3(parts, split(shifted * sign_column), 1, 1)), 0, 0)


def mm3(a, b, ca=1, cb=0):
    def part(x, y):
        return lax.dot_general(
            x, y, (((ca,), (cb,)), ((), ())), preferred_element_type=jnp.float32
        )

    return part(a[0], b[0]) + (part(a[0], b[1]) + part(a[1], b[0]))


def multiply(first, second, first_dim=1, second_dim=0, precision=HI):
    return lax.dot_general(
        first,
        second,
        (((first_dim,), (second_dim,)), ((), ())),
        precision=precision,
        preferred_element_type=jnp.float32,
    )


def remote(source, target, send_sem, recv_sem, row, col):
    return pltpu.make_async_remote_copy(
        src_ref=source,
        dst_ref=target,
        send_sem=send_sem,
        recv_sem=recv_sem,
        device_id={"row": row, "col": col},
        device_id_type=MESH,
    )


class Place:
    def __init__(self, rows, cols):
        self.rows, self.cols, self.planes = rows, cols, rows // 2
        row = lax.axis_index("row")
        self.col = lax.axis_index("col")
        self.plane = row // 2
        self.core = row % 2
        self.row = row
        self.other = 2 * self.plane + (1 - self.core)
        self.me = self.core * cols + self.col

    def peers(self):
        found = []
        for core_step in range(2):
            for col_step in range(self.cols):
                if core_step or col_step:
                    core = lax.rem(self.core + core_step, 2)
                    col = lax.rem(self.col + col_step, self.cols)
                    found.append((2 * self.plane + core, col, core * self.cols + col))
        return found

    def greet(self, line=True):
        barrier = pltpu.get_barrier_semaphore()
        count = 0
        for row, col, _ in self.peers():
            pl.semaphore_signal(
                barrier, inc=1, device_id={"row": row, "col": col}, device_id_type=MESH
            )
            count += 1
        for step in range(1, self.planes) if line else ():
            row = lax.rem(self.row + 2 * step, self.rows)
            pl.semaphore_signal(
                barrier, inc=1, device_id={"row": row, "col": self.col}, device_id_type=MESH
            )
            count += 1
        pl.semaphore_wait(barrier, count)


def plane_scatter(place, peers, x_ref, parts, out_ref, send_sem, recv_sem):
    copies = []
    for slot, (row, col, piece) in enumerate(peers):
        copies.append(
            remote(
                x_ref.at[piece], parts.at[slot], send_sem.at[slot], recv_sem.at[slot], row, col
            )
        )
        copies[-1].start()
    total = x_ref[place.me]
    for slot, copy in enumerate(copies):
        copy.wait_recv()
        total = total + parts[slot]
    out_ref[place.me] = total
    for copy in copies:
        copy.wait_send()


def plane_gather(place, mine, send_sem, recv_sem):
    copies = []
    for slot, (row, col, _) in enumerate(place.peers()):
        copies.append(remote(mine, mine, send_sem.at[slot], recv_sem.at[slot], row, col))
        copies[-1].start()
    return copies


class Spread:
    def __init__(self, place, source_ref, tiles, target_ref, send_sem, recv_sem):
        self.place, self.source, self.tiles, self.target = place, source_ref, tiles, target_ref
        self.send_sem, self.recv_sem = send_sem, recv_sem
        self.tile = target_ref.shape[0] // 2

    def refs(self, index, core):
        start = pl.multiple_of(core * self.tile, self.tile)
        local = self.tiles[index] // self.place.cols
        return (
            self.source.at[pl.ds(start, self.tile), pl.ds(local * self.tile, self.tile)],
            self.target.at[pl.ds(start, self.tile), pl.ds(index * self.tile, self.tile)],
        )

    def holder(self, index):
        return self.place.col == self.tiles[index] % self.place.cols

    def copies(self, index):
        source, target = self.refs(index, self.place.core)
        return [
            remote(
                source,
                target,
                self.send_sem.at[index, slot],
                self.recv_sem.at[index, self.place.core],
                row,
                col,
            )
            for slot, (row, col, _) in enumerate(self.place.peers())
        ]

    def send(self):
        for index in range(len(self.tiles)):
            @pl.when(self.holder(index))
            def _():
                for copy in self.copies(index):
                    copy.start()
                source, target = self.refs(index, self.place.core)
                target[...] = source[...]

    def wait(self):
        for index in range(len(self.tiles)):
            for core in range(2):
                source, target = self.refs(index, core)

                @pl.when(jnp.logical_not(self.holder(index) & (self.place.core == core)))
                def _():
                    remote(
                        source,
                        target,
                        self.send_sem.at[index, 0],
                        self.recv_sem.at[index, core],
                        self.place.other,
                        self.place.col,
                    ).wait_recv()

    def finish(self):
        for index in range(len(self.tiles)):
            @pl.when(self.holder(index))
            def _():
                for copy in self.copies(index):
                    copy.wait_send()


class Chain:
    def __init__(self, place, source, x_ref, panel_ref, sems):
        self.place, self.source, self.x_ref, self.ref = place, source, x_ref, panel_ref
        self.load, self.sends, self.recv, self.share_send, self.share_recv = sems
        self.tile = x_ref.shape[-1]
        self.tiles = x_ref.shape[1]
        self.chunks = self.recv.shape[0]
        self.width = panel_ref.shape[1] // self.chunks
        self.at_source = place.plane == source

    def loads(self):
        start = pl.multiple_of(self.place.core * self.tile, self.tile)
        for tile in range(self.tiles):
            yield pltpu.make_async_copy(
                self.x_ref.at[pl.ds(0, self.tile), tile, 0, :],
                self.ref.at[pl.ds(start, self.tile), pl.ds(tile * self.tile, self.tile)],
                self.load.at[tile],
            )

    def part(self, chunk):
        start = pl.multiple_of(self.place.core * self.tile, self.tile)
        here = chunk * self.width
        if not isinstance(here, int):
            here = pl.multiple_of(here, self.width)
        return self.ref.at[pl.ds(start, self.tile), pl.ds(here, self.width)]

    def hop(self, chunk, step, sem):
        part = self.part(chunk)
        row = lax.rem(self.place.row + 2 * step + self.place.rows, self.place.rows)
        return remote(part, part, self.sends.at[sem, chunk], self.recv.at[chunk], row, self.place.col)

    def shared(self, chunk):
        part = self.part(chunk)
        return remote(
            part,
            part,
            self.share_send.at[chunk],
            self.share_recv.at[chunk],
            self.place.other,
            self.place.col,
        )

    def start(self):
        @pl.when(self.at_source)
        def _():
            for copy in self.loads():
                copy.start()

    def share(self):
        @pl.when(self.at_source)
        def _():
            for copy in self.loads():
                copy.wait()
            for chunk in range(self.chunks):
                self.shared(chunk).start()

    def spread(self, first, last):
        @pl.when(self.at_source)
        def _():
            for chunk in range(first, min(last, self.chunks)):
                if self.source < self.place.planes - 1:
                    self.hop(chunk, 1, 0).start()
                if self.source > 0:
                    self.hop(chunk, -1, 1).start()

    def step(self, chunk):
        place = self.place
        for step, sem, away, more in (
            (1, 0, place.plane > self.source, place.plane < place.planes - 1),
            (-1, 1, place.plane < self.source, place.plane > 0),
        ):
            if step < 0 and self.source == 0 or step > 0 and self.source == place.planes - 1:
                continue

            @pl.when(away)
            def _():
                self.hop(chunk, step, sem).wait_recv()

                @pl.when(more)
                def _():
                    self.hop(chunk, step, sem).start()

                self.shared(chunk).start()

    def join(self):
        for chunk in range(self.chunks):
            self.shared(chunk).wait_recv()

    def ends(self):
        place = self.place
        last = (place.plane == 0) | (place.plane == place.planes - 1)
        return last & jnp.logical_not(self.at_source)

    def middle_step(self, chunk):
        @pl.when(jnp.logical_not(self.ends()))
        def _():
            self.step(chunk)

    def end_steps(self, first):
        @pl.when(self.ends())
        def _():
            for chunk in range(first, self.chunks):
                self.step(chunk)

    def late_step(self, chunk):
        index = chunk - jnp.where(jnp.abs(self.place.plane - self.source) > 1, 1, 0)

        @pl.when((index >= 0) & (index < self.chunks) & jnp.logical_not(self.ends()))
        def _():
            self.step(index)

    def finish(self, joined=False):
        place = self.place
        if joined:
            @pl.when(jnp.logical_not(self.at_source))
            def _():
                self.join()
        else:
            self.join()
        for chunk in range(self.chunks):
            self.shared(chunk).wait_send()
        for step, sem, sent in (
            (1, 0, (place.plane >= self.source) & (place.plane < place.planes - 1)),
            (-1, 1, (place.plane <= self.source) & (place.plane > 0)),
        ):

            @pl.when(sent)
            def _():
                for chunk in range(self.chunks):
                    self.hop(chunk, step, sem).wait_send()

    @staticmethod
    def semaphores(tiles, chunks):
        dma = pltpu.SemaphoreType.DMA
        return [dma((tiles,)), dma((2, chunks)), dma((chunks,)), dma((chunks,)), dma((chunks,))]


CHUNK = 256


def later_steps(chain, first, every, late=False):
    count = [0]

    def hook():
        count[0] += 1
        chunk = first + count[0] // every - 1
        if count[0] % every == 0 and first <= chunk < chain.chunks + late:
            if late:
                chain.late_step(chunk)
            else:
                chain.middle_step(chunk)

    return hook


EARLY = 3
PARTS = 4


def first_kernel(rows, cols, x_ref, inverse_ref, shifted_ref, sign_ref, rows_ref, cols_ref, *refs):
    stack, parts, gram_ref, top_ref = refs[:4]
    send_one, recv_one, line_send, line_recv, send_two, recv_two = refs[4:10]
    load, send_row, recv_row, top_send, top_recv = refs[10:15]
    place = Place(rows, cols)
    tile, tiles = x_ref.shape[-1], x_ref.shape[1]
    panel_tiles = BAND // tile
    held = PANELS * panel_tiles
    chain = Chain(place, 0, x_ref, cols_ref, refs[15:])
    spread = Spread(
        place, cols_ref, tuple(range(panel_tiles, 2 * panel_tiles)), top_ref, top_send, top_recv
    )
    first = place.plane == 0

    share = rows_ref.shape[1] // PARTS

    def spot(col, index):
        start = pl.multiple_of(lax.rem(col, panel_tiles) * tile, tile)
        return rows_ref.at[col // panel_tiles, pl.ds(index * share, share), pl.ds(start, tile)]

    has = place.col < held
    holder = lax.rem(place.col, held)
    begin = pl.multiple_of(lax.rem(holder, panel_tiles) * tile, tile)
    fill = pltpu.make_async_copy(
        x_ref.at[:, 0, 0, :], rows_ref.at[holder // panel_tiles, :, pl.ds(begin, tile)], load.at[0]
    )

    @pl.when(has)
    def _():
        fill.start()

    chain.start()
    place.greet()
    def row_copies(first, last):
        return [
            remote(
                spot(holder, index),
                spot(holder, index),
                send_row.at[index, step - 1],
                recv_row.at[index, holder],
                place.row,
                lax.rem(place.col + step, cols),
            )
            for index in range(first, last)
            for step in range(1, cols)
        ]

    line = [
        remote(
            gram_ref.at[place.me],
            gram_ref.at[place.me],
            line_send.at[step - 1],
            line_recv.at[0],
            lax.rem(place.row + 2 * step, rows),
            place.col,
        )
        for step in range(1, place.planes)
    ]
    chain.share()
    chain.spread(0, EARLY)

    @pl.when(has)
    def _():
        fill.wait()
        for copy in row_copies(0, 1):
            copy.start()

        @pl.when(place.plane > 0)
        def _():
            for copy in row_copies(1, 2):
                copy.start()

    @pl.when(first)
    def _():
        chain.join()
        width = tile * tiles // 2
        offset = place.core * width
        lanes = lax.broadcasted_iota(jnp.int32, (cols_ref.shape[0], width), 1) + offset
        limit = jnp.where(place.col < panel_tiles, tile, 0)
        value = cols_ref[:, pl.ds(pl.multiple_of(offset, tile), width)]
        value = jnp.where(lanes >= limit, value, 0.0)
        gram = mm(value, value, 1, 1)
        size = stack.shape[1]
        for piece in range(stack.shape[0]):
            stack[piece] = gram[piece * size : (piece + 1) * size]
        plane_scatter(place, place.peers(), stack, parts, gram_ref, send_one, recv_one)
        for copy in line:
            copy.start()

    chain.spread(EARLY, chain.chunks)

    for chunk in range(EARLY):
        @pl.when(place.plane <= EARLY - chunk)
        def _():
            chain.middle_step(chunk)

    @pl.when(place.plane > 0)
    def _():
        line[0].wait_recv()

    gathers = plane_gather(place, gram_ref.at[place.me], send_two, recv_two)
    for chunk in range(EARLY):
        @pl.when(place.plane > EARLY - chunk)
        def _():
            chain.middle_step(chunk)

    @pl.when(chain.ends())
    def _():
        chain.step(0)

    spread.send()

    @pl.when(has)
    def _():
        @pl.when(first)
        def _():
            for copy in row_copies(1, 2):
                copy.start()

        for copy in row_copies(2, PARTS):
            copy.start()

    for copy in gathers:
        copy.wait()

    def top():
        spread.wait()
        return top_ref[...]

    size = inverse_ref.shape[0]
    orthogonal_top(
        gram_ref[...].reshape(size, size), top, 0, inverse_ref, shifted_ref, sign_ref,
        later_steps(chain, EARLY, 3),
    )
    chain.end_steps(1)

    @pl.when(first)
    def _():
        for copy in line:
            copy.wait_send()

    spread.finish()

    @pl.when(has)
    def _():
        for copy in row_copies(0, PARTS):
            copy.wait_send()

    for col in range(held):
        @pl.when(place.col != col)
        def _():
            for index in range(PARTS):
                remote(
                    spot(col, index), spot(col, index), send_row.at[index, 0],
                    recv_row.at[index, col], place.row, place.col,
                ).wait_recv()

    chain.finish(True)


def first_panel(x4, collective_id):
    rows, cols = lax.axis_size("row"), lax.axis_size("col")
    row_count, tiles, _, tile = x4.shape
    width = tiles * tile
    count = 2 * cols
    pieces = (count, BAND // count, BAND)
    vmem = pl.BlockSpec(memory_space=pltpu.VMEM)
    dma = pltpu.SemaphoreType.DMA
    panel_tiles = BAND // tile
    square = jax.ShapeDtypeStruct((BAND, BAND), x4.dtype)
    return pl.pallas_call(
        functools.partial(first_kernel, rows, cols),
        out_shape=(
            square,
            square,
            jax.ShapeDtypeStruct((1, BAND), x4.dtype),
            jax.ShapeDtypeStruct((PANELS, row_count, BAND), x4.dtype),
            jax.ShapeDtypeStruct((BAND, width), x4.dtype),
        ),
        in_specs=[pl.BlockSpec(memory_space=pltpu.HBM)],
        out_specs=(vmem,) * 5,
        scratch_shapes=[
            pltpu.VMEM(pieces, x4.dtype),
            pltpu.VMEM((count - 1,) + pieces[1:], x4.dtype),
            pltpu.VMEM(pieces, x4.dtype),
            pltpu.VMEM((BAND, BAND), x4.dtype),
            dma((count - 1,)),
            dma((count - 1,)),
            dma((rows // 2 - 1,)),
            dma((1,)),
            dma((count - 1,)),
            dma((count - 1,)),
            dma((1,)),
            dma((PARTS, cols - 1)),
            dma((PARTS, PANELS * panel_tiles)),
            dma((panel_tiles, count - 1)),
            dma((panel_tiles, 2)),
        ]
        + Chain.semaphores(tiles, width // CHUNK),
        compiler_params=pltpu.CompilerParams(
            collective_id=collective_id, has_side_effects=True, vmem_limit_bytes=56 * MIB
        ),
    )(x4)


def next_kernel(rows, cols, below, *refs):
    refs = list(refs)
    take = lambda count: [refs.pop(0) for _ in range(count)]
    (
        vec_rows, applied_rows, vec_cols, applied, transform_ref, inner_ref, applied_next,
        old_ref, later_ref, x_ref,
    ) = take(10)
    inverse_ref, shifted_ref, sign_ref, panel_ref, cols_ref = take(5)
    old_high, old_low, new_high, new_low, update_ref, ahead_ref = take(6)
    gram_in, gram_sum = take(2)
    near, near_sum, parts, gram_ref, top_ref = refs[:5]
    near_send, near_recv, line_send, line_recv, send_two, recv_two = refs[5:11]
    top_line_send, top_line_recv, top_send, top_recv = refs[11:15]
    place = Place(rows, cols)
    tile = x_ref.shape[-1]
    panel_tiles = BAND // tile
    number = 2 * panel_tiles
    chain = Chain(place, 1, x_ref, cols_ref, refs[15:])
    chain.start()
    place.greet()
    chain.share()
    chain.spread(0, EARLY + 2)
    half_full = 0.5 * mm(transform_ref[...], inner_ref[...], 1, 0)
    half = split(half_full)
    old = old_ref[...]
    ahead = applied_next[...] - mm(half_full, old, 0, 1)
    ahead_ref[...] = ahead
    chain.late_step(0)
    vec = vec_rows[...]
    vec_parts = split(vec)
    change = applied_rows[...] - mm3(vec_parts, half)
    panel = later_ref[1] - mm(vec, ahead, 1, 0) - mm(change, old, 1, 1)
    lines = lax.broadcasted_iota(jnp.int32, panel.shape, 0)
    above = (below + BAND) // tile
    limit = (above // rows + jnp.where(place.row < above % rows, 1, 0)) * tile
    panel = jnp.where(lines >= limit, panel, 0.0)
    panel_ref[...] = panel
    gram_sum[...] = mm(panel, panel, 0, 0)
    change_parts = split(change)
    for start, value in ((0, vec_parts), (BAND, change_parts)):
        old_high[:, start : start + BAND] = value[0]
        old_low[:, start : start + BAND] = value[1]
    size = BAND
    height = gram_in.shape[2]
    for col in range(cols):
        for core in range(2):
            start = (2 * col + core) * height
            gram_in[col, core] = gram_sum[start : start + height, :]
    chain.late_step(1)
    swap = remote(
        gram_in.at[place.col, 1 - place.core], near.at[0], near_send.at[0], near_recv.at[0],
        place.other, place.col,
    )
    swap.start()

    top_plane = number % rows // 2
    start = pl.multiple_of(place.core * tile, tile)
    local = number // rows * tile
    block = panel_ref.at[pl.ds(local, tile), :]
    target = top_ref.at[pl.ds(start, tile), :]
    at_top = place.plane == top_plane

    def top_line(step):
        return remote(
            block, target, top_line_send.at[step - 1], top_line_recv.at[0],
            lax.rem(place.row + 2 * step, rows), place.col,
        )

    top_near = remote(target, target, top_send.at[0], top_recv.at[0], place.other, place.col)
    top_first = remote(block, target, top_send.at[0], top_recv.at[0], place.other, place.col)

    swap.wait_recv()
    near_sum[0] = gram_in[place.col, place.core] + near[0]
    line = [
        remote(
            near_sum.at[0], parts.at[step - 1], line_send.at[step - 1], line_recv.at[step - 1],
            lax.rem(place.row + 2 * step, rows), place.col,
        )
        for step in range(1, place.planes)
    ]
    for copy in line:
        copy.start()

    @pl.when(at_top)
    def _():
        for step in range(1, place.planes):
            top_line(step).start()
        top_first.start()
        target[...] = block[...]

    chain.spread(EARLY + 2, chain.chunks)
    chain.late_step(2)
    group = 5 if x_ref.shape[1] % 10 == 0 else 1
    wide = x_ref.shape[1] // group * tile
    half_t = split(half_full.T)

    def own_cols(index, carry):
        here = pl.ds(pl.multiple_of(index * wide, wide), wide)
        vec = split(vec_cols[:, here])
        change = applied[:, here] - mm3(half_t, vec)
        update_ref[:, here] = change
        for start, value in ((0, split(change)), (size, vec)):
            new_high[start : start + size, here] = value[0]
            new_low[start : start + size, here] = value[1]
        return carry

    lax.fori_loop(0, group, own_cols, 0)
    chain.late_step(3)
    total = near_sum[0]
    for slot, copy in enumerate(line):
        copy.wait_recv()
        total = total + parts[slot]
    piece = 2 * place.col + place.core
    gram_ref[piece] = total
    gathers = plane_gather(place, gram_ref.at[piece], send_two, recv_two)

    @pl.when(jnp.logical_not(at_top))
    def _():
        top_line(1).wait_recv()
        top_near.start()

    for chunk in range(4, 6):
        chain.late_step(chunk)
    for copy in gathers:
        copy.wait()

    def top():
        top_near.wait_recv()
        return top_ref[...]

    orthogonal_top(
        gram_ref[...].reshape(size, size), top, 1, inverse_ref, shifted_ref, sign_ref,
        later_steps(chain, 6, 2, True),
    )
    chain.end_steps(0)
    swap.wait_send()
    for copy in line:
        copy.wait_send()
    top_near.wait_send()

    @pl.when(at_top)
    def _():
        for step in range(1, place.planes):
            top_line(step).wait_send()

    chain.finish()


def next_panel(operands, x4, below, collective_id):
    rows, cols = lax.axis_size("row"), lax.axis_size("col")
    row_count, tiles, _, tile = x4.shape
    width = tiles * tile
    count = 2 * cols
    piece = (BAND // count, BAND)
    planes = rows // 2
    vmem = pl.BlockSpec(memory_space=pltpu.VMEM)
    dma = pltpu.SemaphoreType.DMA
    f32, bf16 = jnp.float32, jnp.bfloat16
    shape = jax.ShapeDtypeStruct
    square = shape((BAND, BAND), f32)
    return pl.pallas_call(
        functools.partial(next_kernel, rows, cols, below),
        out_shape=(
            square,
            square,
            shape((1, BAND), f32),
            shape((row_count, BAND), f32),
            shape((BAND, width), f32),
            shape((row_count, 2 * BAND), bf16),
            shape((row_count, 2 * BAND), bf16),
            shape((2 * BAND, width), bf16),
            shape((2 * BAND, width), bf16),
            shape((BAND, width), f32),
            square,
        ),
        in_specs=[vmem] * len(operands) + [pl.BlockSpec(memory_space=pltpu.HBM)],
        out_specs=(vmem,) * 11,
        scratch_shapes=[
            pltpu.VMEM((cols, 2) + piece, f32),
            pltpu.VMEM((BAND, BAND), f32),
            pltpu.VMEM((1,) + piece, f32),
            pltpu.VMEM((1,) + piece, f32),
            pltpu.VMEM((planes - 1,) + piece, f32),
            pltpu.VMEM((count,) + piece, f32),
            pltpu.VMEM((BAND, BAND), f32),
            dma((1,)),
            dma((1,)),
            dma((planes - 1,)),
            dma((planes - 1,)),
            dma((count - 1,)),
            dma((count - 1,)),
            dma((planes - 1,)),
            dma((1,)),
            dma((1,)),
            dma((1,)),
        ]
        + Chain.semaphores(tiles, width // CHUNK),
        compiler_params=pltpu.CompilerParams(
            collective_id=collective_id, has_side_effects=True, vmem_limit_bytes=44 * MIB
        ),
    )(*operands, x4)


def split(value):
    high = value.astype(jnp.bfloat16)
    return high, (value - high.astype(jnp.float32)).astype(jnp.bfloat16)


def split_outside(value):
    high = lax.reduce_precision(value, 8, 7)
    return high.astype(jnp.bfloat16), (value - high).astype(jnp.bfloat16)


def dot(a, b):
    return jnp.dot(a, b, preferred_element_type=jnp.float32)


def apply_kernel(rows, cols, tiles, fixed, *refs):
    place = Place(rows, cols)
    refs = list(refs)
    take = lambda count: [refs.pop(0) for _ in range(count)]
    x_ref, left_ref, shifted_ref, sign_ref, vec_ref = take(5)
    old_high, old_low, new_high, new_low = take(4) if fixed else [None] * 4
    applied_row_ref, transform_ref, applied_ref, inner_ref = take(4)
    next_ref = take(1)[0] if tiles else None
    kept_ref = take(1)[0] if fixed else None
    block, part, near, pair, left_in, right_in, left_out, right_out, out_ref, row_ref = take(10)
    total_ref, stack, parts = take(3)
    (
        load, near_send, near_recv, left_send, left_recv, right_send, right_recv,
        both_send, both_recv, row_send, row_recv, send_one, recv_one, send_two, recv_two,
    ) = take(15)
    next_sems = take(2) if tiles else None
    store = take(1)[0] if fixed else None
    plane, core, planes = place.plane, place.core, place.planes
    tile = x_ref.shape[-1]
    chunks = block.shape[0]
    pieces = pair.shape[0] // chunks
    depth = pair.shape[1]
    subs = chunks * pieces
    size = left_ref.shape[0] // 2

    def load_of(chunk, index):
        return pltpu.make_async_copy(
            x_ref.at[:, 2 * chunk + index, 0, :],
            block.at[chunk, :, pl.ds(index * tile, tile)],
            load.at[chunk, index],
        )

    def store_of(chunk, index):
        return pltpu.make_async_copy(
            block.at[chunk, :, pl.ds(index * tile, tile)],
            kept_ref.at[:, 2 * chunk + index, 0, :],
            store.at[chunk, index],
        )

    for chunk in range(chunks):
        for index in range(2):
            load_of(chunk, index).start()
    place.greet()

    def near_of(chunk):
        return remote(
            part.at[chunk, 1 - core],
            near.at[chunk],
            near_send.at[chunk],
            near_recv.at[chunk],
            place.other,
            place.col,
        )

    def rightward(source, index):
        return remote(
            source.at[index], left_in.at[index], right_send.at[index], left_recv.at[index],
            lax.rem(place.row + 2, rows), place.col,
        )

    def leftward(source, index):
        return remote(
            source.at[index], right_in.at[index], left_send.at[index], right_recv.at[index],
            lax.rem(place.row + rows - 2, rows), place.col,
        )

    def joined(chunk):
        near_of(chunk).wait_recv()
        for piece in range(pieces):
            pair[chunk * pieces + piece] = part[chunk, core, piece] + near[chunk, piece]

        @pl.when(plane == 0)
        def _():
            for piece in range(pieces):
                rightward(pair, chunk * pieces + piece).start()

        @pl.when(plane == planes - 1)
        def _():
            for piece in range(pieces):
                leftward(pair, chunk * pieces + piece).start()

    def product(chunk, carry):
        for index in range(2):
            load_of(chunk, index).wait()
        if fixed:
            here = pl.ds(pl.multiple_of(chunk * 2 * tile, 2 * tile), 2 * tile)
            change = dot(old_high[...], new_high[:, here]) + (
                dot(old_low[...], new_high[:, here]) + dot(old_high[...], new_low[:, here])
            )
            block[chunk] = block[chunk] - change
            for index in range(2):
                store_of(chunk, index).start()
        high, low = split(block[chunk])
        value = dot(left_ref[...], high)
        value = value[:size] + (value[size:] + dot(left_ref[:size], low))
        for index in range(2):
            for piece in range(pieces):
                part[chunk, index, piece] = value[
                    piece * depth : (piece + 1) * depth, index * tile : (index + 1) * tile
                ]
        near_of(chunk).start()

        @pl.when(chunk > 0)
        def _():
            joined(chunk - 1)

        for piece in range(pieces):
            chain((chunk - BEHIND) * pieces + piece, 0)
        return carry

    left_lag = HOP * jnp.maximum(plane - 1, 0)
    right_lag = HOP * jnp.maximum(planes - 2 - plane, 0)
    last_lag = jnp.maximum(left_lag, right_lag)
    held = cols * core + place.col
    source = held // 2 == plane
    target_row = 2 * plane + lax.rem(place.col, 2)
    to_self = target_row == place.row
    square = cols == 4
    beside = place.col + 1 - 2 * lax.rem(place.col, 2)
    across = lax.rem(place.col + 2, 4)
    targets = (place.col, beside, across) if square else tuple(
        lax.rem(place.col + step, cols) for step in range(cols)
    )
    relays = (lax.rem(place.row, cols) == across) if square else None

    def depths(index):
        return pl.ds(pl.multiple_of(lax.rem(index, pieces) * depth, depth), depth)

    def lanes(index):
        return pl.ds(pl.multiple_of((2 * (index // pieces) + core) * tile, tile), tile)

    def row_lanes(index):
        return pl.ds(pl.multiple_of(index // pieces * tile, tile), tile)

    def both_of(index):
        spot = out_ref.at[depths(index), lanes(index)]
        return remote(spot, spot, both_send.at[index], both_recv.at[index], place.other, place.col)

    def row_of(index, step):
        return remote(
            out_ref.at[depths(index), lanes(index)],
            row_ref.at[depths(index), row_lanes(index)],
            row_send.at[index, step],
            row_recv.at[index],
            target_row,
            targets[step],
        )

    def relay_of(index):
        spot = row_ref.at[depths(index), row_lanes(index)]
        return remote(spot, spot, row_send.at[index, 3], row_recv.at[index], place.row, beside)

    def relay(index):
        @pl.when(relays & (index >= 0) & (index < subs))
        def _():
            relay_of(index).wait_recv()
            relay_of(index).start()

    def chain(step, carry):
        index = step - left_lag

        @pl.when((plane > 0) & (index >= 0) & (index < subs))
        def _():
            rightward(pair, index).wait_recv()

            @pl.when(plane < planes - 1)
            def _():
                right_out[index] = left_in[index] + pair[index]
                rightward(right_out, index).start()

        other = step - right_lag

        @pl.when((plane < planes - 1) & (other >= 0) & (other < subs))
        def _():
            leftward(pair, other).wait_recv()

            @pl.when(plane > 0)
            def _():
                left_out[other] = right_in[other] + pair[other]
                leftward(left_out, other).start()

        done = step - last_lag

        @pl.when((done >= 0) & (done < subs))
        def _():
            @pl.when(plane == 0)
            def _():
                out_ref[depths(done), lanes(done)] = pair[done] + right_in[done]

            @pl.when(plane == planes - 1)
            def _():
                out_ref[depths(done), lanes(done)] = left_in[done] + pair[done]

            @pl.when((plane > 0) & (plane < planes - 1))
            def _():
                out_ref[depths(done), lanes(done)] = right_out[done] + right_in[done]

            both_of(done).start()

            @pl.when(source)
            def _():
                for step in range(1, len(targets)):
                    row_of(done, step).start()

                @pl.when(to_self)
                def _():
                    row_ref[depths(done), row_lanes(done)] = out_ref[depths(done), lanes(done)]

                @pl.when(jnp.logical_not(to_self))
                def _():
                    row_of(done, 0).start()

        if square:
            relay(done - HOP)
        return carry

    lax.fori_loop(0, chunks, product, 0)
    joined(chunks - 1)
    steps = subs + HOP * (planes - 2 + square)
    count = [0, max(chunks - BEHIND, 0) * pieces]

    def hook():
        count[0] += 1
        if count[0] % 2 == 0 and count[1] < steps:
            chain(count[1], 0)
            count[1] += 1

    transform_ref[...] = block_transform(shifted_ref[...], sign_ref[...], hook)
    if count[1] < steps:
        lax.fori_loop(count[1], steps, chain, 0)
    total_ref[...] = jnp.zeros_like(total_ref)
    transform = split(transform_ref[...])

    def finished(number, carry):
        for index in range(2 * pieces):
            both_of(2 * pieces * number + index).wait_recv()
        here = pl.ds(pl.multiple_of(number * 4 * tile, 4 * tile), 4 * tile)
        applied = mm3(transform, split(out_ref[:, here]))
        applied_ref[:, here] = applied
        total_ref[...] += mm3(split(vec_ref[:, here]), split(applied), 1, 1)
        return carry

    def finished_one(number, carry):
        for index in range(pieces):
            both_of(pieces * number + index).wait_recv()
        here = pl.ds(pl.multiple_of(number * 2 * tile, 2 * tile), 2 * tile)
        applied = mm3(transform, split(out_ref[:, here]))
        applied_ref[:, here] = applied
        total_ref[...] += mm3(split(vec_ref[:, here]), split(applied), 1, 1)
        return carry

    if chunks % 2 == 0:
        lax.fori_loop(0, chunks // 2, finished, 0)
    else:
        lax.fori_loop(0, chunks, finished_one, 0)
    height = stack.shape[1]
    for piece in range(stack.shape[0]):
        stack[piece] = total_ref[piece * height : (piece + 1) * height, :]
    if tiles:
        spread = Spread(place, applied_ref, tiles, next_ref, *next_sems)
        spread.send()
    plane_scatter(place, place.peers()[: cols - 1], stack, parts, inner_ref, send_one, recv_one)
    gathers = plane_gather(place, inner_ref.at[place.me], send_two, recv_two)
    gets = jnp.logical_not(source & to_self)
    if square:
        gets = gets & jnp.logical_not(relays)

    def drain(index, carry):
        both_of(index).wait_send()

        @pl.when(plane < planes - 1)
        def _():
            rightward(pair, index).wait_send()

        @pl.when(plane > 0)
        def _():
            leftward(pair, index).wait_send()

        @pl.when(source)
        def _():
            for step in range(1, len(targets)):
                row_of(index, step).wait_send()

            @pl.when(jnp.logical_not(to_self))
            def _():
                row_of(index, 0).wait_send()

        @pl.when(gets)
        def _():
            row_of(index, 0).wait_recv()

        if square:
            @pl.when(relays)
            def _():
                relay_of(index).wait_send()

        return carry

    def drain_chunk(chunk, carry):
        if fixed:
            for index in range(2):
                store_of(chunk, index).wait()
        near_of(chunk).wait_send()
        return carry

    lax.fori_loop(0, subs, drain, 0)
    lax.fori_loop(0, chunks, drain_chunk, 0)
    applied_row_ref[...] = mm3(split(row_ref[...].T), split(transform_ref[...]), 1, 1)
    for copy in gathers:
        copy.wait()
    if tiles:
        spread.wait()
        spread.finish()


PIECES = 2
HOP = 3
BEHIND = 3


def apply(x4, left, shifted, signs, vec_cols, tiles, more, collective_id):
    rows, cols = lax.axis_size("row"), lax.axis_size("col")
    row_count, held_tiles, _, tile = x4.shape
    width = held_tiles * tile
    chunks = held_tiles // 2
    count = 2 * cols
    vmem = pl.BlockSpec(memory_space=pltpu.VMEM)
    hbm = pl.BlockSpec(memory_space=pltpu.HBM)
    dma = pltpu.SemaphoreType.DMA
    f32 = jnp.float32
    piece = (BAND // PIECES, tile)
    subs = PIECES * chunks
    sums = (count, BAND // count, BAND)
    kept = bool(more)
    square = jax.ShapeDtypeStruct((BAND, BAND), f32)
    wide = jax.ShapeDtypeStruct((BAND, width), f32)
    shapes = (
        jax.ShapeDtypeStruct((row_count, BAND), f32),
        square,
        wide,
        jax.ShapeDtypeStruct(sums, f32),
    )
    shapes += (square,) if tiles else ()
    out = pl.pallas_call(
        functools.partial(apply_kernel, rows, cols, tiles, kept),
        out_shape=shapes + ((jax.ShapeDtypeStruct(x4.shape, x4.dtype),) if kept else ()),
        in_specs=[hbm] + [vmem] * (4 + len(more)),
        out_specs=(vmem,) * len(shapes) + ((hbm,) if kept else ()),
        scratch_shapes=[
            pltpu.VMEM((chunks, row_count, 2 * tile), f32),
            pltpu.VMEM((chunks, 2, PIECES) + piece, f32),
            pltpu.VMEM((chunks, PIECES) + piece, f32),
        ]
        + [pltpu.VMEM((subs,) + piece, f32)] * 5
        + [
            pltpu.VMEM((BAND, width), f32),
            pltpu.VMEM((BAND, row_count), f32),
            pltpu.VMEM((BAND, BAND), f32),
            pltpu.VMEM(sums, f32),
            pltpu.VMEM((cols - 1,) + sums[1:], f32),
        ]
        + [dma((chunks, 2)), dma((chunks,)), dma((chunks,))]
        + [dma((subs,))] * 6
        + [dma((subs, cols)), dma((subs,))]
        + [dma((cols - 1,))] * 2
        + [dma((count - 1,))] * 2
        + ([dma((len(tiles), count - 1)), dma((len(tiles), 2))] if tiles else [])
        + ([dma((chunks, 2))] if kept else []),
        compiler_params=pltpu.CompilerParams(
            collective_id=collective_id, has_side_effects=True, vmem_limit_bytes=(60 if kept else 48) * MIB
        ),
    )(x4, left, shifted, signs, vec_cols, *more)
    out = list(out)
    out[3] = out[3].reshape(BAND, BAND)
    return out


def update_kernel(x_ref, left_high, left_low, right_high, right_low, out_ref, block, result, load, store):
    tile = x_ref.shape[-1]
    chunks = x_ref.shape[1] // 2

    def load_of(chunk, index):
        return pltpu.make_async_copy(
            x_ref.at[:, 2 * chunk + index, 0, :],
            block.at[lax.rem(chunk, 2), :, pl.ds(index * tile, tile)],
            load.at[lax.rem(chunk, 2), index],
        )

    def store_of(chunk, index):
        return pltpu.make_async_copy(
            result.at[lax.rem(chunk, 2), :, pl.ds(index * tile, tile)],
            out_ref.at[:, 2 * chunk + index, 0, :],
            store.at[lax.rem(chunk, 2), index],
        )

    for chunk in range(2):
        for index in range(2):
            load_of(chunk, index).start()

    def body(chunk, carry):
        slot = lax.rem(chunk, 2)
        for index in range(2):
            load_of(chunk, index).wait()

        @pl.when(chunk >= 2)
        def _():
            for index in range(2):
                store_of(chunk - 2, index).wait()

        here = pl.ds(pl.multiple_of(chunk * 2 * tile, 2 * tile), 2 * tile)
        value = dot(left_high[...], right_high[:, here]) + (
            dot(left_low[...], right_high[:, here]) + dot(left_high[...], right_low[:, here])
        )
        result[slot] = block[slot] - value
        for index in range(2):
            store_of(chunk, index).start()

        @pl.when(chunk + 2 < chunks)
        def _():
            for index in range(2):
                load_of(chunk + 2, index).start()

        return carry

    lax.fori_loop(0, chunks, body, 0)
    for chunk in range(chunks - 2, chunks):
        for index in range(2):
            store_of(chunk, index).wait()


def update(x4, left, right):
    row_count, tiles, _, tile = x4.shape
    vmem = pl.BlockSpec(memory_space=pltpu.VMEM)
    hbm = pl.BlockSpec(memory_space=pltpu.HBM)
    dma = pltpu.SemaphoreType.DMA
    return pl.pallas_call(
        update_kernel,
        out_shape=jax.ShapeDtypeStruct(x4.shape, x4.dtype),
        in_specs=[hbm] + [vmem] * 4,
        out_specs=hbm,
        scratch_shapes=[pltpu.VMEM((2, row_count, 2 * tile), jnp.float32)] * 2
        + [dma((2, 2)), dma((2, 2))],
        compiler_params=pltpu.CompilerParams(vmem_limit_bytes=48 * MIB),
    )(x4, *left, *right)


def on_device(matrix_tiles):
    tile_shape = matrix_tiles.shape
    block_rows, _, tile_size, block_cols = tile_shape[:4]
    row_count = block_rows * tile_size
    col_count = block_cols * tile_size
    row_devices = lax.axis_size("row")
    col_devices = lax.axis_size("col")
    row_index = lax.axis_index("row")
    panel_tiles = BAND // tile_size
    assert row_devices == 2 * col_devices and PANELS * panel_tiles <= col_devices
    x4 = matrix_tiles.reshape(row_count, block_cols, 1, tile_size)

    def positions(count, devices, index):
        place = jnp.arange(count, dtype=jnp.int32)
        return (place // tile_size * devices + index) * tile_size + place % tile_size

    global_rows = positions(row_count, row_devices, row_index)
    global_cols = positions(col_count, lax.axis_size("col"), lax.axis_index("col"))
    band = jnp.arange(BAND, dtype=jnp.int32)
    inverse, shifted, signs, rows_held, panel_cols = first_panel(x4, 0)
    panel_rows = rows_held[0]
    kept, more = x4, ()
    for panel_index in range(PANELS):
        below = (panel_index + 1) * BAND
        last = panel_index == PANELS - 1
        panel_rows = jnp.where((global_rows >= below)[:, None], panel_rows, 0.0)
        unit_rows = (global_rows[:, None] - below == band[None, :]).astype(jnp.float32)
        unit_rows_t = (band[:, None] == global_rows[None, :] - below).astype(jnp.float32)
        vec_rows = multiply(panel_rows, inverse, 1, 1) - unit_rows * signs
        vec_rows_t = multiply(inverse, panel_rows, 1, 1) - unit_rows_t * signs.reshape(BAND, 1)
        panel_cols = jnp.where((global_cols >= below)[None, :], panel_cols, 0.0)
        unit_cols = (band[:, None] == global_cols[None, :] - below).astype(jnp.float32)
        vec_cols = multiply(inverse, panel_cols) - unit_cols * signs.reshape(BAND, 1)
        first = below // tile_size
        applied_rows, transform, applied, inner, *rest = apply(
            kept,
            jnp.concatenate(split_outside(vec_rows_t), 0),
            shifted,
            signs,
            vec_cols,
            () if last else tuple(range(first, first + panel_tiles)),
            more,
            1 + panel_index,
        )
        if last:
            break
        old_shifted, old_cols = shifted, vec_cols
        (
            inverse, shifted, signs, panel_rows, panel_cols,
            old_high, old_low, new_high, new_low, update_cols, update_next,
        ) = next_panel(
            (
                vec_rows, applied_rows, vec_cols, applied, transform, inner, rest[0], shifted,
                rows_held,
            ),
            x4,
            below,
            3,
        )
        more = (old_high, old_low, new_high, new_low)
        panel_cols = (
            panel_cols - multiply(update_next, old_cols, 0, 0) - multiply(old_shifted, update_cols)
        )
    half_inner = 0.5 * multiply(transform, inner)
    high = lax.Precision.HIGH
    update_rows = applied_rows - multiply(vec_rows, half_inner, precision=high)
    update_cols = applied - multiply(half_inner, vec_cols, 0, 0, precision=high)
    left = split_outside(jnp.concatenate([vec_rows, update_rows], 1))
    right = split_outside(jnp.concatenate([update_cols, vec_cols], 0))
    return update(rest[0], left, right).reshape(tile_shape)


def solution(mesh):
    return jax.shard_map(
        on_device,
        mesh=mesh,
        in_specs=(P(None, "row", None, None, "col", None),),
        out_specs=P(None, "row", None, None, "col", None),
        check_vma=False,
    )
```
